32 devices in a mesh: grp: 4 (over z), seq: 8 (over y, x, core).
Axes of the slice: x: 2, y: 2, z: 4, core: 2. Of those that a mesh axis runs over, the one named last changes fastest.
Arguments:
- queries: bfloat16 [4096, 1232], P(('grp', 'seq')), may hold values from -6 to 6
- key_vectors: bfloat16 [4096, 1232], P(('grp', 'seq')), may hold values from -6 to 6
- value_vectors: bfloat16 [4096, 1232], P(('grp', 'seq')), may hold values from -1 to 3
- output_grad: bfloat16 [4096, 1232], P(('grp', 'seq')), may hold values from -4096 to 4096
- state_in: float32 [11, 112, 112], replicated, may hold values from 38.4 to 64
- norm_in: float32 [11, 112], replicated, may hold values from 38.4 to 64
- grad_state: float32 [11, 112, 112], replicated, may hold values from -1 to 1
- grad_norm: float32 [11, 112], replicated, may hold values from -12 to 12
Outputs:
- query_grad: bfloat16 [4096, 1232], P(('grp', 'seq'))
- key_grad: bfloat16 [4096, 1232], P(('grp', 'seq'))
- value_grad: bfloat16 [4096, 1232], P(('grp', 'seq'))
The draws below stay inside these ranges and needn't reach their ends.
All inputs are finite; a program needn't handle non-finite values.
Results may differ from the reference program's by a relative error of at most 0.006.
Values sent between devices are 32-bit elements; how exact they have to be, the bound alone decides.
No kernel may reach another device: no remote copies, remote signals or barrier semaphores. Data moves between devices by JAX's collectives and lax.ppermute only.
A program may use at most 128 MiB of HBM per device.

```python
import jax
import jax.numpy as jnp
from jax import lax

HEADS = 11
HEAD = 112
TOK_DEV = 128
TOKENS = 4096


def shard_levels(stream_key, extent, split, smallest, top_value):
    factor_of, own = 1.0, jax.random.fold_in(stream_key, 6)
    for dim, parts in split:
        heights = jnp.exp(jax.random.uniform(jax.random.fold_in(own, dim), (parts,), jnp.float32, smallest / len(split), top_value / len(split)))
        factor_of = factor_of * jnp.repeat(heights, extent[dim] // parts).reshape([-1 if axis == dim else 1 for axis in range(len(extent))])
    return factor_of


def noise(stream_key, dims, scale, bound, pieces=(), held_as=jnp.bfloat16):
    drawn = jax.random.normal(stream_key, dims, jnp.float32) * scale
    if len(pieces) > 0:
        drawn = shard_levels(stream_key, dims, pieces, -0.22, 0.18) * drawn
    return jnp.clip(drawn, min=-bound, max=bound).astype(held_as)


def setup_inputs(seed: int = 0) -> dict:
    streams_of = jax.random.split(jax.random.key(seed), 9)
    queries = noise(streams_of[0], (TOKENS, HEADS * HEAD), 1.0, 6.0, ((0, 32),))
    key_vectors = noise(streams_of[1], (TOKENS, HEADS * HEAD), 1.0, 6.0, ((0, 32),))
    value_vectors = jnp.clip(-1.0 + 4.0 * jax.random.uniform(streams_of[2], (TOKENS, HEADS * HEAD), jnp.float32) ** shard_levels(streams_of[2], (TOKENS, HEADS * HEAD), ((0, 32),), -0.2, 0.2), -1.0, 3.0).astype(jnp.bfloat16)
    output_grad = noise(streams_of[3], (TOKENS, HEADS * HEAD), ((TOKENS * HEAD) ** 0.5), 4096.0, ((0, 32),))
    state_in = jnp.clip(jax.random.uniform(streams_of[4], (HEADS, HEAD, HEAD), jnp.float32, 38.4, 64.0), 38.4, 64.0)
    norm_in = jnp.clip(jax.random.uniform(streams_of[5], (HEADS, HEAD), jnp.float32, 38.4, 64.0), 38.4, 64.0)
    grad_state = noise(streams_of[6], (HEADS, HEAD, HEAD), (2.0 / HEAD ** 0.5), 1.0, (), jnp.float32)
    grad_norm = noise(streams_of[7], (HEADS, HEAD), 2.0, 12.0, (), jnp.float32)
    return dict(queries=queries, key_vectors=key_vectors, value_vectors=value_vectors, output_grad=output_grad, state_in=state_in, norm_in=norm_in, grad_state=grad_state, grad_norm=grad_norm)


def shifted_sum(blocks_data):
    running = jnp.cumsum(blocks_data, axis=0)
    return jnp.concatenate([jnp.zeros_like(blocks_data[:1]), running[:-1]], axis=0)


def later_sum(blocks_data):
    return jnp.flip(shifted_sum(jnp.flip(blocks_data, axis=0)), axis=0)


def head_grads(inputs):
    query_head, key_head, value_head, grad_head, state_head, norm_head, carry_head, carry_norm = inputs
    highest = lax.Precision.HIGHEST
    width = query_head.shape[1]
    blocks = query_head.shape[0] // TOK_DEV
    query_feat = jnp.maximum(query_head, 0).astype(jnp.float32).reshape(blocks, TOK_DEV, width)
    key_feat = jnp.maximum(key_head, 0).astype(jnp.float32).reshape(blocks, TOK_DEV, width)
    value_wide = value_head.astype(jnp.float32).reshape(blocks, TOK_DEV, width)
    grad_wide = grad_head.astype(jnp.float32).reshape(blocks, TOK_DEV, width)
    block_state = jnp.einsum('btd,bte->bde', key_feat, value_wide, precision=highest)
    block_norm = jnp.sum(key_feat, axis=1)
    prefix_state = state_head[None] + shifted_sum(block_state)
    prefix_norm = norm_head[None] + shifted_sum(block_norm)
    positions = lax.iota(jnp.int32, TOK_DEV)
    causal = (positions[:, None] >= positions[None, :])[None]
    masked = jnp.where(causal, jnp.einsum('btd,bsd->bts', query_feat, key_feat, precision=highest), 0.0)
    denominator = 1.0 + jnp.einsum('btd,bd->bt', query_feat, prefix_norm, precision=highest) + jnp.sum(masked, axis=2)
    scores_low = lax.optimization_barrier(masked.astype(jnp.bfloat16)).astype(jnp.float32)
    numerator = jnp.einsum('btd,bde->bte', query_feat, prefix_state, precision=highest) + jnp.einsum('bts,bse->bte', scores_low, value_wide, precision=highest)
    output = numerator / denominator[:, :, None]
    num_grad = grad_wide / denominator[:, :, None]
    den_grad = -jnp.sum(grad_wide * output, axis=2) / denominator
    num_grad_low = lax.optimization_barrier(num_grad.astype(jnp.bfloat16)).astype(jnp.float32)
    carry_state = jnp.einsum('btd,bte->bde', query_feat, num_grad_low, precision=highest)
    carry_sum = jnp.einsum('btd,bt->bd', query_feat, den_grad, precision=highest)
    suffix_state = carry_head[None] + later_sum(carry_state)
    suffix_norm = carry_norm[None] + later_sum(carry_sum)
    mixed = jnp.where(causal, jnp.einsum('bte,bse->bts', num_grad_low, value_wide, precision=highest) + den_grad[:, :, None], 0.0)
    mixed_low = lax.optimization_barrier(mixed.astype(jnp.bfloat16)).astype(jnp.float32)
    query_part = jnp.einsum('bte,bde->btd', num_grad, prefix_state, precision=highest) + den_grad[:, :, None] * prefix_norm[:, None, :] + jnp.einsum('bts,bsd->btd', mixed_low, key_feat, precision=highest)
    key_part = jnp.einsum('bse,bde->bsd', value_wide, suffix_state, precision=highest) + suffix_norm[:, None, :] + jnp.einsum('bts,btd->bsd', mixed_low, query_feat, precision=highest)
    value_part = jnp.einsum('bsd,bde->bse', key_feat, suffix_state, precision=highest) + jnp.einsum('bts,bte->bse', scores_low, num_grad_low, precision=highest)
    total = blocks * TOK_DEV
    query_grad = jnp.where(query_head > 0, query_part.reshape(total, width), 0.0).astype(jnp.bfloat16)
    key_grad = jnp.where(key_head > 0, key_part.reshape(total, width), 0.0).astype(jnp.bfloat16)
    value_grad = value_part.reshape(total, width).astype(jnp.bfloat16)
    return query_grad, key_grad, value_grad


def split_heads(array):
    return array.reshape(array.shape[0], HEADS, HEAD).transpose(1, 0, 2)


def join_heads(array):
    return array.transpose(1, 0, 2).reshape(array.shape[1], HEADS * HEAD)


def reference(queries, key_vectors, value_vectors, output_grad, state_in, norm_in, grad_state, grad_norm):
    results = lax.map(head_grads, (split_heads(queries), split_heads(key_vectors), split_heads(value_vectors), split_heads(output_grad), state_in, norm_in, grad_state, grad_norm))
    return (join_heads(results[0]), join_heads(results[1]), join_heads(results[2]))
```

```python
import functools

import jax
import jax.numpy as jnp
from jax import lax
from jax.experimental import pallas as pl
from jax.experimental.pallas import tpu as pltpu
from jax.sharding import PartitionSpec as P

F32 = jnp.float32
BF16 = jnp.bfloat16
LANES = 128
SUB = 8


def dot(x, y, dims):
    return lax.dot_general(x, y, (dims, ((), ())), preferred_element_type=F32)


def nn(x, y):
    return dot(x, y, ((1,), (0,)))


def nt(x, y):
    return dot(x, y, ((1,), (1,)))


def tn(x, y):
    return dot(x, y, ((0,), (0,)))


def exact(x, y):
    return lax.dot_general(
        x, y, (((1,), (0,)), ((), ())), precision=lax.Precision.HIGHEST, preferred_element_type=F32
    )


def parts(x):
    high = x.astype(BF16)
    return high, (x - high.astype(F32)).astype(BF16)


def stacked_parts(row):
    high = row.astype(BF16)
    rest = row - high.astype(F32)
    middle = rest.astype(BF16)
    low = rest - middle.astype(F32)
    zeros = jnp.zeros((SUB - 3, row.shape[1]), F32)
    return jnp.concatenate([high.astype(F32), middle.astype(F32), low, zeros], axis=0).astype(BF16)


def added(rows):
    return rows[0:1] + rows[1:2] + rows[2:3]


class Plan:
    def __init__(self, devices, length, heads, width):
        self.devices, self.length, self.heads, self.width = devices, length, heads, width
        self.half = -(-heads // 2)
        self.shift = heads - self.half
        self.rows = self.half * width
        self.per_slot = devices // SUB
        self.head_tiles = width // SUB
        self.tiles = self.half * self.head_tiles
        self.slots = -(-self.tiles // self.per_slot)
        self.span = self.slots * LANES

    def place(self, base, tile):
        slot, part = divmod(tile, self.per_slot)
        return pl.ds(part * SUB, SUB), pl.ds((base + slot) * LANES, LANES)

    def row_slot(self, head):
        return pl.ds((self.slots + head) * LANES, LANES)

    def own(self, ref, core, head):
        start = pl.multiple_of(core * (self.shift * self.width) + head * self.width, 16)
        return ref[pl.ds(start, self.width), :]

    def other(self, ref, head):
        return ref[head * self.width : (head + 1) * self.width, :]


def my_core():
    return lax.axis_index("seq") & 1


def my_device():
    return lax.axis_index("grp") * lax.axis_size("seq") + lax.axis_index("seq")


def pair_swap(x):
    size = lax.axis_size("seq")
    return lax.ppermute(x, "seq", [(i, i ^ 1) for i in range(size)])


def wide(tile):
    rows, columns = tile.shape
    if columns == LANES:
        return tile
    return jnp.concatenate([tile, jnp.zeros((rows, LANES - columns), tile.dtype)], axis=1)


def store_rows(plan, ref, base, head, block):
    block = wide(block)
    for j in range(plan.head_tiles):
        rows, columns = plan.place(base, head * plan.head_tiles + j)
        ref[rows, columns] = block[j * SUB : (j + 1) * SUB, :]


def store_padding(plan, ref, base):
    for tile in range(plan.tiles, plan.slots * plan.per_slot):
        rows, columns = plan.place(base, tile)
        ref[rows, columns] = jnp.zeros((SUB, LANES), F32)


def load_rows(plan, ref, base, head):
    tiles = []
    for j in range(plan.head_tiles):
        rows, columns = plan.place(base, head * plan.head_tiles + j)
        tiles.append(ref[rows, columns])
    return jnp.concatenate(tiles, axis=0)[:, : plan.width]


def scan_matrix(devices, later):
    row = lax.broadcasted_iota(jnp.int32, (devices, devices), 0)
    column = lax.broadcasted_iota(jnp.int32, (devices, devices), 1)
    beyond = (column // 2 > row // 2) if later else (column // 2 < row // 2)
    return jnp.where(beyond & (column % 2 == row % 2), 1.0, 0.0).astype(F32)


def scan_row(devices, core, chip, later):
    column = lax.broadcasted_iota(jnp.int32, (SUB, devices), 1)
    beyond = (column // 2 > chip) if later else (column // 2 < chip)
    return jnp.where(beyond & (column % 2 == core), 1.0, 0.0).astype(F32)


def causal_mask(length):
    row = lax.broadcasted_iota(jnp.int32, (length, length), 0)
    column = lax.broadcasted_iota(jnp.int32, (length, length), 1)
    return row <= column


def relu(x):
    return jnp.maximum(x, 0)


def chip_state(plan, ids_ref, k_ref, v_ref, k_got_ref, v_got_ref, out_ref):
    core = ids_ref[0]
    ones = jnp.ones((SUB, 2 * plan.length), BF16)
    for h in range(plan.half):
        keys = [relu(plan.own(k_ref, core, h)), relu(plan.other(k_got_ref, h)).astype(BF16)]
        values = [plan.own(v_ref, core, h), plan.other(v_got_ref, h).astype(BF16)]
        keys, values = jnp.concatenate(keys, axis=1), jnp.concatenate(values, axis=1)
        store_rows(plan, out_ref, 0, h, nt(values, keys))
        norm = wide(nt(ones, keys))
        for j in range(plan.devices // SUB):
            out_ref[j * SUB : (j + 1) * SUB, plan.row_slot(h)] = norm
    store_padding(plan, out_ref, 0)


def local_scores(
    plan, ids_ref, k_ref, v_ref, q_ref, k_got_ref, v_got_ref, q_got_ref,
    low_ref, sum_ref, inner_ref, norm_ref,
):
    core = ids_ref[0]
    causal = causal_mask(plan.length)
    ones = jnp.ones((SUB, plan.length), BF16)
    for h in range(plan.half):
        for i in range(2):
            if i == 0:
                a, b = relu(plan.own(q_ref, core, h)), relu(plan.own(k_ref, core, h))
                v = plan.own(v_ref, core, h)
            else:
                a, b = relu(plan.other(q_got_ref, h)), relu(plan.other(k_got_ref, h))
                a, b, v = a.astype(BF16), b.astype(BF16), plan.other(v_got_ref, h).astype(BF16)
            scores = jnp.where(causal, tn(b, a), 0.0)
            sum_ref[i, h : h + 1, :] = 1.0 + jnp.sum(scores, axis=0, keepdims=True)
            low = scores.astype(BF16)
            low_ref[i, h] = low
            inner_ref[i, h] = nn(v, low)
            norm_ref[i, h : h + 1, :] = wide(nt(ones, b))[0:1]


def middle(
    plan, ids_ref, in_ref, sum_ref, q_ref, g_ref, q_got_ref, g_got_ref, norm_ref, norm_in_ref,
    out_ref, den_ref, z_ref,
):
    core, chip = ids_ref[0], ids_ref[1]
    flags = (core.astype(F32), (1 - core).astype(F32))
    width = plan.width
    norms = exact(scan_row(plan.devices, core, chip, False), in_ref[:, plan.span :])
    for h in range(plan.half):
        base = norm_in_ref[pl.ds(core * plan.shift + h, 1), :]
        base = base + norms[0:1, h * LANES : h * LANES + width]
        features, grads = [], []
        for i in range(2):
            z = base + flags[i] * norm_ref[1 - i, h : h + 1, :width]
            z_ref[i, h : h + 1, :] = wide(z)
            if i == 0:
                a, g = relu(plan.own(q_ref, core, h)), plan.own(g_ref, core, h).astype(F32)
            else:
                a, g = relu(plan.other(q_got_ref, h)).astype(BF16), plan.other(g_got_ref, h)
            den = sum_ref[i, h : h + 1, :] + added(nn(stacked_parts(z), a))
            den_ref[i, h : h + 1, :] = den
            features.append(a)
            grads.append((g * (1.0 / den)).astype(BF16))
        state = nt(jnp.concatenate(features, axis=1), jnp.concatenate(grads, axis=1))
        store_rows(plan, out_ref, plan.slots, h, state)
    store_padding(plan, out_ref, plan.slots)
    out_ref[:, : plan.span] = exact(scan_matrix(plan.devices, False), in_ref[:, : plan.span])


def local_grads(
    plan, ids_ref, k_ref, v_ref, q_ref, g_ref, k_got_ref, v_got_ref, q_got_ref, g_got_ref,
    low_ref, den_ref, state_in_ref, grad_state_ref, mixed_ref, value_ref, before_ref, after_ref,
):
    core = ids_ref[0]
    own_first = core == 0
    late = (core.astype(F32), (1 - core).astype(F32))
    early = (late[1], late[0])
    for h in range(plan.half):
        own = [plan.own(ref, core, h) for ref in (k_ref, v_ref, q_ref, g_ref)]
        got = [plan.other(ref, h) for ref in (k_got_ref, v_got_ref, q_got_ref, g_got_ref)]
        us = []
        for i, (_, v, _, g) in enumerate((own, got)):
            u = (g.astype(F32) * (1.0 / den_ref[i, h : h + 1, :])).astype(BF16)
            us.append(u)
            mixed_ref[i, h] = tn(v.astype(BF16), u)
            value_ref[i, h] = nt(u, low_ref[i, h])
        k = jnp.where(own_first, own[0].astype(F32), got[0])
        v = jnp.where(own_first, own[1].astype(F32), got[1])
        first = nt(v.astype(BF16), relu(k).astype(BF16))
        q = jnp.where(own_first, got[2], own[2].astype(F32))
        u = jnp.where(own_first, us[1].astype(F32), us[0].astype(F32))
        second = nt(relu(q).astype(BF16), u.astype(BF16))
        state_in = state_in_ref[core * plan.shift + h].T
        grad_state = grad_state_ref[core * plan.shift + h]
        for i in range(2):
            before_ref[i, h] = state_in + late[i] * first
            after_ref[i, h] = grad_state + early[i] * second


def outputs_grad(
    plan, ids_ref, in_ref, before_ref, q_ref, g_ref, q_got_ref, g_got_ref, den_ref, inner_ref,
    out_ref, state_ref, c_ref, m_ref,
):
    core = ids_ref[0]
    for h in range(plan.half):
        base = load_rows(plan, in_ref, 0, h)
        total = None
        for i in range(2):
            if i == 0:
                a, g = relu(plan.own(q_ref, core, h)), plan.own(g_ref, core, h).astype(F32)
            else:
                a, g = relu(plan.other(q_got_ref, h)).astype(BF16), plan.other(g_got_ref, h)
            state = base + before_ref[i, h]
            state_ref[i, h] = state
            high, low = parts(state)
            numerator = nn(high, a) + nn(low, a) + inner_ref[i, h]
            inverse = 1.0 / den_ref[i, h : h + 1, :]
            along = jnp.sum(g * numerator, axis=0, keepdims=True)
            c = -(along * inverse) * inverse
            c_ref[i, h : h + 1, :] = c
            m = wide(added(nt(stacked_parts(c), a)))
            m_ref[i, h : h + 1, :] = m
            total = m if total is None else total + m
        out_ref[:, plan.row_slot(h)] = jnp.broadcast_to(total, (plan.devices, LANES))
    out_ref[:, : plan.span] = exact(scan_matrix(plan.devices, True), in_ref[:, plan.span :])


def query_grads(
    plan, ids_ref, k_ref, q_ref, g_ref, k_got_ref, q_got_ref, g_got_ref, den_ref, c_ref, z_ref,
    mixed_ref, state_ref, own_ref, send_ref, key_ref,
):
    core = ids_ref[0]
    causal = causal_mask(plan.length)
    width = plan.width
    for i in range(2):
        columns = z_ref[i].T
        for h in range(plan.half):
            rows = slice(h * width, (h + 1) * width)
            if i == 0:
                a, b = relu(plan.own(q_ref, core, h)), relu(plan.own(k_ref, core, h))
                g = plan.own(g_ref, core, h).astype(F32)
            else:
                a, b = relu(plan.other(q_got_ref, h)), relu(plan.other(k_got_ref, h))
                a, b, g = a.astype(BF16), b.astype(BF16), plan.other(g_got_ref, h)
            u = g * (1.0 / den_ref[i, h : h + 1, :])
            c = c_ref[i, h : h + 1, :]
            mixed = jnp.where(causal, mixed_ref[i, h] + c, 0.0).astype(BF16)
            high, low = parts(state_ref[i, h])
            u_high, u_low = parts(u)
            grad = tn(high, u_high) + (tn(low, u_high) + tn(high, u_low))
            grad = grad + columns[:width, h : h + 1] * c + nn(b, mixed)
            grad = jnp.where(a.astype(F32) > 0, grad, 0.0)
            target = own_ref if i == 0 else send_ref
            target[rows, :] = grad
            key_ref[i, h] = nt(a, mixed)


def key_value_grads(
    plan, ids_ref, in_ref, after_ref, grad_norm_ref, m_ref, key_in_ref, value_in_ref, k_ref, v_ref, k_got_ref, v_got_ref, key_ref, value_ref, key_send_ref,
    value_send_ref,
):
    core, chip = ids_ref[0], ids_ref[1]
    flags = ((1 - core).astype(F32), core.astype(F32))
    width = plan.width
    norms = exact(scan_row(plan.devices, core, chip, True), in_ref[:, plan.span :])[0:1]
    norms = jnp.concatenate(
        [norms[:, h * LANES : (h + 1) * LANES] for h in range(plan.half)]
        + [jnp.zeros((SUB - plan.half % SUB, LANES), F32)], axis=0,
    )
    own_rows = [
        grad_norm_ref[pl.ds(core * plan.shift + h, 1), :] for h in range(plan.half)
    ] + [jnp.zeros((SUB - plan.half % SUB, width), F32)]
    norms = norms + wide(jnp.concatenate(own_rows, axis=0))
    for i in range(2):
        columns = (norms + flags[i] * m_ref[1 - i]).T
        for h in range(plan.half):
            rows = slice(h * width, (h + 1) * width)
            high, low = parts(load_rows(plan, in_ref, 0, h) + after_ref[i, h])
            if i == 0:
                b, v = relu(plan.own(k_ref, core, h)), plan.own(v_ref, core, h)
            else:
                b, v = relu(plan.other(k_got_ref, h)).astype(BF16), plan.other(v_got_ref, h).astype(BF16)
            key = nn(high, v) + nn(low, v) + columns[:width, h : h + 1] + key_in_ref[i, h]
            key = jnp.where(b.astype(F32) > 0, key, 0.0)
            value = tn(high, b) + tn(low, b) + value_in_ref[i, h]
            if i == 0:
                key_ref[rows, :] = key
                value_ref[rows, :] = value
            else:
                key_send_ref[rows, :] = key
                value_send_ref[rows, :] = value


def assemble(plan, ids_ref, *refs):
    core = ids_ref[0]
    count = len(refs) // 3
    start = pl.multiple_of(core * (plan.shift * plan.width), 16)
    rest = plan.shift * plan.width
    skip = plan.rows - rest
    other = pl.multiple_of((1 - core) * plan.rows, 16)
    source = pl.multiple_of((1 - core) * skip, 16)
    for own_ref, got_ref, out_ref in zip(refs[:count], refs[count : 2 * count], refs[2 * count :]):
        out_ref[pl.ds(start, plan.rows), :] = own_ref[...].astype(BF16)
        out_ref[pl.ds(other, rest), :] = got_ref[pl.ds(source, rest), :].astype(BF16)


def call(body, outs, args, flops=10_000_000, scratch=()):
    smem = pl.BlockSpec(memory_space=pltpu.SMEM)
    vmem = pl.BlockSpec(memory_space=pltpu.VMEM)
    in_specs = [smem if x.ndim == 1 else vmem for x in args]
    moved = sum(x.size * x.dtype.itemsize for x in (*args, *outs))
    return pl.pallas_call(
        body,
        out_shape=outs,
        in_specs=in_specs,
        out_specs=[vmem] * len(outs),
        scratch_shapes=list(scratch),
        cost_estimate=pl.CostEstimate(flops=flops, bytes_accessed=moved, transcendentals=0),
    )(*args)


def shape(dims, dtype=F32):
    return jax.ShapeDtypeStruct(dims, dtype)


def per_device(
    queries, key_vectors, value_vectors, output_grad, state_in, norm_in, grad_state, grad_norm
):
    both = ("grp", "seq")
    length = queries.shape[0]
    heads, width = norm_in.shape
    devices = lax.axis_size("grp") * lax.axis_size("seq")
    plan = Plan(devices, length, heads, width)
    half = plan.half
    core = my_core()
    who = jnp.stack([core, my_device() >> 1]).astype(jnp.int32)
    q, k, v, g = queries.T, key_vectors.T, value_vectors.T, output_grad.T

    def bind(body):
        return functools.partial(body, plan)

    def exchange(x):
        return lax.all_to_all(x, both, 0, 0, tiled=True)

    def swap_columns(x):
        start = (1 - core) * (plan.shift * width)
        return pair_swap(lax.dynamic_slice_in_dim(x, start, plan.rows, 0).astype(F32))

    tokens = shape((plan.rows, length))
    pair = shape((2, half, width, length))
    square = (2, half, length, length)
    states = shape((2, half, width, width))
    rows = shape((2, SUB * -(-half // SUB), LANES))
    wide_sent = shape((devices, plan.span + half * LANES))

    k_got, v_got = swap_columns(k), swap_columns(v)
    (sent,) = call(bind(chip_state), (wide_sent,), (who, k, v, k_got, v_got))
    got = exchange(sent)
    q_got, g_got = swap_columns(q), swap_columns(g)
    low, sums, inner, norm = call(
        bind(local_scores),
        (shape(square, BF16), rows, pair, rows),
        (who, k, v, q, k_got, v_got, q_got),
    )
    sent, den, z = call(
        bind(middle),
        (shape((devices, 2 * plan.span)), rows, rows),
        (who, got, sums, q, g, q_got, g_got, norm, norm_in),
    )
    got = exchange(sent)
    mixed, value, before, after = call(
        bind(local_grads),
        (shape(square), pair, states, states),
        (who, k, v, q, g, k_got, v_got, q_got, g_got, low, den, state_in, grad_state),
    )
    sent, state, c, m = call(
        bind(outputs_grad),
        (wide_sent, states, rows, rows),
        (who, got, before, q, g, q_got, g_got, den, inner),
    )
    got = exchange(sent)
    query, query_send, key = call(
        bind(query_grads),
        (tokens, tokens, pair),
        (who, k, q, g, k_got, q_got, g_got, den, c, z, mixed, state),
    )
    final = shape((heads * width, length), BF16)
    (query_grad,) = call(bind(assemble), (final,), (who, query, pair_swap(query_send)))
    key, value, key_send, value_send = call(
        bind(key_value_grads),
        (tokens,) * 4,
        (who, got, after, grad_norm, m, key, value, k, v, k_got, v_got),
    )
    key_grad, value_grad = call(
        bind(assemble),
        (final, final),
        (who, key, value, pair_swap(key_send), pair_swap(value_send)),
    )
    return query_grad.T, key_grad.T, value_grad.T


def solution(mesh):
    rows = P(("grp", "seq"), None)
    return jax.shard_map(
        per_device,
        mesh=mesh,
        in_specs=(rows, rows, rows, rows, P(), P(), P(), P()),
        out_specs=(rows, rows, rows),
        check_vma=False,
    )
```

```python
import functools

import jax
import jax.numpy as jnp
from jax import lax
from jax.experimental import pallas as pl
from jax.experimental.pallas import tpu as pltpu
from jax.sharding import PartitionSpec as P

F32 = jnp.float32
BF16 = jnp.bfloat16
LANES = 128
SUB = 8
VMEM_BYTES = 67_043_328
FREE = 48 * 2**20


def dot(x, y, dims):
    return lax.dot_general(x, y, (dims, ((), ())), preferred_element_type=F32)


def nn(x, y):
    return dot(x, y, ((1,), (0,)))


def nt(x, y):
    return dot(x, y, ((1,), (1,)))


def tn(x, y):
    return dot(x, y, ((0,), (0,)))


def parts(x):
    high = x.astype(BF16)
    return high, (x - high.astype(F32)).astype(BF16)


def stacked_parts(row):
    high = row.astype(BF16)
    rest = row - high.astype(F32)
    middle = rest.astype(BF16)
    low = rest - middle.astype(F32)
    zeros = jnp.zeros((SUB - 3, row.shape[1]), F32)
    return jnp.concatenate([high.astype(F32), middle.astype(F32), low, zeros], axis=0).astype(BF16)


def added(rows):
    return rows[0:1] + rows[1:2] + rows[2:3]


class Plan:
    def __init__(self, devices, length, heads, width):
        self.devices, self.length, self.heads, self.width = devices, length, heads, width
        self.half = -(-heads // 2)
        self.shift = heads - self.half
        self.rows = self.half * width
        self.extra = SUB * -(-self.half // SUB)
        self.per_slot = devices // SUB
        self.head_tiles = width // SUB
        self.tiles = self.half * self.head_tiles
        self.slots = -(-self.tiles // self.per_slot)
        self.span = self.slots * LANES

    def place(self, base, tile):
        slot, part = divmod(tile, self.per_slot)
        return pl.ds(part * SUB, SUB), 0, pl.ds((base + slot) * LANES, LANES)

    def columns(self, start, count):
        return slice(None), slice(None), pl.ds(start, count)

    def row_slot(self, head):
        return pl.ds((self.slots + head) * LANES, LANES)

    def own(self, ref, core, head):
        start = pl.multiple_of(core * (self.shift * self.width) + head * self.width, 16)
        return ref[pl.ds(start, self.width), :]

    def other(self, ref, head):
        return ref[head * self.width : (head + 1) * self.width, :]


def my_core():
    return lax.axis_index("seq") & 1


def my_device():
    return lax.axis_index("grp") * lax.axis_size("seq") + lax.axis_index("seq")


def pair_swap(x):
    size = lax.axis_size("seq")
    return lax.ppermute(x, "seq", [(i, i ^ 1) for i in range(size)])


def wide(tile):
    rows, columns = tile.shape
    if columns == LANES:
        return tile
    return jnp.concatenate([tile, jnp.zeros((rows, LANES - columns), tile.dtype)], axis=1)


def store_rows(plan, ref, base, head, block):
    block = wide(block)
    for j in range(plan.head_tiles):
        ref[plan.place(base, head * plan.head_tiles + j)] = block[j * SUB : (j + 1) * SUB, :]


def store_padding(plan, ref, base):
    for tile in range(plan.tiles, plan.slots * plan.per_slot):
        ref[plan.place(base, tile)] = jnp.zeros((SUB, LANES), F32)


def load_rows(plan, ref, base, head):
    tiles = []
    for j in range(plan.head_tiles):
        tiles.append(ref[plan.place(base, head * plan.head_tiles + j)])
    return jnp.concatenate(tiles, axis=0)[:, : plan.width]


def each(count, step, carry):
    if count > 16:
        return lax.fori_loop(0, count, step, carry)
    for i in range(count):
        carry = step(i, carry)
    return carry


def scan_rows(plan, in_ref, start, out_ref, later):
    chips = plan.devices // 2
    columns = pl.ds(start, plan.span)

    def step(i, sums):
        chip = chips - 1 - i if later else i
        grown = []
        for core in range(2):
            row = 2 * chip + core
            out_ref[row, :, : plan.span] = sums[core]
            grown.append(sums[core] + in_ref[row, :, columns])
        return tuple(grown)

    zero = jnp.zeros((1, plan.span), F32)
    each(chips, step, (zero, zero))


def scan_norms(plan, in_ref, core, chip, later):
    columns = pl.ds(plan.span, plan.half * LANES)

    def step(i, total):
        take = (i > chip) if later else (i < chip)
        return total + jnp.where(take, in_ref[2 * i + core, :, columns], 0.0)

    return each(plan.devices // 2, step, jnp.zeros((1, plan.half * LANES), F32))


def causal_mask(length):
    row = lax.broadcasted_iota(jnp.int32, (length, length), 0)
    column = lax.broadcasted_iota(jnp.int32, (length, length), 1)
    return row <= column


def relu(x):
    return jnp.maximum(x, 0)


def block_state(plan, partner, ids_ref, k_ref, v_ref, out_ref):
    core = ids_ref[0]
    if partner:
        core = 1 - core
    ones = jnp.ones((SUB, plan.length), BF16)
    out_ref[plan.rows :, :] = jnp.zeros((plan.extra, LANES), F32)
    for h in range(plan.half):
        b, v = relu(plan.own(k_ref, core, h)), plan.own(v_ref, core, h)
        out_ref[h * plan.width : (h + 1) * plan.width, :] = wide(nt(b, v))
        out_ref[plan.rows + h : plan.rows + h + 1, :] = wide(nt(ones, b))[0:1]


def chip_state(plan, own_ref, got_ref, out_ref):
    for h in range(plan.half):
        rows = slice(h * plan.width, (h + 1) * plan.width)
        store_rows(plan, out_ref, 0, h, own_ref[rows, :] + got_ref[rows, :])
        row = slice(plan.rows + h, plan.rows + h + 1)
        norm = jnp.broadcast_to(own_ref[row, :] + got_ref[row, :], (plan.devices, LANES))
        out_ref[:, 0, plan.row_slot(h)] = norm
    store_padding(plan, out_ref, 0)


def pack_tokens(
    plan, ids_ref, q_ref, k_ref, v_ref, g_ref, q_got_ref, k_got_ref, v_got_ref, g_got_ref,
    a_ref, b_ref, vb_ref, gb_ref, low_ref, sum_ref, norm_ref,
):
    core = ids_ref[0]
    causal = causal_mask(plan.length)
    ones = jnp.ones((SUB, plan.length), BF16)
    sources = ((q_ref, q_got_ref), (k_ref, k_got_ref), (v_ref, v_got_ref), (g_ref, g_got_ref))
    for h in range(plan.half):
        for i in range(2):
            for n, (pair, ref) in enumerate(zip(sources, (a_ref, b_ref, vb_ref, gb_ref))):
                x = plan.other(pair[1], h).astype(BF16) if i else plan.own(pair[0], core, h)
                ref[i, h] = relu(x) if n < 2 else x
            a, b = a_ref[i, h], b_ref[i, h]
            scores = jnp.where(causal, tn(b, a), 0.0)
            sum_ref[i, h : h + 1, :] = 1.0 + jnp.sum(scores, axis=0, keepdims=True)
            low_ref[i, h] = scores.astype(BF16)
            norm_ref[i, h : h + 1, :] = wide(nt(ones, b))[0:1]


def middle(
    plan, ids_ref, in_ref, sum_ref, a_ref, g_ref, norm_ref, norm_in_ref,
    out_ref, inverse_ref, z_ref,
):
    core, chip = ids_ref[0], ids_ref[1]
    flags = (core.astype(F32), (1 - core).astype(F32))
    width = plan.width
    norms = scan_norms(plan, in_ref, core, chip, False)
    scan_rows(plan, in_ref, 0, out_ref, False)
    for h in range(plan.half):
        base = norm_in_ref[pl.ds(core * plan.shift + h, 1), :]
        base = base + norms[0:1, h * LANES : h * LANES + width]
        features, grads = [], []
        for i in range(2):
            z = base + flags[i] * norm_ref[1 - i, h : h + 1, :width]
            z_ref[i, h : h + 1, :] = wide(z)
            a = a_ref[i, h]
            den = sum_ref[i, h : h + 1, :] + added(nn(stacked_parts(z), a))
            inverse = 1.0 / den
            inverse_ref[i, h : h + 1, :] = inverse
            features.append(a)
            grads.append((g_ref[i, h].astype(F32) * inverse).astype(BF16))
        state = nt(jnp.concatenate(features, axis=1), jnp.concatenate(grads, axis=1))
        store_rows(plan, out_ref, plan.slots, h, state)
    store_padding(plan, out_ref, plan.slots)


def before_states(
    plan, ids_ref, a_ref, b_ref, v_ref, g_ref, low_ref, state_in_ref, before_ref, inner_ref
):
    core = ids_ref[0]
    own_first = core == 0
    late = (core.astype(F32), (1 - core).astype(F32))
    for h in range(plan.half):
        for i in range(2):
            inner = nn(v_ref[i, h], low_ref[i, h])
            inner_ref[i, h : h + 1, :] = jnp.sum(
                g_ref[i, h].astype(F32) * inner, axis=0, keepdims=True
            )
        b = jnp.where(own_first, b_ref[0, h].astype(F32), b_ref[1, h].astype(F32)).astype(BF16)
        v = jnp.where(own_first, v_ref[0, h].astype(F32), v_ref[1, h].astype(F32)).astype(BF16)
        first = nt(b, v)
        for i in range(2):
            before_ref[i, h] = state_in_ref[core * plan.shift + h] + late[i] * first


def outputs_grad(
    plan, ids_ref, in_ref, before_ref, a_ref, g_ref, inverse_ref, inner_ref,
    out_ref, product_ref, c_ref, m_ref,
):
    scan_rows(plan, in_ref, plan.span, out_ref, True)
    for h in range(plan.half):
        base = load_rows(plan, in_ref, 0, h)
        total = None
        for i in range(2):
            high, low = parts(base + before_ref[i, h])
            g, a = g_ref[i, h], a_ref[i, h]
            product = nn(jnp.concatenate([high, low], axis=0), g)
            product = product[: plan.width] + product[plan.width :]
            product_ref[i, h] = product
            inverse = inverse_ref[i, h : h + 1, :]
            along = jnp.sum(a.astype(F32) * product, axis=0, keepdims=True)
            c = -((along + inner_ref[i, h : h + 1, :]) * inverse) * inverse
            c_ref[i, h : h + 1, :] = c
            m = wide(added(nt(stacked_parts(c), a)))
            m_ref[i, h : h + 1, :] = m
            total = m if total is None else total + m
        out_ref[:, 0, plan.row_slot(h)] = jnp.broadcast_to(total, (plan.devices, LANES))


def query_grads(
    plan, ids_ref, a_ref, b_ref, v_ref, g_ref, inverse_ref, c_ref, z_ref, product_ref,
    own_ref, send_ref, mixed_ref,
):
    causal = causal_mask(plan.length)
    width = plan.width
    for i in (1, 0):
        columns = z_ref[i].T
        for h in range(plan.half):
            rows = slice(h * width, (h + 1) * width)
            inverse, c = inverse_ref[i, h : h + 1, :], c_ref[i, h : h + 1, :]
            u = (g_ref[i, h].astype(F32) * inverse).astype(BF16)
            mixed = jnp.where(causal, tn(v_ref[i, h], u) + c, 0.0).astype(BF16)
            mixed_ref[i, h] = mixed
            grad = product_ref[i, h] * inverse + columns[:width, h : h + 1] * c
            grad = jnp.where(a_ref[i, h].astype(F32) > 0, grad + nn(b_ref[i, h], mixed), 0.0)
            target = send_ref if i else own_ref
            target[rows, :] = grad


def after_states(
    plan, ids_ref, a_ref, g_ref, inverse_ref, low_ref, mixed_ref, grad_state_ref,
    final_0_ref, final_1_ref,
):
    core = ids_ref[0]
    own_first = core == 0
    early = ((1 - core).astype(F32), core.astype(F32))
    for h in range(plan.half):
        us = []
        for i, ref in enumerate((final_0_ref, final_1_ref)):
            u = (g_ref[i, h].astype(F32) * inverse_ref[i, h : h + 1, :]).astype(BF16)
            us.append(u)
            ref[1, h] = nt(a_ref[i, h], mixed_ref[i, h])
            ref[2, h] = nt(u, low_ref[i, h])
        a = jnp.where(own_first, a_ref[1, h].astype(F32), a_ref[0, h].astype(F32)).astype(BF16)
        u = jnp.where(own_first, us[1].astype(F32), us[0].astype(F32)).astype(BF16)
        second = nt(a, u)
        for i, ref in enumerate((final_0_ref, final_1_ref)):
            ref[0, h] = wide(grad_state_ref[core * plan.shift + h] + early[i] * second)


def key_value_grads(
    plan, i, ids_ref, in_ref, final_ref, grad_norm_ref, m_ref, b_ref, v_ref, key_ref, value_ref
):
    core, chip = ids_ref[0], ids_ref[1]
    flag = (core if i else 1 - core).astype(F32)
    width = plan.width
    norms = scan_norms(plan, in_ref, core, chip, True)
    zeros = plan.extra - plan.half
    norms = jnp.concatenate(
        [norms[:, h * LANES : (h + 1) * LANES] for h in range(plan.half)]
        + [jnp.zeros((zeros, LANES), F32)] * (zeros > 0), axis=0,
    )
    own_rows = [
        grad_norm_ref[pl.ds(core * plan.shift + h, 1), :] for h in range(plan.half)
    ] + [jnp.zeros((zeros, width), F32)] * (zeros > 0)
    norms = norms + wide(jnp.concatenate(own_rows, axis=0))
    columns = (norms + flag * m_ref[1 - i]).T
    for h in range(plan.half):
        rows = slice(h * width, (h + 1) * width)
        high, low = parts(load_rows(plan, in_ref, 0, h) + final_ref[0, h, :, :width])
        b, v = b_ref[i, h], v_ref[i, h]
        both = nn(jnp.concatenate([high, low], axis=0), v)
        key = both[:width] + both[width:] + columns[:width, h : h + 1] + final_ref[1, h]
        key = jnp.where(b.astype(F32) > 0, key, 0.0)
        value = tn(high, b) + tn(low, b) + final_ref[2, h]
        key_ref[rows, :] = key.astype(key_ref.dtype)
        value_ref[rows, :] = value.astype(value_ref.dtype)


def assemble(plan, ids_ref, *refs):
    core = ids_ref[0]
    count = len(refs) // 3
    start = pl.multiple_of(core * (plan.shift * plan.width), 16)
    rest = plan.shift * plan.width
    skip = plan.rows - rest
    other = pl.multiple_of((1 - core) * plan.rows, 16)
    source = pl.multiple_of((1 - core) * skip, 16)
    for own_ref, got_ref, out_ref in zip(refs[:count], refs[count : 2 * count], refs[2 * count :]):
        out_ref[pl.ds(start, plan.rows), :] = own_ref[...].astype(BF16)
        out_ref[pl.ds(other, rest), :] = got_ref[pl.ds(source, rest), :].astype(BF16)


def call(body, outs, args, room=FREE, flops=10_000_000, scratch=()):
    smem = pl.BlockSpec(memory_space=pltpu.SMEM)
    vmem = pl.BlockSpec(memory_space=pltpu.VMEM)
    in_specs = [smem if x.ndim == 1 else vmem for x in args]
    moved = sum(x.size * x.dtype.itemsize for x in (*args, *outs))
    return pl.pallas_call(
        body,
        out_shape=outs,
        in_specs=in_specs,
        out_specs=[vmem] * len(outs),
        scratch_shapes=list(scratch),
        compiler_params=pltpu.CompilerParams(vmem_limit_bytes=VMEM_BYTES - room),
        cost_estimate=pl.CostEstimate(flops=flops, bytes_accessed=moved, transcendentals=0),
    )(*args)


def shape(dims, dtype=F32):
    return jax.ShapeDtypeStruct(dims, dtype)


def per_device(
    queries, key_vectors, value_vectors, output_grad, state_in, norm_in, grad_state, grad_norm
):
    both = ("grp", "seq")
    length = queries.shape[0]
    heads, width = norm_in.shape
    devices = lax.axis_size("grp") * lax.axis_size("seq")
    plan = Plan(devices, length, heads, width)
    half = plan.half
    core = my_core()
    who = jnp.stack([core, my_device() >> 1]).astype(jnp.int32)
    q, k, v, g = queries.T, key_vectors.T, value_vectors.T, output_grad.T

    def bind(body):
        return functools.partial(body, plan)

    def exchange(x):
        return lax.all_to_all(x, both, 0, 0, tiled=True)

    def swap_columns(x):
        start = (1 - core) * (plan.shift * width)
        return pair_swap(lax.dynamic_slice_in_dim(x, start, plan.rows, 0).astype(F32))

    tokens = shape((plan.rows, length))
    packed = shape((2, half, width, length), BF16)
    products = shape((2, half, width, length))
    square = shape((2, half, length, length), BF16)
    states = shape((2, half, width, width))
    rows = shape((2, plan.extra, LANES))
    final = shape((3, half, width, LANES))
    block = shape((plan.rows + plan.extra, LANES))
    sent_single = shape((devices, 1, plan.span + half * LANES))
    sent_double = shape((devices, 1, 2 * plan.span))

    (send,) = call(functools.partial(block_state, plan, True), (block,), (who, k, v))
    block_got = pair_swap(send)
    (block_own,) = call(functools.partial(block_state, plan, False), (block,), (who, k, v))
    (sent,) = call(bind(chip_state), (sent_single,), (block_own, block_got))
    sent, k, v, q, g = lax.optimization_barrier((sent, k, v, q, g))
    got = exchange(sent)
    a, b, v, g, low, sums, norm = call(
        bind(pack_tokens),
        (packed, packed, packed, packed, square, rows, rows),
        (who, q, k, v, g, *(swap_columns(x) for x in (q, k, v, g))),
    )
    sent, inverse, z = call(
        bind(middle),
        (sent_double, rows, rows),
        (who, got, sums, a, g, norm, norm_in),
    )
    got = exchange(sent)
    before, inner = call(
        bind(before_states), (states, rows), (who, a, b, v, g, low, state_in)
    )
    sent, product, c, m = call(
        bind(outputs_grad),
        (sent_single, products, rows, rows),
        (who, got, before, a, g, inverse, inner),
    )
    got = exchange(sent)
    query, query_send, mixed = call(
        bind(query_grads), (tokens, tokens, square), (who, a, b, v, g, inverse, c, z, product)
    )
    query_got = pair_swap(query_send)
    final_0, final_1 = call(
        bind(after_states), (final, final), (who, a, g, inverse, low, mixed, grad_state)
    )
    whole = shape((heads * width, length), BF16)
    (query_grad,) = call(bind(assemble), (whole,), (who, query, query_got))
    got, query_grad = lax.optimization_barrier((got, query_grad))
    key_send, value_send = call(
        functools.partial(key_value_grads, plan, 1),
        (tokens, tokens),
        (who, got, final_1, grad_norm, m, b, v),
    )
    key_got, value_got = pair_swap(key_send), pair_swap(value_send)
    half_tokens = shape((plan.rows, length), BF16)
    key, value = call(
        functools.partial(key_value_grads, plan, 0),
        (half_tokens, half_tokens),
        (who, got, final_0, grad_norm, m, b, v),
    )
    key_grad, value_grad = call(
        bind(assemble), (whole, whole), (who, key, value, key_got, value_got)
    )
    return query_grad.T, key_grad.T, value_grad.T


def solution(mesh):
    rows = P(("grp", "seq"), None)
    return jax.shard_map(
        per_device,
        mesh=mesh,
        in_specs=(rows, rows, rows, rows, P(), P(), P(), P()),
        out_specs=(rows, rows, rows),
        check_vma=False,
    )
```

```python
import functools

import jax
import jax.numpy as jnp
from jax import lax
from jax.experimental import pallas as pl
from jax.experimental.pallas import tpu as pltpu
from jax.sharding import PartitionSpec as P

F32 = jnp.float32
BF16 = jnp.bfloat16
LANES = 128
SUB = 8
VMEM_BYTES = 67_043_328
FREE = 48 * 2**20


def dot(x, y, dims):
    return lax.dot_general(x, y, (dims, ((), ())), preferred_element_type=F32)


def nn(x, y):
    return dot(x, y, ((1,), (0,)))


def nt(x, y):
    return dot(x, y, ((1,), (1,)))


def tn(x, y):
    return dot(x, y, ((0,), (0,)))


def parts(x):
    high = x.astype(BF16)
    return high, (x - high.astype(F32)).astype(BF16)


def stacked_parts(row):
    high = row.astype(BF16)
    rest = row - high.astype(F32)
    middle = rest.astype(BF16)
    low = rest - middle.astype(F32)
    zeros = jnp.zeros((SUB - 3, row.shape[1]), F32)
    return jnp.concatenate([high.astype(F32), middle.astype(F32), low, zeros], axis=0).astype(BF16)


def added(rows):
    return rows[0:1] + rows[1:2] + rows[2:3]


class Plan:
    def __init__(self, devices, length, heads, width):
        self.devices, self.length, self.heads, self.width = devices, length, heads, width
        self.half = -(-heads // 2)
        self.shift = heads - self.half
        self.rows = self.half * width
        self.extra = SUB * -(-self.half // SUB)
        self.per_slot = devices // SUB
        self.head_tiles = width // SUB
        self.tiles = self.half * self.head_tiles
        self.spare = LANES - width
        self.pieces = width // self.spare if self.spare and width % self.spare == 0 else 0
        self.donors = self.tiles // (self.pieces + 1) if self.pieces else 0
        self.stored = self.tiles - self.donors
        self.slots = -(-self.stored // self.per_slot)
        self.span = self.slots * LANES

    def place(self, base, tile):
        slot, part = divmod(tile, self.per_slot)
        return pl.ds(part * SUB, SUB), 0, pl.ds((base + slot) * LANES, LANES)

    def columns(self, start, count):
        return slice(None), slice(None), pl.ds(start, count)

    def row_slot(self, head):
        return pl.ds((self.slots + head) * LANES, LANES)

    def own(self, ref, core, head):
        start = pl.multiple_of(core * (self.shift * self.width) + head * self.width, 16)
        return ref[pl.ds(start, self.width), :]

    def other(self, ref, head):
        return ref[head * self.width : (head + 1) * self.width, :]


def my_core():
    return lax.axis_index("seq") & 1


def my_device():
    return lax.axis_index("grp") * lax.axis_size("seq") + lax.axis_index("seq")


def pair_swap(x):
    size = lax.axis_size("seq")
    return lax.ppermute(x, "seq", [(i, i ^ 1) for i in range(size)])


def wide(tile):
    rows, columns = tile.shape
    if columns == LANES:
        return tile
    return jnp.concatenate([tile, jnp.zeros((rows, LANES - columns), tile.dtype)], axis=1)


def store_rows(plan, ref, base, head, block, held):
    block = wide(block)
    lane = lax.broadcasted_iota(jnp.int32, (SUB, LANES), 1)
    for j in range(plan.head_tiles):
        at = head * plan.head_tiles + j
        tile = block[j * SUB : (j + 1) * SUB, :]
        if at >= plan.stored:
            held[at - plan.stored] = tile
            continue
        if at < plan.donors * plan.pieces:
            donor, piece = divmod(at, plan.pieces)
            moved = pltpu.roll(held[donor], plan.width - piece * plan.spare, 1)
            tile = jnp.where(lane >= plan.width, moved, tile)
        ref[plan.place(base, at)] = tile


def store_padding(plan, ref, base):
    for tile in range(plan.stored, plan.slots * plan.per_slot):
        ref[plan.place(base, tile)] = jnp.zeros((SUB, LANES), F32)


def load_rows(plan, ref, base, head):
    lane = lax.broadcasted_iota(jnp.int32, (SUB, LANES), 1)
    tiles = []
    for j in range(plan.head_tiles):
        at = head * plan.head_tiles + j
        if at < plan.stored:
            tiles.append(ref[plan.place(base, at)])
            continue
        tile = None
        for piece in range(plan.pieces):
            part = ref[plan.place(base, (at - plan.stored) * plan.pieces + piece)]
            part = pltpu.roll(part, (LANES - plan.width + piece * plan.spare) % LANES, 1)
            tile = part if tile is None else jnp.where(lane >= piece * plan.spare, part, tile)
        tiles.append(tile)
    return jnp.concatenate(tiles, axis=0)[:, : plan.width]


def each(count, step, carry):
    if count > 16:
        return lax.fori_loop(0, count, step, carry)
    for i in range(count):
        carry = step(i, carry)
    return carry


def scan_rows(plan, in_ref, start, out_ref, later):
    chips = plan.devices // 2
    columns = pl.ds(start, plan.span)

    def step(i, sums):
        chip = chips - 1 - i if later else i
        grown = []
        for core in range(2):
            row = 2 * chip + core
            out_ref[row, :, : plan.span] = sums[core]
            grown.append(sums[core] + in_ref[row, :, columns])
        return tuple(grown)

    zero = jnp.zeros((1, plan.span), F32)
    each(chips, step, (zero, zero))


def scan_norms(plan, in_ref, core, chip, later):
    columns = pl.ds(plan.span, plan.half * LANES)

    def step(i, total):
        take = (i > chip) if later else (i < chip)
        return total + jnp.where(take, in_ref[2 * i + core, :, columns], 0.0)

    return each(plan.devices // 2, step, jnp.zeros((1, plan.half * LANES), F32))


def causal_mask(length):
    row = lax.broadcasted_iota(jnp.int32, (length, length), 0)
    column = lax.broadcasted_iota(jnp.int32, (length, length), 1)
    return row <= column


def scores_of(a, b, causal):
    return jnp.where(causal, tn(b, a), 0.0)


def relu(x):
    return jnp.maximum(x, 0)


def block_state(plan, partner, ids_ref, k_ref, v_ref, out_ref):
    core = ids_ref[0]
    if partner:
        core = 1 - core
    ones = jnp.ones((SUB, plan.length), BF16)
    out_ref[plan.rows :, :] = jnp.zeros((plan.extra, LANES), F32)
    for h in range(plan.half):
        b, v = relu(plan.own(k_ref, core, h)), plan.own(v_ref, core, h)
        out_ref[h * plan.width : (h + 1) * plan.width, :] = wide(nt(b, v))
        out_ref[plan.rows + h : plan.rows + h + 1, :] = wide(nt(ones, b))[0:1]


def chip_state(plan, own_ref, got_ref, out_ref):
    held = {}
    for h in reversed(range(plan.half)):
        rows = slice(h * plan.width, (h + 1) * plan.width)
        store_rows(plan, out_ref, 0, h, own_ref[rows, :] + got_ref[rows, :], held)
        row = slice(plan.rows + h, plan.rows + h + 1)
        norm = jnp.broadcast_to(own_ref[row, :] + got_ref[row, :], (plan.devices, LANES))
        out_ref[:, 0, plan.row_slot(h)] = norm
    store_padding(plan, out_ref, 0)


def pack_tokens(
    plan, ids_ref, q_ref, k_ref, v_ref, g_ref, q_got_ref, k_got_ref, v_got_ref, g_got_ref,
    a_ref, b_ref, vb_ref, gb_ref, sum_ref, norm_ref,
):
    core = ids_ref[0]
    causal = causal_mask(plan.length)
    ones = jnp.ones((SUB, plan.length), BF16)
    sources = ((q_ref, q_got_ref), (k_ref, k_got_ref), (v_ref, v_got_ref), (g_ref, g_got_ref))
    for h in range(plan.half):
        for i in range(2):
            for n, (pair, ref) in enumerate(zip(sources, (a_ref, b_ref, vb_ref, gb_ref))):
                x = plan.other(pair[1], h).astype(BF16) if i else plan.own(pair[0], core, h)
                ref[i, h] = relu(x) if n < 2 else x
            a, b = a_ref[i, h], b_ref[i, h]
            scores = scores_of(a, b, causal)
            sum_ref[i, h : h + 1, :] = 1.0 + jnp.sum(scores, axis=0, keepdims=True)
            norm_ref[i, h : h + 1, :] = wide(nt(ones, b))[0:1]


def middle(
    plan, ids_ref, in_ref, sum_ref, a_ref, g_ref, norm_ref, norm_in_ref,
    out_ref, inverse_ref, z_ref,
):
    core, chip = ids_ref[0], ids_ref[1]
    flags = (core.astype(F32), (1 - core).astype(F32))
    width = plan.width
    norms = scan_norms(plan, in_ref, core, chip, False)
    scan_rows(plan, in_ref, 0, out_ref, False)
    held = {}
    for h in reversed(range(plan.half)):
        base = norm_in_ref[pl.ds(core * plan.shift + h, 1), :]
        base = base + norms[0:1, h * LANES : h * LANES + width]
        features, grads = [], []
        for i in range(2):
            z = base + flags[i] * norm_ref[1 - i, h : h + 1, :width]
            z_ref[i, h : h + 1, :] = wide(z)
            a = a_ref[i, h]
            den = sum_ref[i, h : h + 1, :] + added(nn(stacked_parts(z), a))
            inverse = 1.0 / den
            inverse_ref[i, h : h + 1, :] = inverse
            features.append(a)
            grads.append((g_ref[i, h].astype(F32) * inverse).astype(BF16))
        state = nt(jnp.concatenate(features, axis=1), jnp.concatenate(grads, axis=1))
        store_rows(plan, out_ref, plan.slots, h, state, held)
    store_padding(plan, out_ref, plan.slots)


def before_states(
    plan, ids_ref, a_ref, b_ref, v_ref, g_ref, state_in_ref, before_ref, inner_ref
):
    core = ids_ref[0]
    causal = causal_mask(plan.length)
    own_first = core == 0
    late = (core.astype(F32), (1 - core).astype(F32))
    for h in range(plan.half):
        for i in range(2):
            low = scores_of(a_ref[i, h], b_ref[i, h], causal).astype(BF16)
            inner = nn(v_ref[i, h], low)
            inner_ref[i, h : h + 1, :] = jnp.sum(
                g_ref[i, h].astype(F32) * inner, axis=0, keepdims=True
            )
        b = jnp.where(own_first, b_ref[0, h].astype(F32), b_ref[1, h].astype(F32)).astype(BF16)
        v = jnp.where(own_first, v_ref[0, h].astype(F32), v_ref[1, h].astype(F32)).astype(BF16)
        first = nt(b, v)
        for i in range(2):
            before_ref[i, h] = state_in_ref[core * plan.shift + h] + late[i] * first


def outputs_grad(
    plan, ids_ref, in_ref, before_ref, a_ref, g_ref, inverse_ref, inner_ref,
    out_ref, product_ref, c_ref, m_ref,
):
    scan_rows(plan, in_ref, plan.span, out_ref, True)
    for h in range(plan.half):
        base = load_rows(plan, in_ref, 0, h)
        total = None
        for i in range(2):
            high, low = parts(base + before_ref[i, h])
            g, a = g_ref[i, h], a_ref[i, h]
            product = nn(jnp.concatenate([high, low], axis=0), g)
            product = product[: plan.width] + product[plan.width :]
            product_ref[i, h] = product
            inverse = inverse_ref[i, h : h + 1, :]
            along = jnp.sum(a.astype(F32) * product, axis=0, keepdims=True)
            c = -((along + inner_ref[i, h : h + 1, :]) * inverse) * inverse
            c_ref[i, h : h + 1, :] = c
            m = wide(added(nt(stacked_parts(c), a)))
            m_ref[i, h : h + 1, :] = m
            total = m if total is None else total + m
        out_ref[:, 0, plan.row_slot(h)] = jnp.broadcast_to(total, (plan.devices, LANES))


def query_grads(
    plan, ids_ref, a_ref, b_ref, v_ref, g_ref, inverse_ref, c_ref, z_ref, product_ref,
    own_ref, send_ref, mixed_ref,
):
    causal = causal_mask(plan.length)
    width = plan.width
    for i in (1, 0):
        columns = z_ref[i].T
        for h in range(plan.half):
            rows = slice(h * width, (h + 1) * width)
            inverse, c = inverse_ref[i, h : h + 1, :], c_ref[i, h : h + 1, :]
            u = (g_ref[i, h].astype(F32) * inverse).astype(BF16)
            mixed = jnp.where(causal, tn(v_ref[i, h], u) + c, 0.0).astype(BF16)
            mixed_ref[i, h] = mixed
            grad = product_ref[i, h] * inverse + columns[:width, h : h + 1] * c
            grad = jnp.where(a_ref[i, h].astype(F32) > 0, grad + nn(b_ref[i, h], mixed), 0.0)
            target = send_ref if i else own_ref
            target[rows, :] = grad


def after_states(
    plan, ids_ref, a_ref, b_ref, g_ref, inverse_ref, mixed_ref, grad_state_ref, *refs
):
    core = ids_ref[0]
    causal = causal_mask(plan.length)
    own_first = core == 0
    early = ((1 - core).astype(F32), core.astype(F32))
    for h in range(plan.half):
        us = []
        for i in range(2):
            u = (g_ref[i, h].astype(F32) * inverse_ref[i, h : h + 1, :]).astype(BF16)
            us.append(u)
            low = scores_of(a_ref[i, h], b_ref[i, h], causal).astype(BF16)
            refs[3 * i + 1][h] = nt(a_ref[i, h], mixed_ref[i, h])
            refs[3 * i + 2][h] = nt(u, low)
        a = jnp.where(own_first, a_ref[1, h].astype(F32), a_ref[0, h].astype(F32)).astype(BF16)
        u = jnp.where(own_first, us[1].astype(F32), us[0].astype(F32)).astype(BF16)
        second = nt(a, u)
        for i in range(2):
            refs[3 * i][h] = grad_state_ref[core * plan.shift + h] + early[i] * second


def key_value_grads(
    plan, i, ids_ref, in_ref, after_ref, key_in_ref, value_in_ref, grad_norm_ref, m_ref, b_ref,
    v_ref, key_ref, value_ref,
):
    core, chip = ids_ref[0], ids_ref[1]
    flag = (core if i else 1 - core).astype(F32)
    width = plan.width
    norms = scan_norms(plan, in_ref, core, chip, True)
    zeros = plan.extra - plan.half
    norms = jnp.concatenate(
        [norms[:, h * LANES : (h + 1) * LANES] for h in range(plan.half)]
        + [jnp.zeros((zeros, LANES), F32)] * (zeros > 0), axis=0,
    )
    own_rows = [
        grad_norm_ref[pl.ds(core * plan.shift + h, 1), :] for h in range(plan.half)
    ] + [jnp.zeros((zeros, width), F32)] * (zeros > 0)
    norms = norms + wide(jnp.concatenate(own_rows, axis=0))
    columns = (norms + flag * m_ref[1 - i]).T
    for h in range(plan.half):
        rows = slice(h * width, (h + 1) * width)
        high, low = parts(load_rows(plan, in_ref, 0, h) + after_ref[h])
        b, v = b_ref[i, h], v_ref[i, h]
        both = nn(jnp.concatenate([high, low], axis=0), v)
        key = both[:width] + both[width:] + columns[:width, h : h + 1] + key_in_ref[h]
        key = jnp.where(b.astype(F32) > 0, key, 0.0)
        value = tn(high, b) + tn(low, b) + value_in_ref[h]
        key_ref[rows, :] = key.astype(key_ref.dtype)
        value_ref[rows, :] = value.astype(value_ref.dtype)


def assemble(plan, ids_ref, *refs):
    core = ids_ref[0]
    count = len(refs) // 3
    start = pl.multiple_of(core * (plan.shift * plan.width), 16)
    rest = plan.shift * plan.width
    skip = plan.rows - rest
    other = pl.multiple_of((1 - core) * plan.rows, 16)
    source = pl.multiple_of((1 - core) * skip, 16)
    for own_ref, got_ref, out_ref in zip(refs[:count], refs[count : 2 * count], refs[2 * count :]):
        out_ref[pl.ds(start, plan.rows), :] = own_ref[...].astype(BF16)
        out_ref[pl.ds(other, rest), :] = got_ref[pl.ds(source, rest), :].astype(BF16)


def call(body, outs, args, room=FREE, flops=10_000_000, scratch=()):
    smem = pl.BlockSpec(memory_space=pltpu.SMEM)
    vmem = pl.BlockSpec(memory_space=pltpu.VMEM)
    in_specs = [smem if x.ndim == 1 else vmem for x in args]
    moved = sum(x.size * x.dtype.itemsize for x in (*args, *outs))
    return pl.pallas_call(
        body,
        out_shape=outs,
        in_specs=in_specs,
        out_specs=[vmem] * len(outs),
        scratch_shapes=list(scratch),
        compiler_params=pltpu.CompilerParams(vmem_limit_bytes=VMEM_BYTES - room),
        cost_estimate=pl.CostEstimate(flops=flops, bytes_accessed=moved, transcendentals=0),
    )(*args)


def shape(dims, dtype=F32):
    return jax.ShapeDtypeStruct(dims, dtype)


def per_device(
    queries, key_vectors, value_vectors, output_grad, state_in, norm_in, grad_state, grad_norm
):
    both = ("grp", "seq")
    length = queries.shape[0]
    heads, width = norm_in.shape
    devices = lax.axis_size("grp") * lax.axis_size("seq")
    plan = Plan(devices, length, heads, width)
    half = plan.half
    core = my_core()
    who = jnp.stack([core, my_device() >> 1]).astype(jnp.int32)
    q, k, v, g = queries.T, key_vectors.T, value_vectors.T, output_grad.T

    def bind(body):
        return functools.partial(body, plan)

    def exchange(x):
        return lax.all_to_all(x, both, 0, 0, tiled=True)

    def swap_columns(x):
        start = (1 - core) * (plan.shift * width)
        return pair_swap(lax.dynamic_slice_in_dim(x, start, plan.rows, 0).astype(F32))

    tokens = shape((plan.rows, length))
    packed = shape((2, half, width, length), BF16)
    products = shape((2, half, width, length))
    square = shape((2, half, length, length), BF16)
    states = shape((2, half, width, width))
    rows = shape((2, plan.extra, LANES))
    after = shape((half, width, width))
    part = shape((half, width, length))
    block = shape((plan.rows + plan.extra, LANES))
    sent_single = shape((devices, 1, plan.span + half * LANES))
    sent_double = shape((devices, 1, 2 * plan.span))

    (send,) = call(functools.partial(block_state, plan, True), (block,), (who, k, v))
    block_got = pair_swap(send)
    (block_own,) = call(functools.partial(block_state, plan, False), (block,), (who, k, v))
    (sent,) = call(bind(chip_state), (sent_single,), (block_own, block_got))
    sent, k, v, q, g = lax.optimization_barrier((sent, k, v, q, g))
    got = exchange(sent)
    a, b, v, g, sums, norm = call(
        bind(pack_tokens),
        (packed, packed, packed, packed, rows, rows),
        (who, q, k, v, g, *(swap_columns(x) for x in (q, k, v, g))),
    )
    sent, inverse, z = call(
        bind(middle),
        (sent_double, rows, rows),
        (who, got, sums, a, g, norm, norm_in),
    )
    got = exchange(sent)
    before, inner = call(
        bind(before_states), (states, rows), (who, a, b, v, g, state_in)
    )
    sent, product, c, m = call(
        bind(outputs_grad),
        (sent_single, products, rows, rows),
        (who, got, before, a, g, inverse, inner),
    )
    got = exchange(sent)
    query, query_send, mixed = call(
        bind(query_grads), (tokens, tokens, square), (who, a, b, v, g, inverse, c, z, product)
    )
    query_got = pair_swap(query_send)
    finals = call(
        bind(after_states), (after, part, part) * 2, (who, a, b, g, inverse, mixed, grad_state)
    )
    whole = shape((heads * width, length), BF16)
    (query_grad,) = call(bind(assemble), (whole,), (who, query, query_got))
    got, query_grad = lax.optimization_barrier((got, query_grad))
    key_send, value_send = call(
        functools.partial(key_value_grads, plan, 1),
        (tokens, tokens),
        (who, got, *finals[3:], grad_norm, m, b, v),
    )
    key_got, value_got = pair_swap(key_send), pair_swap(value_send)
    half_tokens = shape((plan.rows, length), BF16)
    key, value = call(
        functools.partial(key_value_grads, plan, 0),
        (half_tokens, half_tokens),
        (who, got, *finals[:3], grad_norm, m, b, v),
    )
    key_grad, value_grad = call(
        bind(assemble), (whole, whole), (who, key, value, key_got, value_got)
    )
    return query_grad.T, key_grad.T, value_grad.T


def solution(mesh):
    rows = P(("grp", "seq"), None)
    return jax.shard_map(
        per_device,
        mesh=mesh,
        in_specs=(rows, rows, rows, rows, P(), P(), P(), P()),
        out_specs=(rows, rows, rows),
        check_vma=False,
    )
```

```python
import functools

import jax
import jax.numpy as jnp
from jax import lax
from jax.experimental import pallas as pl
from jax.experimental.pallas import tpu as pltpu
from jax.sharding import PartitionSpec as P

F32 = jnp.float32
BF16 = jnp.bfloat16
LANES = 128
SUB = 8
VMEM_BYTES = 67_043_328
FREE = 48 * 2**20


def dot(x, y, dims):
    return lax.dot_general(x, y, (dims, ((), ())), preferred_element_type=F32)


def nn(x, y):
    return dot(x, y, ((1,), (0,)))


def nt(x, y):
    return dot(x, y, ((1,), (1,)))


def tn(x, y):
    return dot(x, y, ((0,), (0,)))


def parts(x):
    high = x.astype(BF16)
    return high, (x - high.astype(F32)).astype(BF16)


def stacked_parts(row):
    high = row.astype(BF16)
    rest = row - high.astype(F32)
    middle = rest.astype(BF16)
    low = rest - middle.astype(F32)
    zeros = jnp.zeros((SUB - 3, row.shape[1]), F32)
    return jnp.concatenate([high.astype(F32), middle.astype(F32), low, zeros], axis=0).astype(BF16)


def added(rows):
    return rows[0:1] + rows[1:2] + rows[2:3]


class Plan:
    def __init__(self, devices, length, heads, width):
        self.devices, self.length, self.heads, self.width = devices, length, heads, width
        self.half = -(-heads // 2)
        self.shift = heads - self.half
        self.rows = self.half * width
        self.extra = SUB * -(-self.half // SUB)
        self.per_slot = devices // SUB
        self.head_tiles = width // SUB
        self.tiles = self.half * self.head_tiles
        self.spare = LANES - width
        self.pieces = width // self.spare if self.spare and width % self.spare == 0 else 0
        self.donors = self.tiles // (self.pieces + 1) if self.pieces else 0
        self.stored = self.tiles - self.donors
        self.whole = self.stored // devices
        self.slots = self.whole * SUB + -(-(self.stored - self.whole * devices) // self.per_slot)
        self.span = self.slots * LANES

    def put(self, ref, base, tile, value):
        if tile < self.whole * self.devices:
            slot, piece = divmod(tile, self.devices)
            columns = pl.ds((base + slot * SUB) * LANES, SUB * LANES)
            ref[piece, :, columns] = value.reshape(1, SUB * LANES)
        else:
            ref[self.place(base, tile)] = value

    def get(self, ref, base, tile):
        if tile < self.whole * self.devices:
            slot, piece = divmod(tile, self.devices)
            columns = pl.ds((base + slot * SUB) * LANES, SUB * LANES)
            return ref[piece, :, columns].reshape(SUB, LANES)
        return ref[self.place(base, tile)]

    def place(self, base, tile):
        slot, part = divmod(tile - self.whole * self.devices, self.per_slot)
        slot += self.whole * SUB
        return pl.ds(part * SUB, SUB), 0, pl.ds((base + slot) * LANES, LANES)

    def own(self, ref, core, head):
        start = pl.multiple_of(core * (self.shift * self.width) + head * self.width, 16)
        return ref[pl.ds(start, self.width), :]

    def other(self, ref, head):
        return ref[head * self.width : (head + 1) * self.width, :]


def my_core():
    return lax.axis_index("seq") & 1


def my_device():
    return lax.axis_index("grp") * lax.axis_size("seq") + lax.axis_index("seq")


def pair_swap(x):
    size = lax.axis_size("seq")
    return lax.ppermute(x, "seq", [(i, i ^ 1) for i in range(size)])


def wide(tile):
    rows, columns = tile.shape
    if columns == LANES:
        return tile
    return jnp.concatenate([tile, jnp.zeros((rows, LANES - columns), tile.dtype)], axis=1)


def store_rows(plan, ref, base, head, block, held):
    block = wide(block)
    lane = lax.broadcasted_iota(jnp.int32, (SUB, LANES), 1)
    for j in range(plan.head_tiles):
        at = head * plan.head_tiles + j
        tile = block[j * SUB : (j + 1) * SUB, :]
        if at >= plan.stored:
            held[at - plan.stored] = tile
            continue
        if at < plan.donors * plan.pieces:
            donor, piece = divmod(at, plan.pieces)
            moved = pltpu.roll(held[donor], plan.width - piece * plan.spare, 1)
            tile = jnp.where(lane >= plan.width, moved, tile)
        plan.put(ref, base, at, tile)


def store_padding(plan, ref, base):
    rest = (plan.slots - plan.whole * SUB) * plan.per_slot + plan.whole * plan.devices
    for tile in range(plan.stored, rest):
        ref[plan.place(base, tile)] = jnp.zeros((SUB, LANES), F32)


def store_norms(plan, ref, rows):
    rows = rows.reshape(1, plan.extra * LANES)[:, : plan.half * LANES]
    for piece in range(plan.devices):
        ref[piece, :, pl.ds(plan.span, plan.half * LANES)] = rows


def load_rows(plan, ref, base, head):
    lane = lax.broadcasted_iota(jnp.int32, (SUB, LANES), 1)
    tiles = []
    for j in range(plan.head_tiles):
        at = head * plan.head_tiles + j
        if at < plan.stored:
            tiles.append(plan.get(ref, base, at))
            continue
        tile = None
        for piece in range(plan.pieces):
            part = plan.get(ref, base, (at - plan.stored) * plan.pieces + piece)
            part = pltpu.roll(part, (LANES - plan.width + piece * plan.spare) % LANES, 1)
            tile = part if tile is None else jnp.where(lane >= piece * plan.spare, part, tile)
        tiles.append(tile)
    return jnp.concatenate(tiles, axis=0)[:, : plan.width]


def each(count, step, carry):
    if count > 16:
        return lax.fori_loop(0, count, step, carry)
    for i in range(count):
        carry = step(i, carry)
    return carry


def scan_rows(plan, in_ref, start, out_ref, later):
    chips = plan.devices // 2
    columns = pl.ds(start, plan.span)

    def step(i, sums):
        chip = chips - 1 - i if later else i
        grown = []
        for core in range(2):
            row = 2 * chip + core
            out_ref[row, :, : plan.span] = sums[core]
            grown.append(sums[core] + in_ref[row, :, columns])
        return tuple(grown)

    zero = jnp.zeros((1, plan.span), F32)
    each(chips, step, (zero, zero))


def scan_norms(plan, in_ref, core, chip, later):
    columns = pl.ds(plan.span, plan.half * LANES)

    def step(i, total):
        take = (i > chip) if later else (i < chip)
        return total + jnp.where(take, in_ref[2 * i + core, :, columns], 0.0)

    return each(plan.devices // 2, step, jnp.zeros((1, plan.half * LANES), F32))


def causal_mask(length):
    row = lax.broadcasted_iota(jnp.int32, (length, length), 0)
    column = lax.broadcasted_iota(jnp.int32, (length, length), 1)
    return row <= column


def scores_of(a, b, causal):
    return jnp.where(causal, tn(b, a), 0.0)


def relu(x):
    return jnp.maximum(x, 0)


def block_states(plan, k_ref, v_ref, send_ref, own_ref):
    core = my_core()
    ones = jnp.ones((SUB, plan.length), BF16)
    for side, out_ref in ((1 - core, send_ref), (core, own_ref)):
        out_ref[plan.rows :, :] = jnp.zeros((plan.extra, LANES), F32)
        for h in range(plan.half):
            b, v = relu(plan.own(k_ref, side, h)), plan.own(v_ref, side, h)
            out_ref[h * plan.width : (h + 1) * plan.width, :] = wide(nt(b, v))
            out_ref[plan.rows + h : plan.rows + h + 1, :] = wide(nt(ones, b))[0:1]


def chip_state(plan, own_ref, got_ref, out_ref):
    held = {}
    for h in reversed(range(plan.half)):
        rows = slice(h * plan.width, (h + 1) * plan.width)
        store_rows(plan, out_ref, 0, h, own_ref[rows, :] + got_ref[rows, :], held)
    store_padding(plan, out_ref, 0)
    store_norms(plan, out_ref, own_ref[plan.rows :, :] + got_ref[plan.rows :, :])


def pack_tokens(
    plan, q_ref, k_ref, v_ref, g_ref, q_got_ref, k_got_ref, v_got_ref, g_got_ref,
    a_ref, b_ref, vb_ref, gb_ref, sum_ref, norm_ref,
):
    core = my_core()
    causal = causal_mask(plan.length)
    ones = jnp.ones((SUB, plan.length), BF16)
    sources = ((q_ref, q_got_ref), (k_ref, k_got_ref), (v_ref, v_got_ref), (g_ref, g_got_ref))
    for h in range(plan.half):
        for i in range(2):
            for n, (pair, ref) in enumerate(zip(sources, (a_ref, b_ref, vb_ref, gb_ref))):
                x = plan.other(pair[1], h).astype(BF16) if i else plan.own(pair[0], core, h)
                ref[i, h] = relu(x) if n < 2 else x
            a, b = a_ref[i, h], b_ref[i, h]
            scores = scores_of(a, b, causal)
            sum_ref[i, h : h + 1, :] = 1.0 + jnp.sum(scores, axis=0, keepdims=True)
            norm_ref[i, h : h + 1, :] = wide(nt(ones, b))[0:1]


def middle(
    plan, in_ref, sum_ref, a_ref, g_ref, norm_ref, norm_in_ref,
    out_ref, inverse_ref, z_ref,
):
    core, chip = my_core(), my_device() >> 1
    flags = (core.astype(F32), (1 - core).astype(F32))
    width = plan.width
    norms = scan_norms(plan, in_ref, core, chip, False)
    scan_rows(plan, in_ref, 0, out_ref, False)
    held = {}
    for h in reversed(range(plan.half)):
        base = norm_in_ref[pl.ds(core * plan.shift + h, 1), :]
        base = base + norms[0:1, h * LANES : h * LANES + width]
        features, grads = [], []
        for i in range(2):
            z = base + flags[i] * norm_ref[1 - i, h : h + 1, :width]
            z_ref[i, h : h + 1, :] = wide(z)
            a = a_ref[i, h]
            den = sum_ref[i, h : h + 1, :] + added(nn(stacked_parts(z), a))
            inverse = 1.0 / den
            inverse_ref[i, h : h + 1, :] = inverse
            features.append(a)
            grads.append((g_ref[i, h].astype(F32) * inverse).astype(BF16))
        state = nt(jnp.concatenate(features, axis=1), jnp.concatenate(grads, axis=1))
        store_rows(plan, out_ref, plan.slots, h, state, held)
    store_padding(plan, out_ref, plan.slots)


def before_states(
    plan, a_ref, b_ref, v_ref, g_ref, state_in_ref, before_ref, inner_ref
):
    core = my_core()
    causal = causal_mask(plan.length)
    own_first = core == 0
    late = (core.astype(F32), (1 - core).astype(F32))
    for h in range(plan.half):
        for i in range(2):
            low = scores_of(a_ref[i, h], b_ref[i, h], causal).astype(BF16)
            inner = nn(v_ref[i, h], low)
            inner_ref[i, h : h + 1, :] = jnp.sum(
                g_ref[i, h].astype(F32) * inner, axis=0, keepdims=True
            )
        b = jnp.where(own_first, b_ref[0, h].astype(F32), b_ref[1, h].astype(F32)).astype(BF16)
        v = jnp.where(own_first, v_ref[0, h].astype(F32), v_ref[1, h].astype(F32)).astype(BF16)
        first = nt(b, v)
        for i in range(2):
            before_ref[i, h] = state_in_ref[core * plan.shift + h] + late[i] * first


def outputs_grad(
    plan, in_ref, before_ref, a_ref, g_ref, inverse_ref, inner_ref,
    out_ref, product_ref, c_ref, m_ref,
):
    scan_rows(plan, in_ref, plan.span, out_ref, True)
    totals = []
    for h in range(plan.half):
        base = load_rows(plan, in_ref, 0, h)
        total = None
        for i in range(2):
            high, low = parts(base + before_ref[i, h])
            g, a = g_ref[i, h], a_ref[i, h]
            product = nn(jnp.concatenate([high, low], axis=0), g)
            product = product[: plan.width] + product[plan.width :]
            product_ref[i, h] = product
            inverse = inverse_ref[i, h : h + 1, :]
            along = jnp.sum(a.astype(F32) * product, axis=0, keepdims=True)
            c = -((along + inner_ref[i, h : h + 1, :]) * inverse) * inverse
            c_ref[i, h : h + 1, :] = c
            m = wide(added(nt(stacked_parts(c), a)))
            m_ref[i, h : h + 1, :] = m
            total = m if total is None else total + m
        totals.append(total)
    totals += [jnp.zeros((1, LANES), F32)] * (plan.extra - plan.half)
    store_norms(plan, out_ref, jnp.concatenate(totals, axis=0))


def query_grads(
    plan, a_ref, b_ref, v_ref, g_ref, inverse_ref, c_ref, z_ref, product_ref,
    own_ref, send_ref, mixed_ref,
):
    causal = causal_mask(plan.length)
    width = plan.width
    for i in (1, 0):
        columns = z_ref[i].T
        for h in range(plan.half):
            rows = slice(h * width, (h + 1) * width)
            inverse, c = inverse_ref[i, h : h + 1, :], c_ref[i, h : h + 1, :]
            u = (g_ref[i, h].astype(F32) * inverse).astype(BF16)
            mixed = jnp.where(causal, tn(v_ref[i, h], u) + c, 0.0).astype(BF16)
            mixed_ref[i, h] = mixed
            grad = product_ref[i, h] * inverse + columns[:width, h : h + 1] * c
            grad = jnp.where(a_ref[i, h].astype(F32) > 0, grad + nn(b_ref[i, h], mixed), 0.0)
            target = send_ref if i else own_ref
            target[rows, :] = grad


def after_states(
    plan, a_ref, b_ref, g_ref, inverse_ref, mixed_ref, grad_state_ref, *refs
):
    core = my_core()
    causal = causal_mask(plan.length)
    own_first = core == 0
    early = ((1 - core).astype(F32), core.astype(F32))
    for h in range(plan.half):
        us = []
        for i in range(2):
            u = (g_ref[i, h].astype(F32) * inverse_ref[i, h : h + 1, :]).astype(BF16)
            us.append(u)
            low = scores_of(a_ref[i, h], b_ref[i, h], causal).astype(BF16)
            refs[3 * i + 1][h] = nt(a_ref[i, h], mixed_ref[i, h])
            refs[3 * i + 2][h] = nt(u, low)
        a = jnp.where(own_first, a_ref[1, h].astype(F32), a_ref[0, h].astype(F32)).astype(BF16)
        u = jnp.where(own_first, us[1].astype(F32), us[0].astype(F32)).astype(BF16)
        second = nt(a, u)
        for i in range(2):
            refs[3 * i][h] = grad_state_ref[core * plan.shift + h] + early[i] * second


def key_value_grads(
    plan, i, in_ref, after_ref, key_in_ref, value_in_ref, grad_norm_ref, m_ref, b_ref,
    v_ref, key_ref, value_ref,
):
    core, chip = my_core(), my_device() >> 1
    flag = (core if i else 1 - core).astype(F32)
    width = plan.width
    norms = scan_norms(plan, in_ref, core, chip, True)
    zeros = plan.extra - plan.half
    norms = jnp.concatenate(
        [norms[:, h * LANES : (h + 1) * LANES] for h in range(plan.half)]
        + [jnp.zeros((zeros, LANES), F32)] * (zeros > 0), axis=0,
    )
    own_rows = [
        grad_norm_ref[pl.ds(core * plan.shift + h, 1), :] for h in range(plan.half)
    ] + [jnp.zeros((zeros, width), F32)] * (zeros > 0)
    norms = norms + wide(jnp.concatenate(own_rows, axis=0))
    columns = (norms + flag * m_ref[1 - i]).T
    for h in range(plan.half):
        rows = slice(h * width, (h + 1) * width)
        high, low = parts(load_rows(plan, in_ref, 0, h) + after_ref[h])
        b, v = b_ref[i, h], v_ref[i, h]
        both = nn(jnp.concatenate([high, low], axis=0), v)
        key = both[:width] + both[width:] + columns[:width, h : h + 1] + key_in_ref[h]
        key = jnp.where(b.astype(F32) > 0, key, 0.0)
        value = tn(high, b) + tn(low, b) + value_in_ref[h]
        key_ref[rows, :] = key.astype(key_ref.dtype)
        value_ref[rows, :] = value.astype(value_ref.dtype)


def assemble(plan, *refs):
    core = my_core()
    count = len(refs) // 3
    start = pl.multiple_of(core * (plan.shift * plan.width), 16)
    rest = plan.shift * plan.width
    skip = plan.rows - rest
    other = pl.multiple_of((1 - core) * plan.rows, 16)
    source = pl.multiple_of((1 - core) * skip, 16)
    for own_ref, got_ref, out_ref in zip(refs[:count], refs[count : 2 * count], refs[2 * count :]):
        out_ref[pl.ds(start, plan.rows), :] = own_ref[...].astype(BF16)
        out_ref[pl.ds(other, rest), :] = got_ref[pl.ds(source, rest), :].astype(BF16)


def call(body, outs, args, room=FREE, flops=10_000_000, scratch=()):
    smem = pl.BlockSpec(memory_space=pltpu.SMEM)
    vmem = pl.BlockSpec(memory_space=pltpu.VMEM)
    in_specs = [smem if x.ndim == 1 else vmem for x in args]
    moved = sum(x.size * x.dtype.itemsize for x in (*args, *outs))
    return pl.pallas_call(
        body,
        out_shape=outs,
        in_specs=in_specs,
        out_specs=[vmem] * len(outs),
        scratch_shapes=list(scratch),
        compiler_params=pltpu.CompilerParams(vmem_limit_bytes=VMEM_BYTES - room),
        cost_estimate=pl.CostEstimate(flops=flops, bytes_accessed=moved, transcendentals=0),
    )(*args)


def shape(dims, dtype=F32):
    return jax.ShapeDtypeStruct(dims, dtype)


def per_device(
    queries, key_vectors, value_vectors, output_grad, state_in, norm_in, grad_state, grad_norm
):
    both = ("grp", "seq")
    length = queries.shape[0]
    heads, width = norm_in.shape
    devices = lax.axis_size("grp") * lax.axis_size("seq")
    plan = Plan(devices, length, heads, width)
    half = plan.half
    core = my_core()
    q, k, v, g = queries.T, key_vectors.T, value_vectors.T, output_grad.T

    def bind(body):
        return functools.partial(body, plan)

    def exchange(x):
        return lax.all_to_all(x, both, 0, 0, tiled=True)

    def swap_columns(x):
        start = (1 - core) * (plan.shift * width)
        return pair_swap(lax.dynamic_slice_in_dim(x, start, plan.rows, 0).astype(F32))

    tokens = shape((plan.rows, length))
    packed = shape((2, half, width, length), BF16)
    products = shape((2, half, width, length))
    square = shape((2, half, length, length), BF16)
    states = shape((2, half, width, width))
    rows = shape((2, plan.extra, LANES))
    after = shape((half, width, width))
    part = shape((half, width, length))
    block = shape((plan.rows + plan.extra, LANES))
    sent_single = shape((devices, 1, plan.span + half * LANES))
    sent_double = shape((devices, 1, 2 * plan.span))

    send, block_own = call(bind(block_states), (block, block), (k, v))
    block_got = pair_swap(send)
    (sent,) = call(bind(chip_state), (sent_single,), (block_own, block_got))
    sent, k, v, q, g = lax.optimization_barrier((sent, k, v, q, g))
    got = exchange(sent)
    a, b, v, g, sums, norm = call(
        bind(pack_tokens),
        (packed, packed, packed, packed, rows, rows),
        (q, k, v, g, *(swap_columns(x) for x in (q, k, v, g))),
    )
    sent, inverse, z = call(
        bind(middle),
        (sent_double, rows, rows),
        (got, sums, a, g, norm, norm_in),
    )
    got = exchange(sent)
    before, inner = call(
        bind(before_states), (states, rows), (a, b, v, g, state_in)
    )
    sent, product, c, m = call(
        bind(outputs_grad),
        (sent_single, products, rows, rows),
        (got, before, a, g, inverse, inner),
    )
    got = exchange(sent)
    query, query_send, mixed = call(
        bind(query_grads), (tokens, tokens, square), (a, b, v, g, inverse, c, z, product)
    )
    query_got = pair_swap(query_send)
    finals = call(
        bind(after_states), (after, part, part) * 2, (a, b, g, inverse, mixed, grad_state)
    )
    whole = shape((heads * width, length), BF16)
    (query_grad,) = call(bind(assemble), (whole,), (query, query_got))
    got, query_grad = lax.optimization_barrier((got, query_grad))
    key_send, value_send = call(
        functools.partial(key_value_grads, plan, 1),
        (tokens, tokens),
        (got, *finals[3:], grad_norm, m, b, v),
    )
    key_got, value_got = pair_swap(key_send), pair_swap(value_send)
    half_tokens = shape((plan.rows, length), BF16)
    key, value = call(
        functools.partial(key_value_grads, plan, 0),
        (half_tokens, half_tokens),
        (got, *finals[:3], grad_norm, m, b, v),
    )
    key_grad, value_grad = call(
        bind(assemble), (whole, whole), (key, value, key_got, value_got)
    )
    return query_grad.T, key_grad.T, value_grad.T


def solution(mesh):
    rows = P(("grp", "seq"), None)
    return jax.shard_map(
        per_device,
        mesh=mesh,
        in_specs=(rows, rows, rows, rows, P(), P(), P(), P()),
        out_specs=(rows, rows, rows),
        check_vma=False,
    )
```

```python
import functools

import jax
import jax.numpy as jnp
from jax import lax
from jax.experimental import pallas as pl
from jax.experimental.pallas import tpu as pltpu
from jax.sharding import PartitionSpec as P

F32 = jnp.float32
BF16 = jnp.bfloat16
LANES = 128
SUB = 8
VMEM_BYTES = 67_043_328
FREE = 48 * 2**20


def dot(x, y, dims):
    return lax.dot_general(x, y, (dims, ((), ())), preferred_element_type=F32)


def nn(x, y):
    return dot(x, y, ((1,), (0,)))


def nt(x, y):
    return dot(x, y, ((1,), (1,)))


def tn(x, y):
    return dot(x, y, ((0,), (0,)))


def parts(x):
    high = x.astype(BF16)
    return high, (x - high.astype(F32)).astype(BF16)


def stacked_parts(row):
    high = row.astype(BF16)
    rest = row - high.astype(F32)
    middle = rest.astype(BF16)
    low = rest - middle.astype(F32)
    zeros = jnp.zeros((SUB - 3, row.shape[1]), F32)
    return jnp.concatenate([high.astype(F32), middle.astype(F32), low, zeros], axis=0).astype(BF16)


def added(rows):
    return rows[0:1] + rows[1:2] + rows[2:3]


class Plan:
    def __init__(self, devices, length, heads, width):
        self.devices, self.length, self.heads, self.width = devices, length, heads, width
        self.half = -(-heads // 2)
        self.shift = heads - self.half
        self.rows = self.half * width
        self.extra = SUB * -(-self.half // SUB)
        self.per_slot = devices // SUB
        self.head_tiles = width // SUB
        self.tiles = self.half * self.head_tiles
        self.spare = LANES - width
        self.pieces = width // self.spare if self.spare and width % self.spare == 0 else 0
        self.donors = self.tiles // (self.pieces + 1) if self.pieces else 0
        self.stored = self.tiles - self.donors
        self.whole = self.stored // devices
        self.slots = self.whole * SUB + -(-(self.stored - self.whole * devices) // self.per_slot)
        self.span = self.slots * LANES

    def put(self, ref, base, tile, value):
        if tile < self.whole * self.devices:
            slot, piece = divmod(tile, self.devices)
            columns = pl.ds((base + slot * SUB) * LANES, SUB * LANES)
            ref[piece, :, columns] = value.reshape(1, SUB * LANES)
        else:
            ref[self.place(base, tile)] = value

    def get(self, ref, base, tile):
        if tile < self.whole * self.devices:
            slot, piece = divmod(tile, self.devices)
            columns = pl.ds((base + slot * SUB) * LANES, SUB * LANES)
            return ref[piece, :, columns].reshape(SUB, LANES)
        return ref[self.place(base, tile)]

    def place(self, base, tile):
        slot, part = divmod(tile - self.whole * self.devices, self.per_slot)
        slot += self.whole * SUB
        return pl.ds(part * SUB, SUB), 0, pl.ds((base + slot) * LANES, LANES)

    def own(self, ref, core, head):
        start = pl.multiple_of(core * (self.shift * self.width) + head * self.width, 16)
        return ref[pl.ds(start, self.width), :]

    def other(self, ref, head):
        return ref[head * self.width : (head + 1) * self.width, :]


def my_core():
    return lax.axis_index("seq") & 1


def my_device():
    return lax.axis_index("grp") * lax.axis_size("seq") + lax.axis_index("seq")


def pair_swap(x):
    size = lax.axis_size("seq")
    return lax.ppermute(x, "seq", [(i, i ^ 1) for i in range(size)])


def wide(tile):
    rows, columns = tile.shape
    if columns == LANES:
        return tile
    return jnp.concatenate([tile, jnp.zeros((rows, LANES - columns), tile.dtype)], axis=1)


def store_rows(plan, ref, base, head, block, held):
    block = wide(block)
    lane = lax.broadcasted_iota(jnp.int32, (SUB, LANES), 1)
    for j in range(plan.head_tiles):
        at = head * plan.head_tiles + j
        tile = block[j * SUB : (j + 1) * SUB, :]
        if at >= plan.stored:
            held[at - plan.stored] = tile
            continue
        if at < plan.donors * plan.pieces:
            donor, piece = divmod(at, plan.pieces)
            moved = pltpu.roll(held[donor], plan.width - piece * plan.spare, 1)
            tile = jnp.where(lane >= plan.width, moved, tile)
        plan.put(ref, base, at, tile)


def store_padding(plan, ref, base):
    rest = (plan.slots - plan.whole * SUB) * plan.per_slot + plan.whole * plan.devices
    for tile in range(plan.stored, rest):
        ref[plan.place(base, tile)] = jnp.zeros((SUB, LANES), F32)


def store_norms(plan, ref, rows):
    rows = rows.reshape(1, plan.extra * LANES)[:, : plan.half * LANES]
    for piece in range(plan.devices):
        ref[piece, :, pl.ds(plan.span, plan.half * LANES)] = rows


def load_rows(plan, ref, base, head):
    lane = lax.broadcasted_iota(jnp.int32, (SUB, LANES), 1)
    tiles = []
    for j in range(plan.head_tiles):
        at = head * plan.head_tiles + j
        if at < plan.stored:
            tiles.append(plan.get(ref, base, at))
            continue
        tile = None
        for piece in range(plan.pieces):
            part = plan.get(ref, base, (at - plan.stored) * plan.pieces + piece)
            part = pltpu.roll(part, (LANES - plan.width + piece * plan.spare) % LANES, 1)
            tile = part if tile is None else jnp.where(lane >= piece * plan.spare, part, tile)
        tiles.append(tile)
    return jnp.concatenate(tiles, axis=0)[:, : plan.width]


def each(count, step, carry):
    if count > 16:
        return lax.fori_loop(0, count, step, carry)
    for i in range(count):
        carry = step(i, carry)
    return carry


def scan_rows(plan, in_ref, start, out_ref, later):
    chips = plan.devices // 2
    columns = pl.ds(start, plan.span)

    def step(i, sums):
        chip = chips - 1 - i if later else i
        grown = []
        for core in range(2):
            row = 2 * chip + core
            out_ref[row, :, : plan.span] = sums[core]
            grown.append(sums[core] + in_ref[row, :, columns])
        return tuple(grown)

    zero = jnp.zeros((1, plan.span), F32)
    each(chips, step, (zero, zero))


def scan_norms(plan, in_ref, core, chip, later):
    columns = pl.ds(plan.span, plan.half * LANES)

    def step(i, total):
        take = (i > chip) if later else (i < chip)
        return total + jnp.where(take, in_ref[2 * i + core, :, columns], 0.0)

    return each(plan.devices // 2, step, jnp.zeros((1, plan.half * LANES), F32))


def causal_mask(length):
    row = lax.broadcasted_iota(jnp.int32, (length, length), 0)
    column = lax.broadcasted_iota(jnp.int32, (length, length), 1)
    return row <= column


def scores_of(a, b, causal):
    return jnp.where(causal, tn(b, a), 0.0)


def relu(x):
    return jnp.maximum(x, 0)


def block_states(plan, k_ref, v_ref, send_ref, own_ref):
    core = my_core()
    ones = jnp.ones((SUB, plan.length), BF16)
    for side, out_ref in ((1 - core, send_ref), (core, own_ref)):
        out_ref[plan.rows :, :] = jnp.zeros((plan.extra, LANES), F32)
        for h in range(plan.half):
            b, v = relu(plan.own(k_ref, side, h)), plan.own(v_ref, side, h)
            out_ref[h * plan.width : (h + 1) * plan.width, :] = wide(nt(b, v))
            out_ref[plan.rows + h : plan.rows + h + 1, :] = wide(nt(ones, b))[0:1]


def chip_state(plan, own_ref, got_ref, out_ref):
    held = {}
    for h in reversed(range(plan.half)):
        rows = slice(h * plan.width, (h + 1) * plan.width)
        store_rows(plan, out_ref, 0, h, own_ref[rows, :] + got_ref[rows, :], held)
    store_padding(plan, out_ref, 0)
    store_norms(plan, out_ref, own_ref[plan.rows :, :] + got_ref[plan.rows :, :])


def pack_tokens(
    plan, q_ref, k_ref, v_ref, g_ref, q_got_ref, k_got_ref, v_got_ref, g_got_ref,
    a_ref, b_ref, vb_ref, gb_ref, sum_ref, norm_ref,
):
    core = my_core()
    causal = causal_mask(plan.length)
    ones = jnp.ones((SUB, plan.length), BF16)
    sources = ((q_ref, q_got_ref), (k_ref, k_got_ref), (v_ref, v_got_ref), (g_ref, g_got_ref))
    for h in range(plan.half):
        for i in range(2):
            for n, (pair, ref) in enumerate(zip(sources, (a_ref, b_ref, vb_ref, gb_ref))):
                x = plan.other(pair[1], h).astype(BF16) if i else plan.own(pair[0], core, h)
                ref[i, h] = relu(x) if n < 2 else x
            a, b = a_ref[i, h], b_ref[i, h]
            scores = scores_of(a, b, causal)
            sum_ref[i, h : h + 1, :] = 1.0 + jnp.sum(scores, axis=0, keepdims=True)
            norm_ref[i, h : h + 1, :] = wide(nt(ones, b))[0:1]


def middle(
    plan, in_ref, sum_ref, a_ref, g_ref, norm_ref, norm_in_ref,
    out_ref, inverse_ref, z_ref,
):
    core, chip = my_core(), my_device() >> 1
    flags = (core.astype(F32), (1 - core).astype(F32))
    width = plan.width
    norms = scan_norms(plan, in_ref, core, chip, False)
    scan_rows(plan, in_ref, 0, out_ref, False)
    held = {}
    for h in reversed(range(plan.half)):
        base = norm_in_ref[pl.ds(core * plan.shift + h, 1), :]
        base = base + norms[0:1, h * LANES : h * LANES + width]
        features, grads = [], []
        for i in range(2):
            z = base + flags[i] * norm_ref[1 - i, h : h + 1, :width]
            z_ref[i, h : h + 1, :] = wide(z)
            a = a_ref[i, h]
            den = sum_ref[i, h : h + 1, :] + added(nn(stacked_parts(z), a))
            inverse = 1.0 / den
            inverse_ref[i, h : h + 1, :] = inverse
            features.append(a)
            grads.append((g_ref[i, h].astype(F32) * inverse).astype(BF16))
        state = nt(jnp.concatenate(features, axis=1), jnp.concatenate(grads, axis=1))
        store_rows(plan, out_ref, plan.slots, h, state, held)
    store_padding(plan, out_ref, plan.slots)


def before_states(
    plan, a_ref, b_ref, v_ref, g_ref, state_in_ref, before_ref, inner_ref
):
    core = my_core()
    causal = causal_mask(plan.length)
    own_first = core == 0
    late = (core.astype(F32), (1 - core).astype(F32))
    for h in range(plan.half):
        for i in range(2):
            low = scores_of(a_ref[i, h], b_ref[i, h], causal).astype(BF16)
            inner = nn(v_ref[i, h], low)
            inner_ref[i, h : h + 1, :] = jnp.sum(
                g_ref[i, h].astype(F32) * inner, axis=0, keepdims=True
            )
        b = jnp.where(own_first, b_ref[0, h].astype(F32), b_ref[1, h].astype(F32)).astype(BF16)
        v = jnp.where(own_first, v_ref[0, h].astype(F32), v_ref[1, h].astype(F32)).astype(BF16)
        first = nt(b, v)
        for i in range(2):
            before_ref[i, h] = state_in_ref[core * plan.shift + h] + late[i] * first


def outputs_grad(
    plan, in_ref, before_ref, a_ref, g_ref, inverse_ref, inner_ref,
    out_ref, product_ref, c_ref, m_ref,
):
    scan_rows(plan, in_ref, plan.span, out_ref, True)
    totals = []
    for h in range(plan.half):
        base = load_rows(plan, in_ref, 0, h)
        total = None
        for i in range(2):
            high, low = parts(base + before_ref[i, h])
            g, a = g_ref[i, h], a_ref[i, h]
            product = nn(jnp.concatenate([high, low], axis=0), g)
            product = product[: plan.width] + product[plan.width :]
            product_ref[i, h] = product
            inverse = inverse_ref[i, h : h + 1, :]
            along = jnp.sum(a.astype(F32) * product, axis=0, keepdims=True)
            c = -((along + inner_ref[i, h : h + 1, :]) * inverse) * inverse
            c_ref[i, h : h + 1, :] = c
            m = wide(added(nt(stacked_parts(c), a)))
            m_ref[i, h : h + 1, :] = m
            total = m if total is None else total + m
        totals.append(total)
    totals += [jnp.zeros((1, LANES), F32)] * (plan.extra - plan.half)
    store_norms(plan, out_ref, jnp.concatenate(totals, axis=0))


def query_grads(
    plan, a_ref, b_ref, v_ref, g_ref, inverse_ref, c_ref, z_ref, product_ref,
    own_ref, send_ref, mixed_ref, a_out_ref, u_out_ref,
):
    causal = causal_mask(plan.length)
    width = plan.width
    for i in (1, 0):
        columns = z_ref[i].T
        for h in range(plan.half):
            rows = slice(h * width, (h + 1) * width)
            inverse, c = inverse_ref[i, h : h + 1, :], c_ref[i, h : h + 1, :]
            u = (g_ref[i, h].astype(F32) * inverse).astype(BF16)
            mixed = jnp.where(causal, tn(v_ref[i, h], u) + c, 0.0).astype(BF16)
            mixed_ref[i, h] = mixed
            a_out_ref[i, h] = a_ref[i, h]
            u_out_ref[i, h] = u
            grad = product_ref[i, h] * inverse + columns[:width, h : h + 1] * c
            grad = jnp.where(a_ref[i, h].astype(F32) > 0, grad + nn(b_ref[i, h], mixed), 0.0)
            target = send_ref if i else own_ref
            target[rows, :] = grad


def after_states(plan, a_ref, b_ref, u_ref, mixed_ref, grad_state_ref, *refs):
    core = my_core()
    causal = causal_mask(plan.length)
    own_first = core == 0
    early = ((1 - core).astype(F32), core.astype(F32))
    for h in range(plan.half):
        for i in range(2):
            low = scores_of(a_ref[i, h], b_ref[i, h], causal).astype(BF16)
            key, value = nt(a_ref[i, h], mixed_ref[i, h]), nt(u_ref[i, h], low)
            key = jnp.where(b_ref[i, h].astype(F32) > 0, key, 0.0)
            rows = slice(h * plan.width, (h + 1) * plan.width)
            refs[3 * i + 1][rows, :] = key
            refs[3 * i + 2][rows, :] = value
        a = jnp.where(own_first, a_ref[1, h].astype(F32), a_ref[0, h].astype(F32)).astype(BF16)
        u = jnp.where(own_first, u_ref[1, h].astype(F32), u_ref[0, h].astype(F32)).astype(BF16)
        second = nt(a, u)
        for i in range(2):
            refs[3 * i][h] = grad_state_ref[core * plan.shift + h] + early[i] * second


def suffix_norms(plan, in_ref, grad_norm_ref, m_ref, i):
    core, chip = my_core(), my_device() >> 1
    flag = (core if i else 1 - core).astype(F32)
    norms = scan_norms(plan, in_ref, core, chip, True)
    zeros = plan.extra - plan.half
    norms = jnp.concatenate(
        [norms[:, h * LANES : (h + 1) * LANES] for h in range(plan.half)]
        + [jnp.zeros((zeros, LANES), F32)] * (zeros > 0), axis=0,
    )
    own_rows = [
        grad_norm_ref[pl.ds(core * plan.shift + h, 1), :] for h in range(plan.half)
    ] + [jnp.zeros((zeros, plan.width), F32)] * (zeros > 0)
    return norms + wide(jnp.concatenate(own_rows, axis=0)) + flag * m_ref[1 - i]


def key_value(state, column, b, v):
    width = state.shape[0]
    high, low = parts(state)
    both = nn(jnp.concatenate([high, low], axis=0), v)
    key = both[:width] + both[width:] + column
    return jnp.where(b.astype(F32) > 0, key, 0.0), tn(high, b) + tn(low, b)


def other_suffix(plan, in_ref, after_ref, grad_norm_ref, m_ref, out_ref):
    out_ref[plan.rows :, :] = suffix_norms(plan, in_ref, grad_norm_ref, m_ref, 1)
    for h in range(plan.half):
        rows = slice(h * plan.width, (h + 1) * plan.width)
        out_ref[rows, :] = wide(load_rows(plan, in_ref, 0, h) + after_ref[h])


def own_grads(
    plan, in_ref, after_ref, grad_norm_ref, m_ref, b_ref, v_ref, key_in_ref, value_in_ref,
    key_ref, value_ref,
):
    columns = suffix_norms(plan, in_ref, grad_norm_ref, m_ref, 0).T
    for h in range(plan.half):
        rows = slice(h * plan.width, (h + 1) * plan.width)
        state = load_rows(plan, in_ref, 0, h) + after_ref[h]
        key, value = key_value(state, columns[: plan.width, h : h + 1], b_ref[0, h], v_ref[0, h])
        key_ref[rows, :] = (key + key_in_ref[rows, :]).astype(BF16)
        value_ref[rows, :] = (value + value_in_ref[rows, :]).astype(BF16)


def rest_grads(
    plan, got_ref, k_ref, v_ref, key_in_ref, value_in_ref, own_key_ref, own_value_ref,
    key_ref, value_ref,
):
    core = my_core()
    width, count = plan.width, plan.shift
    own = pl.multiple_of(core * (count * width), 16)
    key_ref[pl.ds(own, plan.rows), :] = own_key_ref[...]
    value_ref[pl.ds(own, plan.rows), :] = own_value_ref[...]
    skip = (1 - core) * (plan.half - count)
    norms = got_ref[pl.ds(plan.rows + skip, count), :]
    columns = jnp.concatenate([norms, jnp.zeros((plan.extra - count, LANES), F32)], axis=0).T
    for t in range(count):
        source = pl.ds(pl.multiple_of((skip + t) * width, 16), width)
        rows = pl.ds(pl.multiple_of((1 - core) * plan.rows + t * width, 16), width)
        b, v = relu(k_ref[rows, :]), v_ref[rows, :]
        key, value = key_value(got_ref[source, :][:, :width], columns[:width, t : t + 1], b, v)
        key_ref[rows, :] = (key + key_in_ref[source, :]).astype(BF16)
        value_ref[rows, :] = (value + value_in_ref[source, :]).astype(BF16)


def assemble(plan, count, *refs):
    core = my_core()
    start = pl.multiple_of(core * (plan.shift * plan.width), 16)
    rest = plan.shift * plan.width
    skip = plan.rows - rest
    other = pl.multiple_of((1 - core) * plan.rows, 16)
    source = pl.multiple_of((1 - core) * skip, 16)
    for n in range(count):
        own_ref, out_ref = refs[n], refs[len(refs) - count + n]
        out_ref[pl.ds(start, plan.rows), :] = own_ref[...].astype(BF16)
        got = refs[count + n][pl.ds(source, rest), :]
        for ref in refs[2 * count + n : len(refs) - count : count]:
            got = got + ref[pl.ds(source, rest), :]
        out_ref[pl.ds(other, rest), :] = got.astype(BF16)


def call(body, outs, args, room=FREE, flops=10_000_000, scratch=()):
    smem = pl.BlockSpec(memory_space=pltpu.SMEM)
    vmem = pl.BlockSpec(memory_space=pltpu.VMEM)
    in_specs = [smem if x.ndim == 1 else vmem for x in args]
    moved = sum(x.size * x.dtype.itemsize for x in (*args, *outs))
    return pl.pallas_call(
        body,
        out_shape=outs,
        in_specs=in_specs,
        out_specs=[vmem] * len(outs),
        scratch_shapes=list(scratch),
        compiler_params=pltpu.CompilerParams(vmem_limit_bytes=VMEM_BYTES - room),
        cost_estimate=pl.CostEstimate(flops=flops, bytes_accessed=moved, transcendentals=0),
    )(*args)


def shape(dims, dtype=F32):
    return jax.ShapeDtypeStruct(dims, dtype)


def per_device(
    queries, key_vectors, value_vectors, output_grad, state_in, norm_in, grad_state, grad_norm
):
    both = ("grp", "seq")
    length = queries.shape[0]
    heads, width = norm_in.shape
    devices = lax.axis_size("grp") * lax.axis_size("seq")
    plan = Plan(devices, length, heads, width)
    half = plan.half
    core = my_core()
    key_rows, value_rows = key_vectors.T, value_vectors.T
    q, k, v, g = queries.T, key_vectors.T, value_vectors.T, output_grad.T

    def bind(body):
        return functools.partial(body, plan)

    def exchange(x):
        return lax.all_to_all(x, both, 0, 0, tiled=True)

    def swap_columns(x):
        start = (1 - core) * (plan.shift * width)
        return pair_swap(lax.dynamic_slice_in_dim(x, start, plan.rows, 0).astype(F32))

    tokens = shape((plan.rows, length))
    packed = shape((2, half, width, length), BF16)
    products = shape((2, half, width, length))
    square = shape((2, half, length, length), BF16)
    states = shape((2, half, width, width))
    rows = shape((2, plan.extra, LANES))
    after = shape((half, width, width))
    block = shape((plan.rows + plan.extra, LANES))
    sent_single = shape((devices, 1, plan.span + half * LANES))
    sent_double = shape((devices, 1, 2 * plan.span))

    send, block_own = call(bind(block_states), (block, block), (k, v))
    block_got = pair_swap(send)
    (sent,) = call(bind(chip_state), (sent_single,), (block_own, block_got))
    sent, k, v, q, g = lax.optimization_barrier((sent, k, v, q, g))
    got = exchange(sent)
    a, b, v, g, sums, norm = call(
        bind(pack_tokens),
        (packed, packed, packed, packed, rows, rows),
        (q, k, v, g, *(swap_columns(x) for x in (q, k, v, g))),
    )
    before, inner = call(bind(before_states), (states, rows), (a, b, v, g, state_in))
    got, before, inner = lax.optimization_barrier((got, before, inner))
    sent, inverse, z = call(
        bind(middle),
        (sent_double, rows, rows),
        (got, sums, a, g, norm, norm_in),
    )
    got = exchange(sent)
    sent, product, c, m = call(
        bind(outputs_grad),
        (sent_single, products, rows, rows),
        (got, before, a, g, inverse, inner),
    )
    got = exchange(sent)
    query, query_send, mixed, a, u = call(
        bind(query_grads),
        (tokens, tokens, square, packed, packed),
        (a, b, v, g, inverse, c, z, product),
    )
    query_got = pair_swap(query_send)
    finals = call(
        bind(after_states), (after, tokens, tokens) * 2, (a, b, u, mixed, grad_state)
    )
    inner_got = [pair_swap(x) for x in finals[4:]]
    whole = shape((heads * width, length), BF16)
    (query_grad,) = call(functools.partial(assemble, plan, 1), (whole,), (query, query_got))
    got, query_grad, inner_got = lax.optimization_barrier((got, query_grad, inner_got))
    (send,) = call(bind(other_suffix), (block,), (got, finals[3], grad_norm, m))
    rest_got = pair_swap(send)
    own_tokens = shape((plan.rows, length), BF16)
    key, value = call(
        bind(own_grads), (own_tokens, own_tokens), (got, finals[0], grad_norm, m, b, v, *finals[1:3])
    )
    key_grad, value_grad = call(
        bind(rest_grads), (whole, whole), (rest_got, key_rows, value_rows, *inner_got, key, value)
    )
    return query_grad.T, key_grad.T, value_grad.T


def solution(mesh):
    rows = P(("grp", "seq"), None)
    return jax.shard_map(
        per_device,
        mesh=mesh,
        in_specs=(rows, rows, rows, rows, P(), P(), P(), P()),
        out_specs=(rows, rows, rows),
        check_vma=False,
    )
```

```python
import functools
from typing import NamedTuple

import jax
import jax.numpy as jnp
from jax import lax
from jax.experimental import pallas as pl
from jax.experimental.pallas import tpu as pltpu
from jax.sharding import PartitionSpec as P

F32 = jnp.float32
BF16 = jnp.bfloat16
LANES = 128
HALF = LANES // 2
SUB = 8
VMEM_BYTES = 67_043_328
FREE = 48 * 2**20


def dot(x, y, dims):
    return lax.dot_general(x, y, (dims, ((), ())), preferred_element_type=F32)


def nn(x, y):
    return dot(x, y, ((1,), (0,)))


def nt(x, y):
    return dot(x, y, ((1,), (1,)))


def tn(x, y):
    return dot(x, y, ((0,), (0,)))


def parts(x):
    high = x.astype(BF16)
    return high, (x - high.astype(F32)).astype(BF16)


def stacked_parts(row):
    high = row.astype(BF16)
    rest = row - high.astype(F32)
    middle = rest.astype(BF16)
    low = rest - middle.astype(F32)
    zeros = jnp.zeros((SUB - 3, row.shape[1]), F32)
    return jnp.concatenate([high.astype(F32), middle.astype(F32), low, zeros], axis=0).astype(BF16)


def added(rows):
    return rows[0:1] + rows[1:2] + rows[2:3]


class Area(NamedTuple):
    start: int
    half_slot: int
    half_lane: int


class Plan:
    def __init__(self, devices, length, heads, width):
        self.devices, self.length, self.heads, self.width = devices, length, heads, width
        self.half = -(-heads // 2)
        self.shift = heads - self.half
        self.rows = self.half * width
        self.extra = SUB * -(-self.half // SUB)
        self.per_slot = devices // SUB
        self.head_tiles = width // SUB
        self.tiles = self.half * self.head_tiles
        self.spare = LANES - width
        self.pieces = width // self.spare if self.spare and width % self.spare == 0 else 0
        self.donors = self.tiles // (self.pieces + 1) if self.pieces else 0
        self.stored = self.tiles - self.donors
        self.whole = self.stored // devices
        single, self.left = divmod(self.stored - self.whole * devices, self.per_slot)
        self.single_end = self.whole * devices + single * self.per_slot
        self.full = self.whole * SUB + single
        self.span = (self.full + 1) * LANES
        self.norm_slots = self.half - 1
        fits = self.norm_slots < self.pieces <= self.norm_slots + HALF // self.spare
        if not fits or 2 * self.left > self.per_slot:
            raise ValueError("unsupported sizes")
        self.single = self.span + self.norm_slots * LANES
        self.double = (2 * self.full + 1) * LANES

    def put(self, ref, area, tile, value):
        if tile < self.single_end:
            index, shape = self.place(area, tile)
            ref[index] = value.reshape(shape)
        else:
            for side, index in enumerate(self.halves(area, tile - self.single_end)):
                ref[index] = value[:, side * HALF : (side + 1) * HALF]

    def get(self, ref, area, tile):
        if tile < self.single_end:
            return ref[self.place(area, tile)[0]].reshape(SUB, LANES)
        return jnp.concatenate(
            [ref[index] for index in self.halves(area, tile - self.single_end)], axis=1
        )

    def place(self, area, tile):
        if tile < self.whole * self.devices:
            slot, piece = divmod(tile, self.devices)
            columns = pl.ds((area.start + slot * SUB) * LANES, SUB * LANES)
            return (piece, slice(None), columns), (1, SUB * LANES)
        slot, part = divmod(tile - self.whole * self.devices, self.per_slot)
        slot += area.start + self.whole * SUB
        return (pl.ds(part * SUB, SUB), 0, pl.ds(slot * LANES, LANES)), (SUB, LANES)

    def halves(self, area, part):
        columns = pl.ds(area.half_slot * LANES + area.half_lane, HALF)
        for side in range(2):
            yield pl.ds((part + side * (self.per_slot // 2)) * SUB, SUB), 0, columns

    def areas(self):
        full = self.full
        return Area(0, full, 0), Area(full + 1, full, HALF), Area(1, 0, HALF)

    def own(self, ref, core, head):
        start = pl.multiple_of(core * (self.shift * self.width) + head * self.width, 16)
        return ref[pl.ds(start, self.width), :]

    def other(self, ref, head):
        return ref[head * self.width : (head + 1) * self.width, :]


def my_core():
    return lax.axis_index("seq") & 1


def my_device():
    return lax.axis_index("grp") * lax.axis_size("seq") + lax.axis_index("seq")


def pair_swap(x):
    size = lax.axis_size("seq")
    return lax.ppermute(x, "seq", [(i, i ^ 1) for i in range(size)])


def wide(tile):
    rows, columns = tile.shape
    if columns == LANES:
        return tile
    return jnp.concatenate([tile, jnp.zeros((rows, LANES - columns), tile.dtype)], axis=1)


def store_rows(plan, ref, area, head, block, held):
    block = wide(block)
    lane = lax.broadcasted_iota(jnp.int32, (SUB, LANES), 1)
    for j in range(plan.head_tiles):
        at = head * plan.head_tiles + j
        tile = block[j * SUB : (j + 1) * SUB, :]
        if at >= plan.stored:
            held[at - plan.stored] = tile
            continue
        if at < plan.donors * plan.pieces:
            donor, piece = divmod(at, plan.pieces)
            moved = pltpu.roll(held[donor], plan.width - piece * plan.spare, 1)
            tile = jnp.where(lane >= plan.width, moved, tile)
        plan.put(ref, area, at, tile)


def store_padding(plan, ref, area):
    for part in range(plan.left, plan.per_slot // 2):
        for index in plan.halves(area, part):
            ref[index] = jnp.zeros((SUB, HALF), F32)


def store_norms(plan, ref, rows, area):
    spare, width, last = plan.spare, plan.width, plan.half - 1
    free = HALF - area.half_lane
    shape = (SUB, LANES)
    lane = lax.broadcasted_iota(jnp.int32, shape, 1)
    row = lax.broadcasted_iota(jnp.int32, shape, 0)
    carried = jnp.broadcast_to(rows[last : last + 1], shape)
    packed = rows[:SUB]
    for j in range(plan.norm_slots):
        moved = pltpu.roll(carried, width - j * spare, 1)
        packed = jnp.where((row == j) & (lane >= width), moved, packed)
    packed = packed.reshape(1, SUB * LANES)[:, : plan.norm_slots * LANES]
    extra = pltpu.roll(carried, (free - plan.norm_slots * spare) % LANES, 1)
    extra = extra[0:1, free : free + HALF]
    for piece in range(plan.devices):
        ref[piece, :, pl.ds(plan.span, plan.norm_slots * LANES)] = packed
        ref[piece, :, pl.ds(area.half_slot * LANES + free, HALF)] = extra


def load_rows(plan, ref, area, head):
    lane = lax.broadcasted_iota(jnp.int32, (SUB, LANES), 1)
    tiles = []
    for j in range(plan.head_tiles):
        at = head * plan.head_tiles + j
        if at < plan.stored:
            tiles.append(plan.get(ref, area, at))
            continue
        tile = None
        for piece in range(plan.pieces):
            part = plan.get(ref, area, (at - plan.stored) * plan.pieces + piece)
            part = pltpu.roll(part, (LANES - plan.width + piece * plan.spare) % LANES, 1)
            tile = part if tile is None else jnp.where(lane >= piece * plan.spare, part, tile)
        tiles.append(tile)
    return jnp.concatenate(tiles, axis=0)[:, : plan.width]


def each(count, step, carry):
    if count > 16:
        return lax.fori_loop(0, count, step, carry)
    for i in range(count):
        carry = step(i, carry)
    return carry


def scan_rows(plan, in_ref, start, out_ref, later):
    chips = plan.devices // 2
    columns = pl.ds(start, plan.span)

    def step(i, sums):
        chip = chips - 1 - i if later else i
        grown = []
        for core in range(2):
            row = 2 * chip + core
            out_ref[row, :, : plan.span] = sums[core]
            grown.append(sums[core] + in_ref[row, :, columns])
        return tuple(grown)

    zero = jnp.zeros((1, plan.span), F32)
    each(chips, step, (zero, zero))


def scan_norms(plan, in_ref, core, chip, later, area):
    spare, width = plan.spare, plan.width
    free = HALF - area.half_lane
    columns = pl.ds(plan.span, plan.norm_slots * LANES)
    extras = pl.ds(area.half_slot * LANES, LANES)

    def step(i, totals):
        take = (i > chip) if later else (i < chip)
        row = 2 * i + core
        return (
            totals[0] + jnp.where(take, in_ref[row, :, columns], 0.0),
            totals[1] + jnp.where(take, in_ref[row, :, extras], 0.0),
        )

    zeros = (jnp.zeros((1, plan.norm_slots * LANES), F32), jnp.zeros((1, LANES), F32))
    packed, extra = each(plan.devices // 2, step, zeros)
    shape = (SUB, LANES)
    lane = lax.broadcasted_iota(jnp.int32, shape, 1)
    rows = [packed[:, j * LANES : (j + 1) * LANES] for j in range(plan.norm_slots)]
    last = None
    for j, row in enumerate(rows):
        moved = jnp.broadcast_to(row, shape)
        moved = pltpu.roll(moved, (LANES - width + j * spare) % LANES, 1)
        last = moved if last is None else jnp.where(lane >= j * spare, moved, last)
    at = plan.norm_slots * spare
    moved = pltpu.roll(jnp.broadcast_to(extra, shape), (at - free) % LANES, 1)
    last = jnp.where(lane >= at, moved, last)
    return [row[:, :width] for row in rows] + [last[0:1, :width]]


def causal_mask(length):
    row = lax.broadcasted_iota(jnp.int32, (length, length), 0)
    column = lax.broadcasted_iota(jnp.int32, (length, length), 1)
    return row <= column


def scores_of(a, b, causal):
    return jnp.where(causal, tn(b, a), 0.0)


def relu(x):
    return jnp.maximum(x, 0)


def block_states(plan, k_ref, v_ref, send_ref, own_ref):
    core = my_core()
    ones = jnp.ones((SUB, plan.length), BF16)
    for side, out_ref in ((1 - core, send_ref), (core, own_ref)):
        out_ref[plan.rows :, :] = jnp.zeros((plan.extra, LANES), F32)
        for h in range(plan.half):
            b, v = relu(plan.own(k_ref, side, h)), plan.own(v_ref, side, h)
            out_ref[h * plan.width : (h + 1) * plan.width, :] = wide(nt(b, v))
            out_ref[plan.rows + h : plan.rows + h + 1, :] = wide(nt(ones, b))[0:1]


def chip_state(plan, own_ref, got_ref, out_ref):
    area = plan.areas()[0]
    held = {}
    for h in reversed(range(plan.half)):
        rows = slice(h * plan.width, (h + 1) * plan.width)
        store_rows(plan, out_ref, area, h, own_ref[rows, :] + got_ref[rows, :], held)
    store_padding(plan, out_ref, area)
    store_norms(plan, out_ref, own_ref[plan.rows :, :] + got_ref[plan.rows :, :], area)


def pack_tokens(
    plan, q_ref, k_ref, v_ref, g_ref, q_got_ref, k_got_ref, v_got_ref, g_got_ref,
    a_ref, b_ref, vb_ref, gb_ref, sum_ref, norm_ref,
):
    core = my_core()
    causal = causal_mask(plan.length)
    ones = jnp.ones((SUB, plan.length), BF16)
    sources = ((q_ref, q_got_ref), (k_ref, k_got_ref), (v_ref, v_got_ref), (g_ref, g_got_ref))
    for h in range(plan.half):
        for i in range(2):
            for n, (pair, ref) in enumerate(zip(sources, (a_ref, b_ref, vb_ref, gb_ref))):
                x = plan.other(pair[1], h).astype(BF16) if i else plan.own(pair[0], core, h)
                ref[i, h] = relu(x) if n < 2 else x
            a, b = a_ref[i, h], b_ref[i, h]
            scores = scores_of(a, b, causal)
            sum_ref[i, h : h + 1, :] = 1.0 + jnp.sum(scores, axis=0, keepdims=True)
            norm_ref[i, h : h + 1, :] = wide(nt(ones, b))[0:1]


def middle(
    plan, in_ref, sum_ref, a_ref, g_ref, norm_ref, norm_in_ref,
    out_ref, inverse_ref, z_ref,
):
    core, chip = my_core(), my_device() >> 1
    flags = (core.astype(F32), (1 - core).astype(F32))
    width = plan.width
    first, second, _ = plan.areas()
    norms = scan_norms(plan, in_ref, core, chip, False, first)
    scan_rows(plan, in_ref, 0, out_ref, False)
    held = {}
    for h in reversed(range(plan.half)):
        base = norm_in_ref[pl.ds(core * plan.shift + h, 1), :]
        base = base + norms[h]
        features, grads = [], []
        for i in range(2):
            z = base + flags[i] * norm_ref[1 - i, h : h + 1, :width]
            z_ref[i, h : h + 1, :] = wide(z)
            a = a_ref[i, h]
            den = sum_ref[i, h : h + 1, :] + added(nn(stacked_parts(z), a))
            inverse = 1.0 / den
            inverse_ref[i, h : h + 1, :] = inverse
            features.append(a)
            grads.append((g_ref[i, h].astype(F32) * inverse).astype(BF16))
        state = nt(jnp.concatenate(features, axis=1), jnp.concatenate(grads, axis=1))
        store_rows(plan, out_ref, second, h, state, held)
    store_padding(plan, out_ref, second)


def before_states(
    plan, a_ref, b_ref, v_ref, g_ref, state_in_ref, before_ref, inner_ref
):
    core = my_core()
    causal = causal_mask(plan.length)
    own_first = core == 0
    late = (core.astype(F32), (1 - core).astype(F32))
    for h in range(plan.half):
        for i in range(2):
            low = scores_of(a_ref[i, h], b_ref[i, h], causal).astype(BF16)
            inner = nn(v_ref[i, h], low)
            inner_ref[i, h : h + 1, :] = jnp.sum(
                g_ref[i, h].astype(F32) * inner, axis=0, keepdims=True
            )
        b = jnp.where(own_first, b_ref[0, h].astype(F32), b_ref[1, h].astype(F32)).astype(BF16)
        v = jnp.where(own_first, v_ref[0, h].astype(F32), v_ref[1, h].astype(F32)).astype(BF16)
        first = nt(b, v)
        for i in range(2):
            before_ref[i, h] = state_in_ref[core * plan.shift + h] + late[i] * first


def outputs_grad(
    plan, in_ref, before_ref, a_ref, g_ref, inverse_ref, inner_ref,
    out_ref, product_ref, c_ref, m_ref,
):
    first, _, third = plan.areas()
    scan_rows(plan, in_ref, plan.full * LANES, out_ref, True)
    totals = []
    for h in range(plan.half):
        base = load_rows(plan, in_ref, first, h)
        total = None
        for i in range(2):
            high, low = parts(base + before_ref[i, h])
            g, a = g_ref[i, h], a_ref[i, h]
            product = nn(jnp.concatenate([high, low], axis=0), g)
            product = product[: plan.width] + product[plan.width :]
            product_ref[i, h] = product
            inverse = inverse_ref[i, h : h + 1, :]
            along = jnp.sum(a.astype(F32) * product, axis=0, keepdims=True)
            c = -((along + inner_ref[i, h : h + 1, :]) * inverse) * inverse
            c_ref[i, h : h + 1, :] = c
            m = wide(added(nt(stacked_parts(c), a)))
            m_ref[i, h : h + 1, :] = m
            total = m if total is None else total + m
        totals.append(total)
    totals += [jnp.zeros((1, LANES), F32)] * (plan.extra - plan.half)
    store_norms(plan, out_ref, jnp.concatenate(totals, axis=0), third)


def query_grads(
    plan, a_ref, b_ref, v_ref, g_ref, inverse_ref, c_ref, z_ref, product_ref,
    own_ref, send_ref, mixed_ref, a_out_ref, u_out_ref,
):
    causal = causal_mask(plan.length)
    width = plan.width
    for i in (1, 0):
        columns = z_ref[i].T
        for h in range(plan.half):
            rows = slice(h * width, (h + 1) * width)
            inverse, c = inverse_ref[i, h : h + 1, :], c_ref[i, h : h + 1, :]
            u = (g_ref[i, h].astype(F32) * inverse).astype(BF16)
            mixed = jnp.where(causal, tn(v_ref[i, h], u) + c, 0.0).astype(BF16)
            mixed_ref[i, h] = mixed
            a_out_ref[i, h] = a_ref[i, h]
            u_out_ref[i, h] = u
            grad = product_ref[i, h] * inverse + columns[:width, h : h + 1] * c
            grad = jnp.where(a_ref[i, h].astype(F32) > 0, grad + nn(b_ref[i, h], mixed), 0.0)
            target = send_ref if i else own_ref
            target[rows, :] = grad


def after_states(plan, a_ref, b_ref, u_ref, mixed_ref, grad_state_ref, *refs):
    core = my_core()
    causal = causal_mask(plan.length)
    own_first = core == 0
    early = ((1 - core).astype(F32), core.astype(F32))
    for h in range(plan.half):
        for i in range(2):
            low = scores_of(a_ref[i, h], b_ref[i, h], causal).astype(BF16)
            key, value = nt(a_ref[i, h], mixed_ref[i, h]), nt(u_ref[i, h], low)
            key = jnp.where(b_ref[i, h].astype(F32) > 0, key, 0.0)
            rows = slice(h * plan.width, (h + 1) * plan.width)
            refs[3 * i + 1][rows, :] = key
            refs[3 * i + 2][rows, :] = value
        a = jnp.where(own_first, a_ref[1, h].astype(F32), a_ref[0, h].astype(F32)).astype(BF16)
        u = jnp.where(own_first, u_ref[1, h].astype(F32), u_ref[0, h].astype(F32)).astype(BF16)
        second = nt(a, u)
        for i in range(2):
            refs[3 * i][h] = grad_state_ref[core * plan.shift + h] + early[i] * second


def suffix_norms(plan, in_ref, grad_norm_ref, m_ref, i):
    core, chip = my_core(), my_device() >> 1
    flag = (core if i else 1 - core).astype(F32)
    norms = scan_norms(plan, in_ref, core, chip, True, plan.areas()[2])
    rows = [
        norm + grad_norm_ref[pl.ds(core * plan.shift + h, 1), :] for h, norm in enumerate(norms)
    ]
    zeros = plan.extra - plan.half
    rows += [jnp.zeros((zeros, plan.width), F32)] * (zeros > 0)
    return wide(jnp.concatenate(rows, axis=0)) + flag * m_ref[1 - i]


def key_value(state, column, b, v):
    width = state.shape[0]
    high, low = parts(state)
    both = nn(jnp.concatenate([high, low], axis=0), v)
    key = both[:width] + both[width:] + column
    return jnp.where(b.astype(F32) > 0, key, 0.0), tn(high, b) + tn(low, b)


def other_suffix(plan, in_ref, after_ref, grad_norm_ref, m_ref, out_ref):
    out_ref[plan.rows :, :] = suffix_norms(plan, in_ref, grad_norm_ref, m_ref, 1)
    for h in range(plan.half):
        rows = slice(h * plan.width, (h + 1) * plan.width)
        out_ref[rows, :] = wide(load_rows(plan, in_ref, plan.areas()[2], h) + after_ref[h])


def own_grads(
    plan, in_ref, after_ref, grad_norm_ref, m_ref, b_ref, v_ref, key_in_ref, value_in_ref,
    key_ref, value_ref,
):
    columns = suffix_norms(plan, in_ref, grad_norm_ref, m_ref, 0).T
    for h in range(plan.half):
        rows = slice(h * plan.width, (h + 1) * plan.width)
        state = load_rows(plan, in_ref, plan.areas()[2], h) + after_ref[h]
        key, value = key_value(state, columns[: plan.width, h : h + 1], b_ref[0, h], v_ref[0, h])
        key_ref[rows, :] = (key + key_in_ref[rows, :]).astype(BF16)
        value_ref[rows, :] = (value + value_in_ref[rows, :]).astype(BF16)


def rest_grads(
    plan, got_ref, k_ref, v_ref, key_in_ref, value_in_ref, own_key_ref, own_value_ref,
    key_ref, value_ref,
):
    core = my_core()
    width, count = plan.width, plan.shift
    own = pl.multiple_of(core * (count * width), 16)
    key_ref[pl.ds(own, plan.rows), :] = own_key_ref[...]
    value_ref[pl.ds(own, plan.rows), :] = own_value_ref[...]
    skip = (1 - core) * (plan.half - count)
    norms = got_ref[pl.ds(plan.rows + skip, count), :]
    columns = jnp.concatenate([norms, jnp.zeros((plan.extra - count, LANES), F32)], axis=0).T
    for t in range(count):
        source = pl.ds(pl.multiple_of((skip + t) * width, 16), width)
        rows = pl.ds(pl.multiple_of((1 - core) * plan.rows + t * width, 16), width)
        b, v = relu(k_ref[rows, :]), v_ref[rows, :]
        key, value = key_value(got_ref[source, :][:, :width], columns[:width, t : t + 1], b, v)
        key_ref[rows, :] = (key + key_in_ref[source, :]).astype(BF16)
        value_ref[rows, :] = (value + value_in_ref[source, :]).astype(BF16)


def assemble(plan, count, *refs):
    core = my_core()
    start = pl.multiple_of(core * (plan.shift * plan.width), 16)
    rest = plan.shift * plan.width
    skip = plan.rows - rest
    other = pl.multiple_of((1 - core) * plan.rows, 16)
    source = pl.multiple_of((1 - core) * skip, 16)
    for n in range(count):
        own_ref, out_ref = refs[n], refs[len(refs) - count + n]
        out_ref[pl.ds(start, plan.rows), :] = own_ref[...].astype(BF16)
        got = refs[count + n][pl.ds(source, rest), :]
        for ref in refs[2 * count + n : len(refs) - count : count]:
            got = got + ref[pl.ds(source, rest), :]
        out_ref[pl.ds(other, rest), :] = got.astype(BF16)


def call(body, outs, args, room=FREE, flops=10_000_000, scratch=()):
    smem = pl.BlockSpec(memory_space=pltpu.SMEM)
    vmem = pl.BlockSpec(memory_space=pltpu.VMEM)
    in_specs = [smem if x.ndim == 1 else vmem for x in args]
    moved = sum(x.size * x.dtype.itemsize for x in (*args, *outs))
    return pl.pallas_call(
        body,
        out_shape=outs,
        in_specs=in_specs,
        out_specs=[vmem] * len(outs),
        scratch_shapes=list(scratch),
        compiler_params=pltpu.CompilerParams(vmem_limit_bytes=VMEM_BYTES - room),
        cost_estimate=pl.CostEstimate(flops=flops, bytes_accessed=moved, transcendentals=0),
    )(*args)


def shape(dims, dtype=F32):
    return jax.ShapeDtypeStruct(dims, dtype)


def per_device(
    queries, key_vectors, value_vectors, output_grad, state_in, norm_in, grad_state, grad_norm
):
    both = ("grp", "seq")
    length = queries.shape[0]
    heads, width = norm_in.shape
    devices = lax.axis_size("grp") * lax.axis_size("seq")
    plan = Plan(devices, length, heads, width)
    half = plan.half
    core = my_core()
    key_rows, value_rows = key_vectors.T, value_vectors.T
    q, k, v, g = queries.T, key_vectors.T, value_vectors.T, output_grad.T

    def bind(body):
        return functools.partial(body, plan)

    def exchange(x):
        return lax.all_to_all(x, both, 0, 0, tiled=True)

    def swap_columns(x):
        start = (1 - core) * (plan.shift * width)
        return pair_swap(lax.dynamic_slice_in_dim(x, start, plan.rows, 0).astype(F32))

    tokens = shape((plan.rows, length))
    packed = shape((2, half, width, length), BF16)
    products = shape((2, half, width, length))
    square = shape((2, half, length, length), BF16)
    states = shape((2, half, width, width))
    rows = shape((2, plan.extra, LANES))
    after = shape((half, width, width))
    block = shape((plan.rows + plan.extra, LANES))
    sent_single = shape((devices, 1, plan.single))
    sent_double = shape((devices, 1, plan.double))

    send, block_own = call(bind(block_states), (block, block), (k, v))
    block_got = pair_swap(send)
    (sent,) = call(bind(chip_state), (sent_single,), (block_own, block_got))
    sent, k, v, q, g = lax.optimization_barrier((sent, k, v, q, g))
    got = exchange(sent)
    a, b, v, g, sums, norm = call(
        bind(pack_tokens),
        (packed, packed, packed, packed, rows, rows),
        (q, k, v, g, *(swap_columns(x) for x in (q, k, v, g))),
    )
    before, inner = call(bind(before_states), (states, rows), (a, b, v, g, state_in))
    got, before, inner = lax.optimization_barrier((got, before, inner))
    sent, inverse, z = call(
        bind(middle),
        (sent_double, rows, rows),
        (got, sums, a, g, norm, norm_in),
    )
    got = exchange(sent)
    sent, product, c, m = call(
        bind(outputs_grad),
        (sent_single, products, rows, rows),
        (got, before, a, g, inverse, inner),
    )
    got = exchange(sent)
    query, query_send, mixed, a, u = call(
        bind(query_grads),
        (tokens, tokens, square, packed, packed),
        (a, b, v, g, inverse, c, z, product),
    )
    query_got = pair_swap(query_send)
    finals = call(
        bind(after_states), (after, tokens, tokens) * 2, (a, b, u, mixed, grad_state)
    )
    inner_got = [pair_swap(x) for x in finals[4:]]
    whole = shape((heads * width, length), BF16)
    (query_grad,) = call(functools.partial(assemble, plan, 1), (whole,), (query, query_got))
    got, query_grad, inner_got = lax.optimization_barrier((got, query_grad, inner_got))
    (send,) = call(bind(other_suffix), (block,), (got, finals[3], grad_norm, m))
    rest_got = pair_swap(send)
    own_tokens = shape((plan.rows, length), BF16)
    key, value = call(
        bind(own_grads), (own_tokens, own_tokens), (got, finals[0], grad_norm, m, b, v, *finals[1:3])
    )
    key_grad, value_grad = call(
        bind(rest_grads), (whole, whole), (rest_got, key_rows, value_rows, *inner_got, key, value)
    )
    return query_grad.T, key_grad.T, value_grad.T


def solution(mesh):
    rows = P(("grp", "seq"), None)
    return jax.shard_map(
        per_device,
        mesh=mesh,
        in_specs=(rows, rows, rows, rows, P(), P(), P(), P()),
        out_specs=(rows, rows, rows),
        check_vma=False,
    )
```

```python
import functools
from typing import NamedTuple

import jax
import jax.numpy as jnp
from jax import lax
from jax.experimental import pallas as pl
from jax.experimental.pallas import tpu as pltpu
from jax.sharding import PartitionSpec as P

F32 = jnp.float32
BF16 = jnp.bfloat16
LANES = 128
HALF = LANES // 2
SUB = 8
VMEM_BYTES = 67_043_328
FREE = 48 * 2**20


def dot(x, y, dims):
    return lax.dot_general(x, y, (dims, ((), ())), preferred_element_type=F32)


def nn(x, y):
    return dot(x, y, ((1,), (0,)))


def nt(x, y):
    return dot(x, y, ((1,), (1,)))


def tn(x, y):
    return dot(x, y, ((0,), (0,)))


def parts(x):
    high = x.astype(BF16)
    return high, (x - high.astype(F32)).astype(BF16)


def stacked_parts(row):
    high = row.astype(BF16)
    rest = row - high.astype(F32)
    middle = rest.astype(BF16)
    low = rest - middle.astype(F32)
    zeros = jnp.zeros((SUB - 3, row.shape[1]), F32)
    return jnp.concatenate([high.astype(F32), middle.astype(F32), low, zeros], axis=0).astype(BF16)


def added(rows):
    return rows[0:1] + rows[1:2] + rows[2:3]


class Area(NamedTuple):
    start: int
    half_slot: int
    half_lane: int


class Plan:
    def __init__(self, devices, length, heads, width):
        self.devices, self.length, self.heads, self.width = devices, length, heads, width
        self.half = -(-heads // 2)
        self.shift = heads - self.half
        self.rows = self.half * width
        self.extra = SUB * -(-self.half // SUB)
        self.per_slot = devices // SUB
        self.head_tiles = width // SUB
        self.tiles = self.half * self.head_tiles
        self.spare = LANES - width
        self.pieces = width // self.spare if self.spare and width % self.spare == 0 else 0
        self.donors = self.tiles // (self.pieces + 1) if self.pieces else 0
        self.stored = self.tiles - self.donors
        self.whole = self.stored // devices
        single, self.left = divmod(self.stored - self.whole * devices, self.per_slot)
        self.single_end = self.whole * devices + single * self.per_slot
        self.full = self.whole * SUB + single
        self.span = (self.full + 1) * LANES
        self.norm_slots = self.half - 1
        fits = self.norm_slots < self.pieces <= self.norm_slots + HALF // self.spare
        if not fits or 2 * self.left > self.per_slot:
            raise ValueError("unsupported sizes")
        self.single = self.span + self.norm_slots * LANES
        self.double = (2 * self.full + 1) * LANES

    def put(self, ref, area, tile, value):
        if tile < self.single_end:
            index, shape = self.place(area, tile)
            ref[index] = value.reshape(shape)
        else:
            for side, index in enumerate(self.halves(area, tile - self.single_end)):
                ref[index] = value[:, side * HALF : (side + 1) * HALF]

    def get(self, ref, area, tile):
        if tile < self.single_end:
            return ref[self.place(area, tile)[0]].reshape(SUB, LANES)
        return jnp.concatenate(
            [ref[index] for index in self.halves(area, tile - self.single_end)], axis=1
        )

    def place(self, area, tile):
        if tile < self.whole * self.devices:
            slot, piece = divmod(tile, self.devices)
            columns = pl.ds((area.start + slot * SUB) * LANES, SUB * LANES)
            return (piece, slice(None), columns), (1, SUB * LANES)
        slot, part = divmod(tile - self.whole * self.devices, self.per_slot)
        slot += area.start + self.whole * SUB
        return (pl.ds(part * SUB, SUB), 0, pl.ds(slot * LANES, LANES)), (SUB, LANES)

    def halves(self, area, part):
        columns = pl.ds(area.half_slot * LANES + area.half_lane, HALF)
        for side in range(2):
            yield pl.ds((part + side * (self.per_slot // 2)) * SUB, SUB), 0, columns

    def areas(self):
        full = self.full
        return Area(0, full, 0), Area(full + 1, full, HALF), Area(1, 0, HALF)

    def own(self, ref, core, head):
        start = pl.multiple_of(core * (self.shift * self.width) + head * self.width, 16)
        return ref[pl.ds(start, self.width), :]

    def other(self, ref, head):
        return ref[head * self.width : (head + 1) * self.width, :]


def my_core():
    return lax.axis_index("seq") & 1


def my_device():
    return lax.axis_index("grp") * lax.axis_size("seq") + lax.axis_index("seq")


def pair_swap(x):
    size = lax.axis_size("seq")
    return lax.ppermute(x, "seq", [(i, i ^ 1) for i in range(size)])


def wide(tile):
    rows, columns = tile.shape
    if columns == LANES:
        return tile
    return jnp.concatenate([tile, jnp.zeros((rows, LANES - columns), tile.dtype)], axis=1)


def store_rows(plan, ref, area, head, block, held):
    block = wide(block)
    lane = lax.broadcasted_iota(jnp.int32, (SUB, LANES), 1)
    for j in range(plan.head_tiles):
        at = head * plan.head_tiles + j
        tile = block[j * SUB : (j + 1) * SUB, :]
        if at >= plan.stored:
            held[at - plan.stored] = tile
            continue
        if at < plan.donors * plan.pieces:
            donor, piece = divmod(at, plan.pieces)
            moved = pltpu.roll(held[donor], plan.width - piece * plan.spare, 1)
            tile = jnp.where(lane >= plan.width, moved, tile)
        plan.put(ref, area, at, tile)


def store_padding(plan, ref, area):
    for part in range(plan.left, plan.per_slot // 2):
        for index in plan.halves(area, part):
            ref[index] = jnp.zeros((SUB, HALF), F32)


def store_norms(plan, ref, rows, area):
    spare, width, last = plan.spare, plan.width, plan.half - 1
    free = HALF - area.half_lane
    shape = (SUB, LANES)
    lane = lax.broadcasted_iota(jnp.int32, shape, 1)
    row = lax.broadcasted_iota(jnp.int32, shape, 0)
    carried = jnp.broadcast_to(rows[last : last + 1], shape)
    packed = rows[:SUB]
    for j in range(plan.norm_slots):
        moved = pltpu.roll(carried, width - j * spare, 1)
        packed = jnp.where((row == j) & (lane >= width), moved, packed)
    packed = packed.reshape(1, SUB * LANES)[:, : plan.norm_slots * LANES]
    extra = pltpu.roll(carried, (free - plan.norm_slots * spare) % LANES, 1)
    extra = extra[0:1, free : free + HALF]
    for piece in range(plan.devices):
        ref[piece, :, pl.ds(plan.span, plan.norm_slots * LANES)] = packed
        ref[piece, :, pl.ds(area.half_slot * LANES + free, HALF)] = extra


def load_rows(plan, ref, area, head):
    lane = lax.broadcasted_iota(jnp.int32, (SUB, LANES), 1)
    tiles = []
    for j in range(plan.head_tiles):
        at = head * plan.head_tiles + j
        if at < plan.stored:
            tiles.append(plan.get(ref, area, at))
            continue
        tile = None
        for piece in range(plan.pieces):
            part = plan.get(ref, area, (at - plan.stored) * plan.pieces + piece)
            part = pltpu.roll(part, (LANES - plan.width + piece * plan.spare) % LANES, 1)
            tile = part if tile is None else jnp.where(lane >= piece * plan.spare, part, tile)
        tiles.append(tile)
    return jnp.concatenate(tiles, axis=0)[:, : plan.width]


def each(count, step, carry):
    if count > 16:
        return lax.fori_loop(0, count, step, carry)
    for i in range(count):
        carry = step(i, carry)
    return carry


def scan_rows(plan, in_ref, start, out_ref, later):
    chips = plan.devices // 2
    columns = pl.ds(start, plan.span)

    def step(i, sums):
        chip = chips - 1 - i if later else i
        grown = []
        for core in range(2):
            row = 2 * chip + core
            out_ref[row, :, : plan.span] = sums[core]
            grown.append(sums[core] + in_ref[row, :, columns])
        return tuple(grown)

    zero = jnp.zeros((1, plan.span), F32)
    each(chips, step, (zero, zero))


def scan_norms(plan, in_ref, core, chip, later, area):
    spare, width = plan.spare, plan.width
    free = HALF - area.half_lane
    columns = pl.ds(plan.span, plan.norm_slots * LANES)
    extras = pl.ds(area.half_slot * LANES, LANES)

    def step(i, totals):
        take = (i > chip) if later else (i < chip)
        row = 2 * i + core
        return (
            totals[0] + jnp.where(take, in_ref[row, :, columns], 0.0),
            totals[1] + jnp.where(take, in_ref[row, :, extras], 0.0),
        )

    zeros = (jnp.zeros((1, plan.norm_slots * LANES), F32), jnp.zeros((1, LANES), F32))
    packed, extra = each(plan.devices // 2, step, zeros)
    shape = (SUB, LANES)
    lane = lax.broadcasted_iota(jnp.int32, shape, 1)
    rows = [packed[:, j * LANES : (j + 1) * LANES] for j in range(plan.norm_slots)]
    last = None
    for j, row in enumerate(rows):
        moved = jnp.broadcast_to(row, shape)
        moved = pltpu.roll(moved, (LANES - width + j * spare) % LANES, 1)
        last = moved if last is None else jnp.where(lane >= j * spare, moved, last)
    at = plan.norm_slots * spare
    moved = pltpu.roll(jnp.broadcast_to(extra, shape), (at - free) % LANES, 1)
    last = jnp.where(lane >= at, moved, last)
    return [row[:, :width] for row in rows] + [last[0:1, :width]]


def causal_mask(length):
    row = lax.broadcasted_iota(jnp.int32, (length, length), 0)
    column = lax.broadcasted_iota(jnp.int32, (length, length), 1)
    return row <= column


def scores_of(a, b, causal):
    return jnp.where(causal, tn(b, a), 0.0)


def relu(x):
    return jnp.maximum(x, 0)


def block_state(plan, other, kv_ref, out_ref):
    core = my_core()
    side = 1 - core if other else core
    size = plan.heads * plan.width
    k_ref, v_ref = kv_ref.at[:size, :], kv_ref.at[size:, :]
    ones = jnp.ones((SUB, plan.length), BF16)
    out_ref[plan.rows :, :] = jnp.zeros((plan.extra, LANES), F32)
    for h in range(plan.half):
        b, v = relu(plan.own(k_ref, side, h)), plan.own(v_ref, side, h)
        out_ref[h * plan.width : (h + 1) * plan.width, :] = wide(nt(b, v))
        out_ref[plan.rows + h : plan.rows + h + 1, :] = wide(nt(ones, b))[0:1]


def chip_state(plan, own_ref, got_ref, out_ref):
    area = plan.areas()[0]
    held = {}
    for h in reversed(range(plan.half)):
        rows = slice(h * plan.width, (h + 1) * plan.width)
        store_rows(plan, out_ref, area, h, own_ref[rows, :] + got_ref[rows, :], held)
    store_padding(plan, out_ref, area)
    store_norms(plan, out_ref, own_ref[plan.rows :, :] + got_ref[plan.rows :, :], area)


def pack_tokens(
    plan, q_ref, k_ref, v_ref, g_ref, q_got_ref, k_got_ref, v_got_ref, g_got_ref,
    a_ref, b_ref, vb_ref, gb_ref, sum_ref, norm_ref,
):
    core = my_core()
    causal = causal_mask(plan.length)
    ones = jnp.ones((SUB, plan.length), BF16)
    sources = ((q_ref, q_got_ref), (k_ref, k_got_ref), (v_ref, v_got_ref), (g_ref, g_got_ref))
    for h in range(plan.half):
        for i in range(2):
            for n, (pair, ref) in enumerate(zip(sources, (a_ref, b_ref, vb_ref, gb_ref))):
                x = plan.other(pair[1], h).astype(BF16) if i else plan.own(pair[0], core, h)
                ref[i, h] = relu(x) if n < 2 else x
            a, b = a_ref[i, h], b_ref[i, h]
            scores = scores_of(a, b, causal)
            sum_ref[i, h : h + 1, :] = 1.0 + jnp.sum(scores, axis=0, keepdims=True)
            norm_ref[i, h : h + 1, :] = wide(nt(ones, b))[0:1]


def middle(
    plan, in_ref, sum_ref, a_ref, g_ref, norm_ref, norm_in_ref,
    out_ref, inverse_ref, z_ref,
):
    core, chip = my_core(), my_device() >> 1
    flags = (core.astype(F32), (1 - core).astype(F32))
    width = plan.width
    first, second, _ = plan.areas()
    norms = scan_norms(plan, in_ref, core, chip, False, first)
    scan_rows(plan, in_ref, 0, out_ref, False)
    held = {}
    for h in reversed(range(plan.half)):
        base = norm_in_ref[pl.ds(core * plan.shift + h, 1), :]
        base = base + norms[h]
        features, grads = [], []
        for i in range(2):
            z = base + flags[i] * norm_ref[1 - i, h : h + 1, :width]
            z_ref[i, h : h + 1, :] = wide(z)
            a = a_ref[i, h]
            den = sum_ref[i, h : h + 1, :] + added(nn(stacked_parts(z), a))
            inverse = 1.0 / den
            inverse_ref[i, h : h + 1, :] = inverse
            features.append(a)
            grads.append((g_ref[i, h].astype(F32) * inverse).astype(BF16))
        state = nt(jnp.concatenate(features, axis=1), jnp.concatenate(grads, axis=1))
        store_rows(plan, out_ref, second, h, state, held)
    store_padding(plan, out_ref, second)


def before_states(
    plan, a_ref, b_ref, v_ref, g_ref, state_in_ref, before_ref, inner_ref
):
    core = my_core()
    causal = causal_mask(plan.length)
    own_first = core == 0
    late = (core.astype(F32), (1 - core).astype(F32))
    for h in range(plan.half):
        for i in range(2):
            low = scores_of(a_ref[i, h], b_ref[i, h], causal).astype(BF16)
            inner = nn(v_ref[i, h], low)
            inner_ref[i, h : h + 1, :] = jnp.sum(
                g_ref[i, h].astype(F32) * inner, axis=0, keepdims=True
            )
        b = jnp.where(own_first, b_ref[0, h].astype(F32), b_ref[1, h].astype(F32)).astype(BF16)
        v = jnp.where(own_first, v_ref[0, h].astype(F32), v_ref[1, h].astype(F32)).astype(BF16)
        first = nt(b, v)
        for i in range(2):
            before_ref[i, h] = state_in_ref[core * plan.shift + h] + late[i] * first


def outputs_grad(
    plan, in_ref, before_ref, a_ref, g_ref, inverse_ref, inner_ref,
    out_ref, product_ref, c_ref, m_ref,
):
    first, _, third = plan.areas()
    scan_rows(plan, in_ref, plan.full * LANES, out_ref, True)
    totals = []
    for h in range(plan.half):
        base = load_rows(plan, in_ref, first, h)
        total = None
        for i in range(2):
            high, low = parts(base + before_ref[i, h])
            g, a = g_ref[i, h], a_ref[i, h]
            product = nn(jnp.concatenate([high, low], axis=0), g)
            product = product[: plan.width] + product[plan.width :]
            product_ref[i, h] = product
            inverse = inverse_ref[i, h : h + 1, :]
            along = jnp.sum(a.astype(F32) * product, axis=0, keepdims=True)
            c = -((along + inner_ref[i, h : h + 1, :]) * inverse) * inverse
            c_ref[i, h : h + 1, :] = c
            m = wide(added(nt(stacked_parts(c), a)))
            m_ref[i, h : h + 1, :] = m
            total = m if total is None else total + m
        totals.append(total)
    totals += [jnp.zeros((1, LANES), F32)] * (plan.extra - plan.half)
    store_norms(plan, out_ref, jnp.concatenate(totals, axis=0), third)


def query_grads(
    plan, a_ref, b_ref, v_ref, g_ref, inverse_ref, c_ref, z_ref, product_ref,
    own_ref, send_ref, mixed_ref, a_out_ref, u_out_ref,
):
    causal = causal_mask(plan.length)
    width = plan.width
    for i in (1, 0):
        columns = z_ref[i].T
        for h in range(plan.half):
            rows = slice(h * width, (h + 1) * width)
            inverse, c = inverse_ref[i, h : h + 1, :], c_ref[i, h : h + 1, :]
            u = (g_ref[i, h].astype(F32) * inverse).astype(BF16)
            mixed = jnp.where(causal, tn(v_ref[i, h], u) + c, 0.0).astype(BF16)
            mixed_ref[i, h] = mixed
            a_out_ref[i, h] = a_ref[i, h]
            u_out_ref[i, h] = u
            grad = product_ref[i, h] * inverse + columns[:width, h : h + 1] * c
            grad = jnp.where(a_ref[i, h].astype(F32) > 0, grad + nn(b_ref[i, h], mixed), 0.0)
            target = send_ref if i else own_ref
            target[rows, :] = grad


def after_states(plan, a_ref, b_ref, u_ref, mixed_ref, grad_state_ref, *refs):
    core = my_core()
    causal = causal_mask(plan.length)
    own_first = core == 0
    early = ((1 - core).astype(F32), core.astype(F32))
    for h in range(plan.half):
        for i in range(2):
            low = scores_of(a_ref[i, h], b_ref[i, h], causal).astype(BF16)
            key, value = nt(a_ref[i, h], mixed_ref[i, h]), nt(u_ref[i, h], low)
            key = jnp.where(b_ref[i, h].astype(F32) > 0, key, 0.0)
            rows = slice(h * plan.width, (h + 1) * plan.width)
            refs[3 * i + 1][rows, :] = key
            refs[3 * i + 2][rows, :] = value
        a = jnp.where(own_first, a_ref[1, h].astype(F32), a_ref[0, h].astype(F32)).astype(BF16)
        u = jnp.where(own_first, u_ref[1, h].astype(F32), u_ref[0, h].astype(F32)).astype(BF16)
        second = nt(a, u)
        for i in range(2):
            refs[3 * i][h] = grad_state_ref[core * plan.shift + h] + early[i] * second


def suffix_norms(plan, in_ref, grad_norm_ref, m_ref, i):
    core, chip = my_core(), my_device() >> 1
    flag = (core if i else 1 - core).astype(F32)
    norms = scan_norms(plan, in_ref, core, chip, True, plan.areas()[2])
    rows = [
        norm + grad_norm_ref[pl.ds(core * plan.shift + h, 1), :] for h, norm in enumerate(norms)
    ]
    zeros = plan.extra - plan.half
    rows += [jnp.zeros((zeros, plan.width), F32)] * (zeros > 0)
    return wide(jnp.concatenate(rows, axis=0)) + flag * m_ref[1 - i]


def key_value(state, column, b, v):
    width = state.shape[0]
    high, low = parts(state)
    both = nn(jnp.concatenate([high, low], axis=0), v)
    key = both[:width] + both[width:] + column
    return jnp.where(b.astype(F32) > 0, key, 0.0), tn(high, b) + tn(low, b)


def other_suffix(plan, in_ref, after_ref, grad_norm_ref, m_ref, out_ref):
    out_ref[plan.rows :, :] = suffix_norms(plan, in_ref, grad_norm_ref, m_ref, 1)
    for h in range(plan.half):
        rows = slice(h * plan.width, (h + 1) * plan.width)
        out_ref[rows, :] = wide(load_rows(plan, in_ref, plan.areas()[2], h) + after_ref[h])


def own_grads(
    plan, in_ref, after_ref, grad_norm_ref, m_ref, b_ref, v_ref, key_in_ref, value_in_ref,
    key_ref, value_ref,
):
    columns = suffix_norms(plan, in_ref, grad_norm_ref, m_ref, 0).T
    for h in range(plan.half):
        rows = slice(h * plan.width, (h + 1) * plan.width)
        state = load_rows(plan, in_ref, plan.areas()[2], h) + after_ref[h]
        key, value = key_value(state, columns[: plan.width, h : h + 1], b_ref[0, h], v_ref[0, h])
        key_ref[rows, :] = (key + key_in_ref[rows, :]).astype(BF16)
        value_ref[rows, :] = (value + value_in_ref[rows, :]).astype(BF16)


def rest_grads(
    plan, got_ref, k_ref, v_ref, key_in_ref, value_in_ref, own_key_ref, own_value_ref,
    key_ref, value_ref,
):
    core = my_core()
    width, count = plan.width, plan.shift
    own = pl.multiple_of(core * (count * width), 16)
    key_ref[pl.ds(own, plan.rows), :] = own_key_ref[...]
    value_ref[pl.ds(own, plan.rows), :] = own_value_ref[...]
    skip = (1 - core) * (plan.half - count)
    norms = got_ref[pl.ds(plan.rows + skip, count), :]
    columns = jnp.concatenate([norms, jnp.zeros((plan.extra - count, LANES), F32)], axis=0).T
    for t in range(count):
        source = pl.ds(pl.multiple_of((skip + t) * width, 16), width)
        rows = pl.ds(pl.multiple_of((1 - core) * plan.rows + t * width, 16), width)
        b, v = relu(k_ref[rows, :]), v_ref[rows, :]
        key, value = key_value(got_ref[source, :][:, :width], columns[:width, t : t + 1], b, v)
        key_ref[rows, :] = (key + key_in_ref[source, :]).astype(BF16)
        value_ref[rows, :] = (value + value_in_ref[source, :]).astype(BF16)


def assemble(plan, count, *refs):
    core = my_core()
    start = pl.multiple_of(core * (plan.shift * plan.width), 16)
    rest = plan.shift * plan.width
    skip = plan.rows - rest
    other = pl.multiple_of((1 - core) * plan.rows, 16)
    source = pl.multiple_of((1 - core) * skip, 16)
    for n in range(count):
        own_ref, out_ref = refs[n], refs[len(refs) - count + n]
        out_ref[pl.ds(start, plan.rows), :] = own_ref[...].astype(BF16)
        got = refs[count + n][pl.ds(source, rest), :]
        for ref in refs[2 * count + n : len(refs) - count : count]:
            got = got + ref[pl.ds(source, rest), :]
        out_ref[pl.ds(other, rest), :] = got.astype(BF16)


def call(body, outs, args, room=FREE, flops=10_000_000, scratch=()):
    smem = pl.BlockSpec(memory_space=pltpu.SMEM)
    vmem = pl.BlockSpec(memory_space=pltpu.VMEM)
    in_specs = [smem if x.ndim == 1 else vmem for x in args]
    moved = sum(x.size * x.dtype.itemsize for x in (*args, *outs))
    return pl.pallas_call(
        body,
        out_shape=outs,
        in_specs=in_specs,
        out_specs=[vmem] * len(outs),
        scratch_shapes=list(scratch),
        compiler_params=pltpu.CompilerParams(vmem_limit_bytes=VMEM_BYTES - room),
        cost_estimate=pl.CostEstimate(flops=flops, bytes_accessed=moved, transcendentals=0),
    )(*args)


def shape(dims, dtype=F32):
    return jax.ShapeDtypeStruct(dims, dtype)


def per_device(
    queries, key_vectors, value_vectors, output_grad, state_in, norm_in, grad_state, grad_norm
):
    both = ("grp", "seq")
    length = queries.shape[0]
    heads, width = norm_in.shape
    devices = lax.axis_size("grp") * lax.axis_size("seq")
    plan = Plan(devices, length, heads, width)
    half = plan.half
    core = my_core()
    key_rows, value_rows = key_vectors.T, value_vectors.T
    q, k, v, g = queries.T, key_vectors.T, value_vectors.T, output_grad.T

    def bind(body):
        return functools.partial(body, plan)

    def exchange(x):
        return lax.all_to_all(x, both, 0, 0, tiled=True)

    def swap_columns(x):
        start = (1 - core) * (plan.shift * width)
        return pair_swap(lax.dynamic_slice_in_dim(x, start, plan.rows, 0).astype(F32))

    tokens = shape((plan.rows, length))
    packed = shape((2, half, width, length), BF16)
    products = shape((2, half, width, length))
    square = shape((2, half, length, length), BF16)
    states = shape((2, half, width, width))
    rows = shape((2, plan.extra, LANES))
    after = shape((half, width, width))
    block = shape((plan.rows + plan.extra, LANES))
    sent_single = shape((devices, 1, plan.single))
    sent_double = shape((devices, 1, plan.double))

    keys_values = jnp.concatenate([k, v], axis=0)
    (send,) = call(functools.partial(block_state, plan, True), (block,), (keys_values,))
    block_got = pair_swap(send)
    (block_own,) = call(functools.partial(block_state, plan, False), (block,), (keys_values,))
    (sent,) = call(bind(chip_state), (sent_single,), (block_own, block_got))
    sent, k, v, q, g = lax.optimization_barrier((sent, k, v, q, g))
    got = exchange(sent)
    a, b, v, g, sums, norm = call(
        bind(pack_tokens),
        (packed, packed, packed, packed, rows, rows),
        (q, k, v, g, *(swap_columns(x) for x in (q, k, v, g))),
    )
    before, inner = call(bind(before_states), (states, rows), (a, b, v, g, state_in))
    got, before, inner = lax.optimization_barrier((got, before, inner))
    sent, inverse, z = call(
        bind(middle),
        (sent_double, rows, rows),
        (got, sums, a, g, norm, norm_in),
    )
    got = exchange(sent)
    sent, product, c, m = call(
        bind(outputs_grad),
        (sent_single, products, rows, rows),
        (got, before, a, g, inverse, inner),
    )
    got = exchange(sent)
    query, query_send, mixed, a, u = call(
        bind(query_grads),
        (tokens, tokens, square, packed, packed),
        (a, b, v, g, inverse, c, z, product),
    )
    query_got = pair_swap(query_send)
    finals = call(
        bind(after_states), (after, tokens, tokens) * 2, (a, b, u, mixed, grad_state)
    )
    inner_got = [pair_swap(x) for x in finals[4:]]
    whole = shape((heads * width, length), BF16)
    (query_grad,) = call(functools.partial(assemble, plan, 1), (whole,), (query, query_got))
    got, query_grad, inner_got = lax.optimization_barrier((got, query_grad, inner_got))
    (send,) = call(bind(other_suffix), (block,), (got, finals[3], grad_norm, m))
    rest_got = pair_swap(send)
    own_tokens = shape((plan.rows, length), BF16)
    key, value = call(
        bind(own_grads), (own_tokens, own_tokens), (got, finals[0], grad_norm, m, b, v, *finals[1:3])
    )
    key_grad, value_grad = call(
        bind(rest_grads), (whole, whole), (rest_got, key_rows, value_rows, *inner_got, key, value)
    )
    return query_grad.T, key_grad.T, value_grad.T


def solution(mesh):
    rows = P(("grp", "seq"), None)
    return jax.shard_map(
        per_device,
        mesh=mesh,
        in_specs=(rows, rows, rows, rows, P(), P(), P(), P()),
        out_specs=(rows, rows, rows),
        check_vma=False,
    )
```

```python
import functools
from typing import NamedTuple

import jax
import jax.numpy as jnp
from jax import lax
from jax.experimental import pallas as pl
from jax.experimental.pallas import tpu as pltpu
from jax.sharding import PartitionSpec as P

F32 = jnp.float32
BF16 = jnp.bfloat16
LANES = 128
HALF = LANES // 2
SUB = 8
VMEM_BYTES = 67_043_328
FREE = 48 * 2**20


def dot(x, y, dims):
    return lax.dot_general(x, y, (dims, ((), ())), preferred_element_type=F32)


def nn(x, y):
    return dot(x, y, ((1,), (0,)))


def nt(x, y):
    return dot(x, y, ((1,), (1,)))


def tn(x, y):
    return dot(x, y, ((0,), (0,)))


def parts(x):
    high = x.astype(BF16)
    return high, (x - high.astype(F32)).astype(BF16)


def stacked_parts(row):
    high = row.astype(BF16)
    rest = row - high.astype(F32)
    middle = rest.astype(BF16)
    low = rest - middle.astype(F32)
    zeros = jnp.zeros((SUB - 3, row.shape[1]), F32)
    return jnp.concatenate([high.astype(F32), middle.astype(F32), low, zeros], axis=0).astype(BF16)


def added(rows):
    return rows[0:1] + rows[1:2] + rows[2:3]


class Area(NamedTuple):
    start: int
    half_slot: int
    half_lane: int


class Plan:
    def __init__(self, groups, members, length, heads, width):
        self.groups, self.members, devices = groups, members, groups * members
        self.devices, self.length, self.heads, self.width = devices, length, heads, width
        self.half = -(-heads // 2)
        self.shift = heads - self.half
        self.rows = self.half * width
        self.extra = SUB * -(-self.half // SUB)
        self.per_slot = devices // SUB
        self.head_tiles = width // SUB
        self.tiles = self.half * self.head_tiles
        self.spare = LANES - width
        self.pieces = width // self.spare if self.spare and width % self.spare == 0 else 0
        self.donors = self.tiles // (self.pieces + 1) if self.pieces else 0
        self.stored = self.tiles - self.donors
        self.whole = self.stored // devices
        single, self.left = divmod(self.stored - self.whole * devices, self.per_slot)
        self.single_end = self.whole * devices + single * self.per_slot
        self.full = self.whole * SUB + single
        self.span = (self.full + 1) * LANES
        self.norm_slots = self.half - 1
        fits = self.norm_slots < self.pieces <= self.norm_slots + HALF // self.spare
        if not fits or 2 * self.left > self.per_slot:
            raise ValueError("unsupported sizes")
        self.single = self.span + self.norm_slots * LANES
        self.double = (2 * self.full + 1) * LANES

    def put(self, ref, area, tile, value):
        if tile < self.single_end:
            index, shape = self.place(area, tile)
            ref[index] = value.reshape(shape)
        else:
            for side, index in enumerate(self.halves(area, tile - self.single_end)):
                ref[index] = value[:, side * HALF : (side + 1) * HALF]

    def get(self, ref, area, tile):
        if tile < self.single_end:
            return ref[self.place(area, tile)[0]].reshape(SUB, LANES)
        return jnp.concatenate(
            [ref[index] for index in self.halves(area, tile - self.single_end)], axis=1
        )

    def place(self, area, tile):
        if tile < self.whole * self.devices:
            slot, piece = divmod(tile, self.devices)
            columns = pl.ds((area.start + slot * SUB) * LANES, SUB * LANES)
            return (piece, slice(None), columns), (1, SUB * LANES)
        slot, part = divmod(tile - self.whole * self.devices, self.per_slot)
        slot += area.start + self.whole * SUB
        return (pl.ds(part * SUB, SUB), 0, pl.ds(slot * LANES, LANES)), (SUB, LANES)

    def halves(self, area, part):
        columns = pl.ds(area.half_slot * LANES + area.half_lane, HALF)
        for side in range(2):
            yield pl.ds((part + side * (self.per_slot // 2)) * SUB, SUB), 0, columns

    def areas(self):
        full = self.full
        return Area(0, full, 0), Area(full + 1, full, HALF), Area(1, 0, HALF)

    def row(self, chip, core):
        first, members = 2 * chip, self.members
        if isinstance(chip, int):
            group, member = divmod(first, members)
        else:
            group, member = lax.div(first, members), lax.rem(first, members)
        return (member + core) * self.groups + group

    def own(self, ref, core, head):
        start = pl.multiple_of(core * (self.shift * self.width) + head * self.width, 16)
        return ref[pl.ds(start, self.width), :]

    def other(self, ref, head):
        return ref[head * self.width : (head + 1) * self.width, :]


def my_core():
    return lax.axis_index("seq") & 1


def my_device():
    return lax.axis_index("grp") * lax.axis_size("seq") + lax.axis_index("seq")


def pair_swap(x):
    size = lax.axis_size("seq")
    return lax.ppermute(x, "seq", [(i, i ^ 1) for i in range(size)])


def wide(tile):
    rows, columns = tile.shape
    if columns == LANES:
        return tile
    return jnp.concatenate([tile, jnp.zeros((rows, LANES - columns), tile.dtype)], axis=1)


def store_rows(plan, ref, area, head, block, held):
    block = wide(block)
    lane = lax.broadcasted_iota(jnp.int32, (SUB, LANES), 1)
    for j in range(plan.head_tiles):
        at = head * plan.head_tiles + j
        tile = block[j * SUB : (j + 1) * SUB, :]
        if at >= plan.stored:
            held[at - plan.stored] = tile
            continue
        if at < plan.donors * plan.pieces:
            donor, piece = divmod(at, plan.pieces)
            moved = pltpu.roll(held[donor], plan.width - piece * plan.spare, 1)
            tile = jnp.where(lane >= plan.width, moved, tile)
        plan.put(ref, area, at, tile)


def store_padding(plan, ref, area):
    for part in range(plan.left, plan.per_slot // 2):
        for index in plan.halves(area, part):
            ref[index] = jnp.zeros((SUB, HALF), F32)


def store_norms(plan, ref, rows, area):
    spare, width, last = plan.spare, plan.width, plan.half - 1
    free = HALF - area.half_lane
    shape = (SUB, LANES)
    lane = lax.broadcasted_iota(jnp.int32, shape, 1)
    row = lax.broadcasted_iota(jnp.int32, shape, 0)
    carried = jnp.broadcast_to(rows[last : last + 1], shape)
    packed = rows[:SUB]
    for j in range(plan.norm_slots):
        moved = pltpu.roll(carried, width - j * spare, 1)
        packed = jnp.where((row == j) & (lane >= width), moved, packed)
    packed = packed.reshape(1, SUB * LANES)[:, : plan.norm_slots * LANES]
    extra = pltpu.roll(carried, (free - plan.norm_slots * spare) % LANES, 1)
    extra = extra[0:1, free : free + HALF]
    for piece in range(plan.devices):
        ref[piece, :, pl.ds(plan.span, plan.norm_slots * LANES)] = packed
        ref[piece, :, pl.ds(area.half_slot * LANES + free, HALF)] = extra


def load_rows(plan, ref, area, head):
    lane = lax.broadcasted_iota(jnp.int32, (SUB, LANES), 1)
    tiles = []
    for j in range(plan.head_tiles):
        at = head * plan.head_tiles + j
        if at < plan.stored:
            tiles.append(plan.get(ref, area, at))
            continue
        tile = None
        for piece in range(plan.pieces):
            part = plan.get(ref, area, (at - plan.stored) * plan.pieces + piece)
            part = pltpu.roll(part, (LANES - plan.width + piece * plan.spare) % LANES, 1)
            tile = part if tile is None else jnp.where(lane >= piece * plan.spare, part, tile)
        tiles.append(tile)
    return jnp.concatenate(tiles, axis=0)[:, : plan.width]


def each(count, step, carry):
    if count > 16:
        return lax.fori_loop(0, count, step, carry)
    for i in range(count):
        carry = step(i, carry)
    return carry


def scan_rows(plan, in_ref, start, out_ref, later):
    chips = plan.devices // 2
    columns = pl.ds(start, plan.span)

    def step(i, sums):
        chip = chips - 1 - i if later else i
        grown = []
        for core in range(2):
            row = plan.row(chip, core)
            out_ref[row, :, : plan.span] = sums[core]
            grown.append(sums[core] + in_ref[row, :, columns])
        return tuple(grown)

    zero = jnp.zeros((1, plan.span), F32)
    each(chips, step, (zero, zero))


def scan_norms(plan, in_ref, core, chip, later, area):
    spare, width = plan.spare, plan.width
    free = HALF - area.half_lane
    columns = pl.ds(plan.span, plan.norm_slots * LANES)
    extras = pl.ds(area.half_slot * LANES, LANES)

    def step(i, totals):
        take = (i > chip) if later else (i < chip)
        row = plan.row(i, core)
        return (
            totals[0] + jnp.where(take, in_ref[row, :, columns], 0.0),
            totals[1] + jnp.where(take, in_ref[row, :, extras], 0.0),
        )

    zeros = (jnp.zeros((1, plan.norm_slots * LANES), F32), jnp.zeros((1, LANES), F32))
    packed, extra = each(plan.devices // 2, step, zeros)
    shape = (SUB, LANES)
    lane = lax.broadcasted_iota(jnp.int32, shape, 1)
    rows = [packed[:, j * LANES : (j + 1) * LANES] for j in range(plan.norm_slots)]
    last = None
    for j, row in enumerate(rows):
        moved = jnp.broadcast_to(row, shape)
        moved = pltpu.roll(moved, (LANES - width + j * spare) % LANES, 1)
        last = moved if last is None else jnp.where(lane >= j * spare, moved, last)
    at = plan.norm_slots * spare
    moved = pltpu.roll(jnp.broadcast_to(extra, shape), (at - free) % LANES, 1)
    last = jnp.where(lane >= at, moved, last)
    return [row[:, :width] for row in rows] + [last[0:1, :width]]


def causal_mask(length):
    row = lax.broadcasted_iota(jnp.int32, (length, length), 0)
    column = lax.broadcasted_iota(jnp.int32, (length, length), 1)
    return row <= column


def scores_of(a, b, causal):
    return jnp.where(causal, tn(b, a), 0.0)


def relu(x):
    return jnp.maximum(x, 0)


def block_state(plan, other, kv_ref, out_ref):
    core = my_core()
    side = 1 - core if other else core
    size = plan.heads * plan.width
    k_ref, v_ref = kv_ref.at[:size, :], kv_ref.at[size:, :]
    ones = jnp.ones((SUB, plan.length), BF16)
    out_ref[plan.rows :, :] = jnp.zeros((plan.extra, LANES), F32)
    for h in range(plan.half):
        b, v = relu(plan.own(k_ref, side, h)), plan.own(v_ref, side, h)
        out_ref[h * plan.width : (h + 1) * plan.width, :] = wide(nt(b, v))
        out_ref[plan.rows + h : plan.rows + h + 1, :] = wide(nt(ones, b))[0:1]


def chip_state(plan, own_ref, got_ref, out_ref):
    area = plan.areas()[0]
    held = {}
    for h in reversed(range(plan.half)):
        rows = slice(h * plan.width, (h + 1) * plan.width)
        store_rows(plan, out_ref, area, h, own_ref[rows, :] + got_ref[rows, :], held)
    store_padding(plan, out_ref, area)
    store_norms(plan, out_ref, own_ref[plan.rows :, :] + got_ref[plan.rows :, :], area)


def pack_tokens(
    plan, q_ref, k_ref, v_ref, g_ref, q_got_ref, k_got_ref, v_got_ref, g_got_ref,
    a_ref, b_ref, vb_ref, gb_ref, sum_ref, norm_ref,
):
    core = my_core()
    causal = causal_mask(plan.length)
    ones = jnp.ones((SUB, plan.length), BF16)
    sources = ((q_ref, q_got_ref), (k_ref, k_got_ref), (v_ref, v_got_ref), (g_ref, g_got_ref))
    for h in range(plan.half):
        for i in range(2):
            for n, (pair, ref) in enumerate(zip(sources, (a_ref, b_ref, vb_ref, gb_ref))):
                x = plan.other(pair[1], h).astype(BF16) if i else plan.own(pair[0], core, h)
                ref[i, h] = relu(x) if n < 2 else x
            a, b = a_ref[i, h], b_ref[i, h]
            scores = scores_of(a, b, causal)
            sum_ref[i, h : h + 1, :] = 1.0 + jnp.sum(scores, axis=0, keepdims=True)
            norm_ref[i, h : h + 1, :] = wide(nt(ones, b))[0:1]


def middle(
    plan, in_ref, sum_ref, a_ref, g_ref, norm_ref, norm_in_ref,
    out_ref, inverse_ref, z_ref,
):
    core, chip = my_core(), my_device() >> 1
    flags = (core.astype(F32), (1 - core).astype(F32))
    width = plan.width
    first, second, _ = plan.areas()
    norms = scan_norms(plan, in_ref, core, chip, False, first)
    scan_rows(plan, in_ref, 0, out_ref, False)
    held = {}
    for h in reversed(range(plan.half)):
        base = norm_in_ref[pl.ds(core * plan.shift + h, 1), :]
        base = base + norms[h]
        features, grads = [], []
        for i in range(2):
            z = base + flags[i] * norm_ref[1 - i, h : h + 1, :width]
            z_ref[i, h : h + 1, :] = wide(z)
            a = a_ref[i, h]
            den = sum_ref[i, h : h + 1, :] + added(nn(stacked_parts(z), a))
            inverse = 1.0 / den
            inverse_ref[i, h : h + 1, :] = inverse
            features.append(a)
            grads.append((g_ref[i, h].astype(F32) * inverse).astype(BF16))
        state = nt(jnp.concatenate(features, axis=1), jnp.concatenate(grads, axis=1))
        store_rows(plan, out_ref, second, h, state, held)
    store_padding(plan, out_ref, second)


def before_states(
    plan, a_ref, b_ref, v_ref, g_ref, state_in_ref, before_ref, inner_ref
):
    core = my_core()
    causal = causal_mask(plan.length)
    own_first = core == 0
    late = (core.astype(F32), (1 - core).astype(F32))
    for h in range(plan.half):
        for i in range(2):
            low = scores_of(a_ref[i, h], b_ref[i, h], causal).astype(BF16)
            inner = nn(v_ref[i, h], low)
            inner_ref[i, h : h + 1, :] = jnp.sum(
                g_ref[i, h].astype(F32) * inner, axis=0, keepdims=True
            )
        b = jnp.where(own_first, b_ref[0, h].astype(F32), b_ref[1, h].astype(F32)).astype(BF16)
        v = jnp.where(own_first, v_ref[0, h].astype(F32), v_ref[1, h].astype(F32)).astype(BF16)
        first = nt(b, v)
        for i in range(2):
            before_ref[i, h] = state_in_ref[core * plan.shift + h] + late[i] * first


def outputs_grad(
    plan, in_ref, before_ref, a_ref, g_ref, inverse_ref, inner_ref,
    out_ref, product_ref, c_ref, m_ref,
):
    first, _, third = plan.areas()
    scan_rows(plan, in_ref, plan.full * LANES, out_ref, True)
    totals = []
    for h in range(plan.half):
        base = load_rows(plan, in_ref, first, h)
        total = None
        for i in range(2):
            high, low = parts(base + before_ref[i, h])
            g, a = g_ref[i, h], a_ref[i, h]
            product = nn(jnp.concatenate([high, low], axis=0), g)
            product = product[: plan.width] + product[plan.width :]
            product_ref[i, h] = product
            inverse = inverse_ref[i, h : h + 1, :]
            along = jnp.sum(a.astype(F32) * product, axis=0, keepdims=True)
            c = -((along + inner_ref[i, h : h + 1, :]) * inverse) * inverse
            c_ref[i, h : h + 1, :] = c
            m = wide(added(nt(stacked_parts(c), a)))
            m_ref[i, h : h + 1, :] = m
            total = m if total is None else total + m
        totals.append(total)
    totals += [jnp.zeros((1, LANES), F32)] * (plan.extra - plan.half)
    store_norms(plan, out_ref, jnp.concatenate(totals, axis=0), third)


def query_grads(
    plan, a_ref, b_ref, v_ref, g_ref, inverse_ref, c_ref, z_ref, product_ref,
    own_ref, send_ref, mixed_ref, a_out_ref, u_out_ref,
):
    causal = causal_mask(plan.length)
    width = plan.width
    for i in (1, 0):
        columns = z_ref[i].T
        for h in range(plan.half):
            rows = slice(h * width, (h + 1) * width)
            inverse, c = inverse_ref[i, h : h + 1, :], c_ref[i, h : h + 1, :]
            u = (g_ref[i, h].astype(F32) * inverse).astype(BF16)
            mixed = jnp.where(causal, tn(v_ref[i, h], u) + c, 0.0).astype(BF16)
            mixed_ref[i, h] = mixed
            a_out_ref[i, h] = a_ref[i, h]
            u_out_ref[i, h] = u
            grad = product_ref[i, h] * inverse + columns[:width, h : h + 1] * c
            grad = jnp.where(a_ref[i, h].astype(F32) > 0, grad + nn(b_ref[i, h], mixed), 0.0)
            target = send_ref if i else own_ref
            target[rows, :] = grad


def after_states(plan, a_ref, b_ref, u_ref, mixed_ref, grad_state_ref, *refs):
    core = my_core()
    causal = causal_mask(plan.length)
    own_first = core == 0
    early = ((1 - core).astype(F32), core.astype(F32))
    for h in range(plan.half):
        for i in range(2):
            low = scores_of(a_ref[i, h], b_ref[i, h], causal).astype(BF16)
            key, value = nt(a_ref[i, h], mixed_ref[i, h]), nt(u_ref[i, h], low)
            key = jnp.where(b_ref[i, h].astype(F32) > 0, key, 0.0)
            rows = slice(h * plan.width, (h + 1) * plan.width)
            refs[3 * i + 1][rows, :] = key
            refs[3 * i + 2][rows, :] = value
        a = jnp.where(own_first, a_ref[1, h].astype(F32), a_ref[0, h].astype(F32)).astype(BF16)
        u = jnp.where(own_first, u_ref[1, h].astype(F32), u_ref[0, h].astype(F32)).astype(BF16)
        second = nt(a, u)
        for i in range(2):
            refs[3 * i][h] = grad_state_ref[core * plan.shift + h] + early[i] * second


def suffix_norms(plan, in_ref, grad_norm_ref, m_ref, i):
    core, chip = my_core(), my_device() >> 1
    flag = (core if i else 1 - core).astype(F32)
    norms = scan_norms(plan, in_ref, core, chip, True, plan.areas()[2])
    rows = [
        norm + grad_norm_ref[pl.ds(core * plan.shift + h, 1), :] for h, norm in enumerate(norms)
    ]
    zeros = plan.extra - plan.half
    rows += [jnp.zeros((zeros, plan.width), F32)] * (zeros > 0)
    return wide(jnp.concatenate(rows, axis=0)) + flag * m_ref[1 - i]


def key_value(state, column, b, v):
    width = state.shape[0]
    high, low = parts(state)
    both = nn(jnp.concatenate([high, low], axis=0), v)
    key = both[:width] + both[width:] + column
    return jnp.where(b.astype(F32) > 0, key, 0.0), tn(high, b) + tn(low, b)


def other_suffix(plan, in_ref, after_ref, grad_norm_ref, m_ref, out_ref):
    out_ref[plan.rows :, :] = suffix_norms(plan, in_ref, grad_norm_ref, m_ref, 1)
    for h in range(plan.half):
        rows = slice(h * plan.width, (h + 1) * plan.width)
        out_ref[rows, :] = wide(load_rows(plan, in_ref, plan.areas()[2], h) + after_ref[h])


def own_grads(
    plan, in_ref, after_ref, grad_norm_ref, m_ref, b_ref, v_ref, key_in_ref, value_in_ref,
    key_ref, value_ref,
):
    columns = suffix_norms(plan, in_ref, grad_norm_ref, m_ref, 0).T
    for h in range(plan.half):
        rows = slice(h * plan.width, (h + 1) * plan.width)
        state = load_rows(plan, in_ref, plan.areas()[2], h) + after_ref[h]
        key, value = key_value(state, columns[: plan.width, h : h + 1], b_ref[0, h], v_ref[0, h])
        key_ref[rows, :] = (key + key_in_ref[rows, :]).astype(BF16)
        value_ref[rows, :] = (value + value_in_ref[rows, :]).astype(BF16)


def rest_grads(
    plan, got_ref, k_ref, v_ref, key_in_ref, value_in_ref, own_key_ref, own_value_ref,
    key_ref, value_ref,
):
    core = my_core()
    width, count = plan.width, plan.shift
    own = pl.multiple_of(core * (count * width), 16)
    key_ref[pl.ds(own, plan.rows), :] = own_key_ref[...]
    value_ref[pl.ds(own, plan.rows), :] = own_value_ref[...]
    skip = (1 - core) * (plan.half - count)
    norms = got_ref[pl.ds(plan.rows + skip, count), :]
    columns = jnp.concatenate([norms, jnp.zeros((plan.extra - count, LANES), F32)], axis=0).T
    for t in range(count):
        source = pl.ds(pl.multiple_of((skip + t) * width, 16), width)
        rows = pl.ds(pl.multiple_of((1 - core) * plan.rows + t * width, 16), width)
        b, v = relu(k_ref[rows, :]), v_ref[rows, :]
        key, value = key_value(got_ref[source, :][:, :width], columns[:width, t : t + 1], b, v)
        key_ref[rows, :] = (key + key_in_ref[source, :]).astype(BF16)
        value_ref[rows, :] = (value + value_in_ref[source, :]).astype(BF16)


def assemble(plan, count, *refs):
    core = my_core()
    start = pl.multiple_of(core * (plan.shift * plan.width), 16)
    rest = plan.shift * plan.width
    skip = plan.rows - rest
    other = pl.multiple_of((1 - core) * plan.rows, 16)
    source = pl.multiple_of((1 - core) * skip, 16)
    for n in range(count):
        own_ref, out_ref = refs[n], refs[len(refs) - count + n]
        out_ref[pl.ds(start, plan.rows), :] = own_ref[...].astype(BF16)
        got = refs[count + n][pl.ds(source, rest), :]
        for ref in refs[2 * count + n : len(refs) - count : count]:
            got = got + ref[pl.ds(source, rest), :]
        out_ref[pl.ds(other, rest), :] = got.astype(BF16)


def call(body, outs, args, room=FREE, flops=10_000_000, scratch=()):
    smem = pl.BlockSpec(memory_space=pltpu.SMEM)
    vmem = pl.BlockSpec(memory_space=pltpu.VMEM)
    in_specs = [smem if x.ndim == 1 else vmem for x in args]
    moved = sum(x.size * x.dtype.itemsize for x in (*args, *outs))
    return pl.pallas_call(
        body,
        out_shape=outs,
        in_specs=in_specs,
        out_specs=[vmem] * len(outs),
        scratch_shapes=list(scratch),
        compiler_params=pltpu.CompilerParams(vmem_limit_bytes=VMEM_BYTES - room),
        cost_estimate=pl.CostEstimate(flops=flops, bytes_accessed=moved, transcendentals=0),
    )(*args)


def shape(dims, dtype=F32):
    return jax.ShapeDtypeStruct(dims, dtype)


def per_device(
    queries, key_vectors, value_vectors, output_grad, state_in, norm_in, grad_state, grad_norm
):
    both = ("seq", "grp")
    length = queries.shape[0]
    heads, width = norm_in.shape
    plan = Plan(lax.axis_size("grp"), lax.axis_size("seq"), length, heads, width)
    devices = plan.devices
    half = plan.half
    core = my_core()
    key_rows, value_rows = key_vectors.T, value_vectors.T
    q, k, v, g = queries.T, key_vectors.T, value_vectors.T, output_grad.T

    def bind(body):
        return functools.partial(body, plan)

    def exchange(x):
        return lax.all_to_all(x, both, 0, 0, tiled=True)

    def swap_columns(x):
        start = (1 - core) * (plan.shift * width)
        return pair_swap(lax.dynamic_slice_in_dim(x, start, plan.rows, 0).astype(F32))

    tokens = shape((plan.rows, length))
    packed = shape((2, half, width, length), BF16)
    products = shape((2, half, width, length))
    square = shape((2, half, length, length), BF16)
    states = shape((2, half, width, width))
    rows = shape((2, plan.extra, LANES))
    after = shape((half, width, width))
    block = shape((plan.rows + plan.extra, LANES))
    sent_single = shape((devices, 1, plan.single))
    sent_double = shape((devices, 1, plan.double))

    keys_values = jnp.concatenate([k, v], axis=0)
    (send,) = call(functools.partial(block_state, plan, True), (block,), (keys_values,))
    block_got = pair_swap(send)
    (block_own,) = call(functools.partial(block_state, plan, False), (block,), (keys_values,))
    (sent,) = call(bind(chip_state), (sent_single,), (block_own, block_got))
    sent, k, v, q, g = lax.optimization_barrier((sent, k, v, q, g))
    got = exchange(sent)
    a, b, v, g, sums, norm = call(
        bind(pack_tokens),
        (packed, packed, packed, packed, rows, rows),
        (q, k, v, g, *(swap_columns(x) for x in (q, k, v, g))),
    )
    before, inner = call(bind(before_states), (states, rows), (a, b, v, g, state_in))
    got, before, inner = lax.optimization_barrier((got, before, inner))
    sent, inverse, z = call(
        bind(middle),
        (sent_double, rows, rows),
        (got, sums, a, g, norm, norm_in),
    )
    got = exchange(sent)
    sent, product, c, m = call(
        bind(outputs_grad),
        (sent_single, products, rows, rows),
        (got, before, a, g, inverse, inner),
    )
    got = exchange(sent)
    query, query_send, mixed, a, u = call(
        bind(query_grads),
        (tokens, tokens, square, packed, packed),
        (a, b, v, g, inverse, c, z, product),
    )
    query_got = pair_swap(query_send)
    finals = call(
        bind(after_states), (after, tokens, tokens) * 2, (a, b, u, mixed, grad_state)
    )
    inner_got = [pair_swap(x) for x in finals[4:]]
    whole = shape((heads * width, length), BF16)
    (query_grad,) = call(functools.partial(assemble, plan, 1), (whole,), (query, query_got))
    got, query_grad, inner_got = lax.optimization_barrier((got, query_grad, inner_got))
    (send,) = call(bind(other_suffix), (block,), (got, finals[3], grad_norm, m))
    rest_got = pair_swap(send)
    own_tokens = shape((plan.rows, length), BF16)
    key, value = call(
        bind(own_grads), (own_tokens, own_tokens), (got, finals[0], grad_norm, m, b, v, *finals[1:3])
    )
    key_grad, value_grad = call(
        bind(rest_grads), (whole, whole), (rest_got, key_rows, value_rows, *inner_got, key, value)
    )
    return query_grad.T, key_grad.T, value_grad.T


def solution(mesh):
    rows = P(("grp", "seq"), None)
    return jax.shard_map(
        per_device,
        mesh=mesh,
        in_specs=(rows, rows, rows, rows, P(), P(), P(), P()),
        out_specs=(rows, rows, rows),
        check_vma=False,
    )
```

```python
import functools
from typing import NamedTuple

import jax
import jax.numpy as jnp
from jax import lax
from jax.experimental import pallas as pl
from jax.experimental.pallas import tpu as pltpu
from jax.sharding import PartitionSpec as P

F32 = jnp.float32
BF16 = jnp.bfloat16
LANES = 128
HALF = LANES // 2
SUB = 8
VMEM_BYTES = 67_043_328
FREE = 48 * 2**20


def dot(x, y, dims):
    return lax.dot_general(x, y, (dims, ((), ())), preferred_element_type=F32)


def nn(x, y):
    return dot(x, y, ((1,), (0,)))


def nt(x, y):
    return dot(x, y, ((1,), (1,)))


def tn(x, y):
    return dot(x, y, ((0,), (0,)))


def parts(x):
    high = x.astype(BF16)
    return high, (x - high.astype(F32)).astype(BF16)


def stacked_parts(row):
    high = row.astype(BF16)
    rest = row - high.astype(F32)
    middle = rest.astype(BF16)
    low = rest - middle.astype(F32)
    zeros = jnp.zeros((SUB - 3, row.shape[1]), F32)
    return jnp.concatenate([high.astype(F32), middle.astype(F32), low, zeros], axis=0).astype(BF16)


def added(rows):
    return rows[0:1] + rows[1:2] + rows[2:3]


class Area(NamedTuple):
    start: int
    half_slot: int
    half_lane: int


class Plan:
    def __init__(self, groups, members, length, heads, width):
        self.groups, self.members, devices = groups, members, groups * members
        self.devices, self.length, self.heads, self.width = devices, length, heads, width
        self.half = -(-heads // 2)
        self.shift = heads - self.half
        self.rows = self.half * width
        self.extra = SUB * -(-self.half // SUB)
        self.per_slot = devices // SUB
        self.head_tiles = width // SUB
        self.tiles = self.half * self.head_tiles
        self.spare = LANES - width
        self.pieces = width // self.spare if self.spare and width % self.spare == 0 else 0
        self.donors = self.tiles // (self.pieces + 1) if self.pieces else 0
        self.stored = self.tiles - self.donors
        self.whole = self.stored // devices
        single, self.left = divmod(self.stored - self.whole * devices, self.per_slot)
        self.single_end = self.whole * devices + single * self.per_slot
        self.full = self.whole * SUB + single
        self.span = (self.full + 1) * LANES
        self.norm_slots = self.half - 1
        fits = self.norm_slots < self.pieces <= self.norm_slots + HALF // self.spare
        if not fits or 2 * self.left > self.per_slot:
            raise ValueError("unsupported sizes")
        self.single = self.span + self.norm_slots * LANES
        self.double = (2 * self.full + 1) * LANES

    def put(self, ref, area, tile, value):
        if tile < self.single_end:
            index, shape = self.place(area, tile)
            ref[index] = value.reshape(shape)
        else:
            for side, index in enumerate(self.halves(area, tile - self.single_end)):
                ref[index] = value[:, side * HALF : (side + 1) * HALF]

    def get(self, ref, area, tile):
        if tile < self.single_end:
            return ref[self.place(area, tile)[0]].reshape(SUB, LANES)
        return jnp.concatenate(
            [ref[index] for index in self.halves(area, tile - self.single_end)], axis=1
        )

    def place(self, area, tile):
        if tile < self.whole * self.devices:
            slot, piece = divmod(tile, self.devices)
            columns = pl.ds((area.start + slot * SUB) * LANES, SUB * LANES)
            return (piece, slice(None), columns), (1, SUB * LANES)
        slot, part = divmod(tile - self.whole * self.devices, self.per_slot)
        slot += area.start + self.whole * SUB
        return (pl.ds(part * SUB, SUB), 0, pl.ds(slot * LANES, LANES)), (SUB, LANES)

    def halves(self, area, part):
        columns = pl.ds(area.half_slot * LANES + area.half_lane, HALF)
        for side in range(2):
            yield pl.ds((part + side * (self.per_slot // 2)) * SUB, SUB), 0, columns

    def areas(self):
        full = self.full
        return Area(0, full, 0), Area(full + 1, full, HALF), Area(1, 0, HALF)

    def row(self, chip, core):
        first, members = 2 * chip, self.members
        if isinstance(chip, int):
            group, member = divmod(first, members)
        else:
            group, member = lax.div(first, members), lax.rem(first, members)
        return (member + core) * self.groups + group

    def own(self, ref, core, head):
        start = pl.multiple_of(core * (self.shift * self.width) + head * self.width, 16)
        return ref[pl.ds(start, self.width), :]

    def other(self, ref, head):
        return ref[head * self.width : (head + 1) * self.width, :]


def my_core():
    return lax.axis_index("seq") & 1


def my_device():
    return lax.axis_index("grp") * lax.axis_size("seq") + lax.axis_index("seq")


def pair_swap(x):
    size = lax.axis_size("seq")
    return lax.ppermute(x, "seq", [(i, i ^ 1) for i in range(size)])


def wide(tile):
    rows, columns = tile.shape
    if columns == LANES:
        return tile
    return jnp.concatenate([tile, jnp.zeros((rows, LANES - columns), tile.dtype)], axis=1)


def store_rows(plan, ref, area, head, block, held):
    block = wide(block)
    lane = lax.broadcasted_iota(jnp.int32, (SUB, LANES), 1)
    for j in range(plan.head_tiles):
        at = head * plan.head_tiles + j
        tile = block[j * SUB : (j + 1) * SUB, :]
        if at >= plan.stored:
            held[at - plan.stored] = tile
            continue
        if at < plan.donors * plan.pieces:
            donor, piece = divmod(at, plan.pieces)
            moved = pltpu.roll(held[donor], plan.width - piece * plan.spare, 1)
            tile = jnp.where(lane >= plan.width, moved, tile)
        plan.put(ref, area, at, tile)


def store_padding(plan, ref, area):
    for part in range(plan.left, plan.per_slot // 2):
        for index in plan.halves(area, part):
            ref[index] = jnp.zeros((SUB, HALF), F32)


def store_norms(plan, ref, rows, area):
    spare, width, last = plan.spare, plan.width, plan.half - 1
    free = HALF - area.half_lane
    shape = (SUB, LANES)
    lane = lax.broadcasted_iota(jnp.int32, shape, 1)
    row = lax.broadcasted_iota(jnp.int32, shape, 0)
    carried = jnp.broadcast_to(rows[last : last + 1], shape)
    packed = rows[:SUB]
    for j in range(plan.norm_slots):
        moved = pltpu.roll(carried, width - j * spare, 1)
        packed = jnp.where((row == j) & (lane >= width), moved, packed)
    packed = packed.reshape(1, SUB * LANES)[:, : plan.norm_slots * LANES]
    extra = pltpu.roll(carried, (free - plan.norm_slots * spare) % LANES, 1)
    extra = extra[0:1, free : free + HALF]
    for piece in range(plan.devices):
        ref[piece, :, pl.ds(plan.span, plan.norm_slots * LANES)] = packed
        ref[piece, :, pl.ds(area.half_slot * LANES + free, HALF)] = extra


def load_rows(plan, ref, area, head):
    lane = lax.broadcasted_iota(jnp.int32, (SUB, LANES), 1)
    tiles = []
    for j in range(plan.head_tiles):
        at = head * plan.head_tiles + j
        if at < plan.stored:
            tiles.append(plan.get(ref, area, at))
            continue
        tile = None
        for piece in range(plan.pieces):
            part = plan.get(ref, area, (at - plan.stored) * plan.pieces + piece)
            part = pltpu.roll(part, (LANES - plan.width + piece * plan.spare) % LANES, 1)
            tile = part if tile is None else jnp.where(lane >= piece * plan.spare, part, tile)
        tiles.append(tile)
    return jnp.concatenate(tiles, axis=0)[:, : plan.width]


def each(count, step, carry):
    if count > 16:
        return lax.fori_loop(0, count, step, carry)
    for i in range(count):
        carry = step(i, carry)
    return carry


def scan_rows(plan, in_ref, start, out_ref, later):
    chips = plan.devices // 2
    columns = pl.ds(start, plan.span)

    def step(i, sums):
        chip = chips - 1 - i if later else i
        grown = []
        for core in range(2):
            row = plan.row(chip, core)
            out_ref[row, :, : plan.span] = sums[core]
            grown.append(sums[core] + in_ref[row, :, columns])
        return tuple(grown)

    zero = jnp.zeros((1, plan.span), F32)
    each(chips, step, (zero, zero))


def scan_norms(plan, in_ref, core, chip, later, area):
    spare, width = plan.spare, plan.width
    free = HALF - area.half_lane
    columns = pl.ds(plan.span, plan.norm_slots * LANES)
    extras = pl.ds(area.half_slot * LANES, LANES)

    def step(i, totals):
        take = (i > chip) if later else (i < chip)
        row = plan.row(i, core)
        return (
            totals[0] + jnp.where(take, in_ref[row, :, columns], 0.0),
            totals[1] + jnp.where(take, in_ref[row, :, extras], 0.0),
        )

    zeros = (jnp.zeros((1, plan.norm_slots * LANES), F32), jnp.zeros((1, LANES), F32))
    packed, extra = each(plan.devices // 2, step, zeros)
    shape = (SUB, LANES)
    lane = lax.broadcasted_iota(jnp.int32, shape, 1)
    rows = [packed[:, j * LANES : (j + 1) * LANES] for j in range(plan.norm_slots)]
    last = None
    for j, row in enumerate(rows):
        moved = jnp.broadcast_to(row, shape)
        moved = pltpu.roll(moved, (LANES - width + j * spare) % LANES, 1)
        last = moved if last is None else jnp.where(lane >= j * spare, moved, last)
    at = plan.norm_slots * spare
    moved = pltpu.roll(jnp.broadcast_to(extra, shape), (at - free) % LANES, 1)
    last = jnp.where(lane >= at, moved, last)
    return [row[:, :width] for row in rows] + [last[0:1, :width]]


def causal_mask(length):
    row = lax.broadcasted_iota(jnp.int32, (length, length), 0)
    column = lax.broadcasted_iota(jnp.int32, (length, length), 1)
    return row <= column


def scores_of(a, b, causal):
    return jnp.where(causal, tn(b, a), 0.0)


def relu(x):
    return jnp.maximum(x, 0)


def block_state(plan, other, kv_ref, out_ref):
    core = my_core()
    side = 1 - core if other else core
    size = plan.heads * plan.width
    k_ref, v_ref = kv_ref.at[:size, :], kv_ref.at[size:, :]
    ones = jnp.ones((SUB, plan.length), BF16)
    out_ref[plan.rows :, :] = jnp.zeros((plan.extra, LANES), F32)
    for h in range(plan.half):
        b, v = relu(plan.own(k_ref, side, h)), plan.own(v_ref, side, h)
        out_ref[h * plan.width : (h + 1) * plan.width, :] = wide(nt(b, v))
        out_ref[plan.rows + h : plan.rows + h + 1, :] = wide(nt(ones, b))[0:1]


def chip_state(plan, own_ref, got_ref, out_ref):
    area = plan.areas()[0]
    held = {}
    for h in reversed(range(plan.half)):
        rows = slice(h * plan.width, (h + 1) * plan.width)
        store_rows(plan, out_ref, area, h, own_ref[rows, :] + got_ref[rows, :], held)
    store_padding(plan, out_ref, area)
    store_norms(plan, out_ref, own_ref[plan.rows :, :] + got_ref[plan.rows :, :], area)


def pack_tokens(
    plan, q_ref, k_ref, v_ref, g_ref, q_got_ref, k_got_ref, v_got_ref, g_got_ref,
    a_ref, b_ref, vb_ref, gb_ref, sum_ref, norm_ref,
):
    core = my_core()
    causal = causal_mask(plan.length)
    ones = jnp.ones((SUB, plan.length), BF16)
    sources = ((q_ref, q_got_ref), (k_ref, k_got_ref), (v_ref, v_got_ref), (g_ref, g_got_ref))
    for h in range(plan.half):
        for i in range(2):
            for n, (pair, ref) in enumerate(zip(sources, (a_ref, b_ref, vb_ref, gb_ref))):
                x = plan.other(pair[1], h).astype(BF16) if i else plan.own(pair[0], core, h)
                ref[i, h] = relu(x) if n < 2 else x
            a, b = a_ref[i, h], b_ref[i, h]
            scores = scores_of(a, b, causal)
            sum_ref[i, h : h + 1, :] = 1.0 + jnp.sum(scores, axis=0, keepdims=True)
            norm_ref[i, h : h + 1, :] = wide(nt(ones, b))[0:1]


def middle(
    plan, in_ref, sum_ref, a_ref, g_ref, norm_ref, norm_in_ref,
    out_ref, inverse_ref, z_ref,
):
    core, chip = my_core(), my_device() >> 1
    flags = (core.astype(F32), (1 - core).astype(F32))
    width = plan.width
    first, second, _ = plan.areas()
    norms = scan_norms(plan, in_ref, core, chip, False, first)
    scan_rows(plan, in_ref, 0, out_ref, False)
    held = {}
    for h in reversed(range(plan.half)):
        base = norm_in_ref[pl.ds(core * plan.shift + h, 1), :]
        base = base + norms[h]
        features, grads = [], []
        for i in range(2):
            z = base + flags[i] * norm_ref[1 - i, h : h + 1, :width]
            z_ref[i, h : h + 1, :] = wide(z)
            a = a_ref[i, h]
            den = sum_ref[i, h : h + 1, :] + added(nn(stacked_parts(z), a))
            inverse = 1.0 / den
            inverse_ref[i, h : h + 1, :] = inverse
            features.append(a)
            grads.append((g_ref[i, h].astype(F32) * inverse).astype(BF16))
        state = nt(jnp.concatenate(features, axis=1), jnp.concatenate(grads, axis=1))
        store_rows(plan, out_ref, second, h, state, held)
    store_padding(plan, out_ref, second)


def before_states(
    plan, a_ref, b_ref, v_ref, g_ref, state_in_ref, before_ref, inner_ref
):
    core = my_core()
    causal = causal_mask(plan.length)
    own_first = core == 0
    late = (core.astype(F32), (1 - core).astype(F32))
    for h in range(plan.half):
        for i in range(2):
            low = scores_of(a_ref[i, h], b_ref[i, h], causal).astype(BF16)
            inner = nn(v_ref[i, h], low)
            inner_ref[i, h : h + 1, :] = jnp.sum(
                g_ref[i, h].astype(F32) * inner, axis=0, keepdims=True
            )
        b = jnp.where(own_first, b_ref[0, h].astype(F32), b_ref[1, h].astype(F32)).astype(BF16)
        v = jnp.where(own_first, v_ref[0, h].astype(F32), v_ref[1, h].astype(F32)).astype(BF16)
        first = nt(b, v)
        for i in range(2):
            before_ref[i, h] = state_in_ref[core * plan.shift + h] + late[i] * first


def outputs_grad(
    plan, sends, in_ref, before_ref, a_ref, g_ref, inverse_ref, inner_ref,
    out_ref, product_ref, c_ref, m_ref,
):
    first, _, third = plan.areas()
    scan_rows(plan, in_ref, plan.full * LANES, out_ref, True)
    sends.flush(LANES, plan.span - LANES)
    totals = []
    for h in range(plan.half):
        base = load_rows(plan, in_ref, first, h)
        total = None
        for i in range(2):
            high, low = parts(base + before_ref[i, h])
            g, a = g_ref[i, h], a_ref[i, h]
            product = nn(jnp.concatenate([high, low], axis=0), g)
            product = product[: plan.width] + product[plan.width :]
            product_ref[i, h] = product
            inverse = inverse_ref[i, h : h + 1, :]
            along = jnp.sum(a.astype(F32) * product, axis=0, keepdims=True)
            c = -((along + inner_ref[i, h : h + 1, :]) * inverse) * inverse
            c_ref[i, h : h + 1, :] = c
            m = wide(added(nt(stacked_parts(c), a)))
            m_ref[i, h : h + 1, :] = m
            total = m if total is None else total + m
        totals.append(total)
    totals += [jnp.zeros((1, LANES), F32)] * (plan.extra - plan.half)
    store_norms(plan, out_ref, jnp.concatenate(totals, axis=0), third)
    sends.flush(0, LANES)
    sends.flush(plan.span, plan.norm_slots * LANES)


def query_grads(
    plan, a_ref, b_ref, v_ref, g_ref, inverse_ref, c_ref, z_ref, product_ref,
    own_ref, send_ref, mixed_ref, a_out_ref, u_out_ref,
):
    causal = causal_mask(plan.length)
    width = plan.width
    for i in (1, 0):
        columns = z_ref[i].T
        for h in range(plan.half):
            rows = slice(h * width, (h + 1) * width)
            inverse, c = inverse_ref[i, h : h + 1, :], c_ref[i, h : h + 1, :]
            u = (g_ref[i, h].astype(F32) * inverse).astype(BF16)
            mixed = jnp.where(causal, tn(v_ref[i, h], u) + c, 0.0).astype(BF16)
            mixed_ref[i, h] = mixed
            a_out_ref[i, h] = a_ref[i, h]
            u_out_ref[i, h] = u
            grad = product_ref[i, h] * inverse + columns[:width, h : h + 1] * c
            grad = jnp.where(a_ref[i, h].astype(F32) > 0, grad + nn(b_ref[i, h], mixed), 0.0)
            target = send_ref if i else own_ref
            target[rows, :] = grad


def after_states(plan, a_ref, b_ref, u_ref, mixed_ref, grad_state_ref, *refs):
    core = my_core()
    causal = causal_mask(plan.length)
    own_first = core == 0
    early = ((1 - core).astype(F32), core.astype(F32))
    for h in range(plan.half):
        for i in range(2):
            low = scores_of(a_ref[i, h], b_ref[i, h], causal).astype(BF16)
            key, value = nt(a_ref[i, h], mixed_ref[i, h]), nt(u_ref[i, h], low)
            key = jnp.where(b_ref[i, h].astype(F32) > 0, key, 0.0)
            rows = slice(h * plan.width, (h + 1) * plan.width)
            refs[3 * i + 1][rows, :] = key
            refs[3 * i + 2][rows, :] = value
        a = jnp.where(own_first, a_ref[1, h].astype(F32), a_ref[0, h].astype(F32)).astype(BF16)
        u = jnp.where(own_first, u_ref[1, h].astype(F32), u_ref[0, h].astype(F32)).astype(BF16)
        second = nt(a, u)
        for i in range(2):
            refs[3 * i][h] = grad_state_ref[core * plan.shift + h] + early[i] * second


def suffix_norms(plan, in_ref, grad_norm_ref, m_ref, i):
    core, chip = my_core(), my_device() >> 1
    flag = (core if i else 1 - core).astype(F32)
    norms = scan_norms(plan, in_ref, core, chip, True, plan.areas()[2])
    rows = [
        norm + grad_norm_ref[pl.ds(core * plan.shift + h, 1), :] for h, norm in enumerate(norms)
    ]
    zeros = plan.extra - plan.half
    rows += [jnp.zeros((zeros, plan.width), F32)] * (zeros > 0)
    return wide(jnp.concatenate(rows, axis=0)) + flag * m_ref[1 - i]


def key_value(state, column, b, v):
    width = state.shape[0]
    high, low = parts(state)
    both = nn(jnp.concatenate([high, low], axis=0), v)
    key = both[:width] + both[width:] + column
    return jnp.where(b.astype(F32) > 0, key, 0.0), tn(high, b) + tn(low, b)


def other_suffix(plan, in_ref, after_ref, grad_norm_ref, m_ref, out_ref):
    core, count, width = my_core(), plan.shift, plan.width
    out_ref[count * width :, :] = suffix_norms(plan, in_ref, grad_norm_ref, m_ref, 1)
    for h in range(plan.half):
        state = wide(load_rows(plan, in_ref, plan.areas()[2], h) + after_ref[h])
        at = h - core * (plan.half - count)

        def store():
            start = pl.multiple_of(jnp.clip(at, 0, count - 1) * width, 16)
            out_ref[pl.ds(start, width), :] = state

        if plan.half - count <= h < count:
            store()
        else:
            pl.when((at >= 0) & (at < count))(store)


def own_grads(
    plan, in_ref, after_ref, grad_norm_ref, m_ref, b_ref, v_ref, key_in_ref, value_in_ref,
    key_ref, value_ref,
):
    columns = suffix_norms(plan, in_ref, grad_norm_ref, m_ref, 0).T
    for h in range(plan.half):
        rows = slice(h * plan.width, (h + 1) * plan.width)
        state = load_rows(plan, in_ref, plan.areas()[2], h) + after_ref[h]
        key, value = key_value(state, columns[: plan.width, h : h + 1], b_ref[0, h], v_ref[0, h])
        key_ref[rows, :] = (key + key_in_ref[rows, :]).astype(BF16)
        value_ref[rows, :] = (value + value_in_ref[rows, :]).astype(BF16)


def rest_grads(
    plan, got_ref, k_ref, v_ref, key_in_ref, value_in_ref, own_key_ref, own_value_ref,
    key_ref, value_ref,
):
    core = my_core()
    width, count = plan.width, plan.shift
    own = pl.multiple_of(core * (count * width), 16)
    key_ref[pl.ds(own, plan.rows), :] = own_key_ref[...]
    value_ref[pl.ds(own, plan.rows), :] = own_value_ref[...]
    skip = (1 - core) * (plan.half - count)
    norms = got_ref[pl.ds(count * width + skip, count), :]
    columns = jnp.concatenate([norms, jnp.zeros((plan.extra - count, LANES), F32)], axis=0).T
    for t in range(count):
        source = pl.ds(pl.multiple_of((skip + t) * width, 16), width)
        rows = pl.ds(pl.multiple_of((1 - core) * plan.rows + t * width, 16), width)
        b, v = relu(k_ref[rows, :]), v_ref[rows, :]
        state = got_ref[t * width : (t + 1) * width, :][:, :width]
        key, value = key_value(state, columns[:width, t : t + 1], b, v)
        key_ref[rows, :] = (key + key_in_ref[source, :]).astype(BF16)
        value_ref[rows, :] = (value + value_in_ref[source, :]).astype(BF16)


def assemble(plan, count, *refs):
    core = my_core()
    start = pl.multiple_of(core * (plan.shift * plan.width), 16)
    rest = plan.shift * plan.width
    skip = plan.rows - rest
    other = pl.multiple_of((1 - core) * plan.rows, 16)
    source = pl.multiple_of((1 - core) * skip, 16)
    for n in range(count):
        own_ref, out_ref = refs[n], refs[len(refs) - count + n]
        out_ref[pl.ds(start, plan.rows), :] = own_ref[...].astype(BF16)
        got = refs[count + n][pl.ds(source, rest), :]
        for ref in refs[2 * count + n : len(refs) - count : count]:
            got = got + ref[pl.ds(source, rest), :]
        out_ref[pl.ds(other, rest), :] = got.astype(BF16)


class Sends:
    def __init__(self, buffer, target, sems):
        self.buffer, self.target, self.sems, self.copies = buffer, target, sems, []

    def flush(self, start, count):
        at = slice(None), slice(None), pl.ds(start, count)
        sem = self.sems.at[len(self.copies)]
        copy = pltpu.make_async_copy(self.buffer.at[at], self.target.at[at], sem)
        copy.start()
        self.copies.append(copy)

    def finish(self):
        for copy in self.copies:
            copy.wait()


def call(body, outs, args, room=FREE, flops=10_000_000, send=False, reuse=None):
    vmem = pl.BlockSpec(memory_space=pltpu.VMEM)
    anywhere = pl.BlockSpec(memory_space=pl.ANY)
    moved = sum(x.size * x.dtype.itemsize for x in (*args, *outs))
    in_specs, out_specs, scratch, kernel = [vmem] * len(args), [vmem] * len(outs), [], body
    aliases = {}
    count = len(args)
    if send:
        out_specs[0] = anywhere
        scratch = [pltpu.VMEM(outs[0].shape, outs[0].dtype), pltpu.SemaphoreType.DMA((4,))]
        if reuse is not None:
            args, in_specs = (*args, reuse), [*in_specs, anywhere]
            aliases = {count: 0}

        def kernel(*refs):
            ins, refs = refs[:count], refs[len(args) :]
            out_refs, (buffer, sems) = refs[: len(outs)], refs[len(outs) :]
            sends = Sends(buffer, out_refs[0], sems)
            body(sends, *ins, buffer, *out_refs[1:])
            sends.finish()

    return pl.pallas_call(
        kernel,
        out_shape=outs,
        in_specs=in_specs,
        out_specs=out_specs,
        scratch_shapes=scratch,
        input_output_aliases=aliases,
        compiler_params=pltpu.CompilerParams(vmem_limit_bytes=VMEM_BYTES - room),
        cost_estimate=pl.CostEstimate(flops=flops, bytes_accessed=moved, transcendentals=0),
    )(*args)


def shape(dims, dtype=F32):
    return jax.ShapeDtypeStruct(dims, dtype)


def per_device(
    queries, key_vectors, value_vectors, output_grad, state_in, norm_in, grad_state, grad_norm
):
    both = ("seq", "grp")
    length = queries.shape[0]
    heads, width = norm_in.shape
    plan = Plan(lax.axis_size("grp"), lax.axis_size("seq"), length, heads, width)
    devices = plan.devices
    half = plan.half
    core = my_core()
    key_rows, value_rows = key_vectors.T, value_vectors.T
    q, k, v, g = queries.T, key_vectors.T, value_vectors.T, output_grad.T

    def bind(body):
        return functools.partial(body, plan)

    def exchange(x):
        return lax.all_to_all(x, both, 0, 0, tiled=True)

    def swap_columns(x):
        start = (1 - core) * (plan.shift * width)
        return pair_swap(lax.dynamic_slice_in_dim(x, start, plan.rows, 0).astype(F32))

    tokens = shape((plan.rows, length))
    packed = shape((2, half, width, length), BF16)
    products = shape((2, half, width, length))
    square = shape((2, half, length, length), BF16)
    states = shape((2, half, width, width))
    rows = shape((2, plan.extra, LANES))
    after = shape((half, width, width))
    block = shape((plan.rows + plan.extra, LANES))
    sent_single = shape((devices, 1, plan.single))
    sent_double = shape((devices, 1, plan.double))

    keys_values = jnp.concatenate([k, v], axis=0)
    (send,) = call(functools.partial(block_state, plan, True), (block,), (keys_values,))
    block_got = pair_swap(send)
    (block_own,) = call(functools.partial(block_state, plan, False), (block,), (keys_values,))
    (sent,) = call(bind(chip_state), (sent_single,), (block_own, block_got))
    first_sent = sent
    sent, k, v, q, g = lax.optimization_barrier((sent, k, v, q, g))
    got = exchange(sent)
    a, b, v, g, sums, norm = call(
        bind(pack_tokens),
        (packed, packed, packed, packed, rows, rows),
        (q, k, v, g, *(swap_columns(x) for x in (q, k, v, g))),
    )
    before, inner = call(bind(before_states), (states, rows), (a, b, v, g, state_in))
    got, before, inner = lax.optimization_barrier((got, before, inner))
    sent, inverse, z = call(
        bind(middle),
        (sent_double, rows, rows),
        (got, sums, a, g, norm, norm_in),
    )
    got = exchange(sent)
    sent, product, c, m = call(
        bind(outputs_grad),
        (sent_single, products, rows, rows),
        (got, before, a, g, inverse, inner),
        send=True,
        reuse=first_sent,
    )
    got = exchange(sent)
    query, query_send, mixed, a, u = call(
        bind(query_grads),
        (tokens, tokens, square, packed, packed),
        (a, b, v, g, inverse, c, z, product),
    )
    query_got = pair_swap(query_send)
    finals = call(
        bind(after_states), (after, tokens, tokens) * 2, (a, b, u, mixed, grad_state)
    )
    inner_got = [pair_swap(x) for x in finals[4:]]
    whole = shape((heads * width, length), BF16)
    (query_grad,) = call(functools.partial(assemble, plan, 1), (whole,), (query, query_got))
    got, query_grad, inner_got = lax.optimization_barrier((got, query_grad, inner_got))
    rest = shape((plan.shift * width + plan.extra, LANES))
    (send,) = call(bind(other_suffix), (rest,), (got, finals[3], grad_norm, m))
    rest_got = pair_swap(send)
    own_tokens = shape((plan.rows, length), BF16)
    key, value = call(
        bind(own_grads), (own_tokens, own_tokens), (got, finals[0], grad_norm, m, b, v, *finals[1:3])
    )
    key_grad, value_grad = call(
        bind(rest_grads), (whole, whole), (rest_got, key_rows, value_rows, *inner_got, key, value)
    )
    return query_grad.T, key_grad.T, value_grad.T


def solution(mesh):
    rows = P(("grp", "seq"), None)
    return jax.shard_map(
        per_device,
        mesh=mesh,
        in_specs=(rows, rows, rows, rows, P(), P(), P(), P()),
        out_specs=(rows, rows, rows),
        check_vma=False,
    )
```
